512 devices in a mesh: grp: 16 (over z, core), dev: 32 (over y, x).
Axes of the slice: x: 4, y: 8, z: 8, core: 2. Of those that a mesh axis runs over, the one named last changes fastest.
Arguments:
- old_fields: float32 [3, 4096, 32, 1024], P(None, ('grp', 'dev')), as said below
- old_counts: int32 [512], replicated, may hold values from 2 to 6, as said below
Outputs:
- pressure_out: float32 [512, 1024, 128], P('grp', 'dev')
- residual: float32 [512, 1024, 128], P('grp', 'dev')
The draws below stay inside these ranges and needn't reach their ends.
Inputs may be any that keep to these rules, and one draw needn't show every extreme that they name: `old_counts`: the counts sum to 2048; each device's first box number, start[e], lies between e * 4 and e * 4 + 4 / 2; the slots of a device beyond its count hold data that belongs to no box. `old_fields`: coefficient entries (component 2) are positive; components 0 and 1 are real-valued of order one.
All inputs are finite; a program needn't handle non-finite values.
Results may differ from the reference program's by a relative error of at most 0.0003.
Values sent between devices are 32-bit elements; how exact they have to be, the bound alone decides.
No kernel may reach another device: no remote copies, remote signals or barrier semaphores. Data moves between devices by JAX's collectives and lax.ppermute only.
A program may use at most 64 MiB of HBM per device.

```python
import jax
import jax.numpy as jnp
from jax import lax

BOX = 32
BOX_DEV = 4
CAPO = 8
SLOTS = 4096
NBOX = 2048
NX = 512
NY = 1024
NZ = 128
N_GRP = 16
N_DEV = 32


def draw_old_counts(key, part):
    devices = NBOX // BOX_DEV
    half_box = BOX_DEV // 2
    first_key, second_key = jax.random.split(jax.random.fold_in(key, 11))
    shifts = jax.random.randint(first_key, (devices + 1,), 0, half_box + 1)
    chosen = jax.random.randint(second_key, (), 2, devices - 2)
    shifts = shifts.at[chosen].set(half_box).at[1].set(half_box).at[devices - 1].set(half_box)
    shifts = shifts.at[0].set(0).at[devices].set(0)
    return (BOX_DEV + shifts[1:] - shifts[:-1]).astype(jnp.int32)


def draw_old_fields(key, part):
    keys = jax.random.split(jax.random.fold_in(key, 23), 3)
    shape = (SLOTS, BOX, BOX * BOX)
    pressure = jax.random.normal(keys[0], shape, jnp.float32)
    right_side = jax.random.normal(keys[1], shape, jnp.float32)
    coefficient = jnp.exp(jax.random.uniform(keys[2], shape, jnp.float32, -2.3, 2.3))
    return jnp.stack([pressure, right_side, coefficient]).astype(jnp.float32)


def setup_inputs(seed: int = 0) -> dict:
    seeds = jax.random.split(jax.random.key(seed), 3)
    old_fields = draw_old_fields(jax.random.fold_in(seeds[2], 71), 0)
    old_counts = draw_old_counts(jax.random.fold_in(seeds[2], 71), 0)
    return dict(old_fields=old_fields, old_counts=old_counts)


def beta_parts(coefficient):
    padded = jnp.pad(coefficient, 1)
    centre = padded[1:-1, 1:-1, 1:-1]
    sizes = centre.shape
    betas = []
    for axis_id in range(3):
        for offset in (0, 2):
            starts = [1, 1, 1]
            starts[axis_id] = offset
            neighbour = lax.dynamic_slice(padded, starts, sizes)
            betas.append((0.5 * (centre + neighbour), axis_id, offset))
    return betas


def beta_phi(pressure, betas):
    padded = jnp.pad(pressure, 1)
    sizes = pressure.shape
    total = jnp.zeros(sizes, jnp.float32)
    for beta, axis_id, offset in betas:
        starts = [1, 1, 1]
        starts[axis_id] = offset
        total = total + beta * lax.dynamic_slice(padded, starts, sizes)
    return total


def reference(old_fields, old_counts):
    ends = jnp.cumsum(old_counts).astype(jnp.int32)
    starts = (ends - old_counts).astype(jnp.int32)
    wanted = jnp.arange(NBOX, dtype=jnp.int32)
    owner_dev = jnp.sum((ends[None, :] <= wanted[:, None]).astype(jnp.int32), axis=1).astype(jnp.int32)
    slot_id = (owner_dev * CAPO + wanted - starts[owner_dev]).astype(jnp.int32)
    moved = jnp.take(old_fields, slot_id, axis=1)
    moved = moved.reshape(3, N_GRP, N_DEV, BOX_DEV, BOX, BOX, BOX)
    moved = jnp.transpose(moved, (0, 1, 4, 2, 5, 3, 6)).reshape(3, NX, NY, NZ)
    pressure = moved[0]
    right_side = moved[1]
    coefficient = moved[2]
    betas = beta_parts(coefficient)
    beta_sum = betas[0][0]
    for beta, axis_id, offset in betas[1:]:
        beta_sum = beta_sum + beta
    parity = (lax.broadcasted_iota(jnp.int32, (NX, NY, NZ), 0) + lax.broadcasted_iota(jnp.int32, (NX, NY, NZ), 1) + lax.broadcasted_iota(jnp.int32, (NX, NY, NZ), 2)) % 2
    red_mask = parity == 0
    first = jnp.where(red_mask, (right_side + beta_phi(pressure, betas)) / beta_sum, pressure)
    second = jnp.where(red_mask, first, (right_side + beta_phi(first, betas)) / beta_sum)
    residual = right_side - (beta_sum * second - beta_phi(second, betas))
    return second, residual
```

```python
import jax
import jax.numpy as jnp
from jax import lax
from jax.experimental import pallas as pl
from jax.experimental.pallas import tpu as pltpu
from jax.sharding import PartitionSpec as P

EDGE = 32
LANES = 128
GROUPS = EDGE * EDGE // LANES
COLUMN = 4
FIELDS = 3
MOVED = 2
KINDS = 5
SHELL = GROUPS + 6
CORE = 3 * (GROUPS - 2)
TALL = EDGE + 8
SLABS = EDGE + 6
XMSG = EDGE + 4
F32 = jnp.float32
VMEM = pltpu.VMEM


def iota(shape, dim):
    return lax.broadcasted_iota(jnp.int32, shape, dim)


def moved_boxes(counts_ref):
    device = lax.axis_index("grp") * lax.axis_size("dev") + lax.axis_index("dev")
    counts = counts_ref[...]
    index = iota(counts.shape, 0) * LANES + iota(counts.shape, 1)
    start = jnp.sum(jnp.where(index < device, counts, 0))
    return jnp.clip(start - device * COLUMN, 0, MOVED)


def lane_group(g):
    return pl.ds(g * LANES, LANES)


def fetch_moved(old_ref, boxes, sems, moved):
    copies = []
    for f in range(FIELDS):
        for c in range(MOVED):
            copies.append(pltpu.make_async_copy(old_ref.at[f, COLUMN + c - moved], boxes.at[f, c], sems.at[f, c]))
    for copy in copies:
        copy.start()
    for copy in copies:
        copy.wait()


def box_tiles(boxes, f, c, g, which):
    low = iota((8, LANES), 0) < 4
    if which == "edge":
        return jnp.where(low, boxes[f, c, 0:8, lane_group(g)], boxes[f, c, 24:32, lane_group(g)])
    if which == 0:
        return jnp.where(low, boxes[f, c, 24:32, lane_group(g)], boxes[f, c, 0:8, lane_group(g)])
    return boxes[f, c, 8 * which : 8 * which + 8, lane_group(g)]


def pack(boxes, out, at, g, which):
    shape = (8, LANES)
    lane = iota(shape, 1)
    block = lane // EDGE
    black = (iota(shape, 0) + block + lane) % 2 == 1
    even = block % 2 == 0
    first, second = [[box_tiles(boxes, f, c, g, which) for f in range(FIELDS)] for c in range(MOVED)]
    turned = [pltpu.roll(v, EDGE, 1) for v in second]
    out[0, at] = jnp.where(black, first[0], turned[0])
    for f in (1, 2):
        out[2 * f - 1, at] = jnp.where(even, first[f], turned[f])
        out[2 * f, at] = jnp.where(even, turned[f], first[f])


def pack_shell(counts_ref, old_ref, out, boxes, sems):
    fetch_moved(old_ref, boxes, sems, moved_boxes(counts_ref))
    for g in range(GROUPS):
        pack(boxes, out, g, g, "edge")
    for side, g in enumerate((0, GROUPS - 1)):
        for which in range(3):
            pack(boxes, out, GROUPS + 3 * side + which, g, which)


def pack_core(counts_ref, old_ref, out, boxes, sems):
    fetch_moved(old_ref, boxes, sems, moved_boxes(counts_ref))
    for g in range(1, GROUPS - 1):
        for which in range(3):
            pack(boxes, out, 3 * (g - 1) + which, g, which)


def relayout(counts_ref, old_ref, out, edge_out, boxes, sems):
    moved = moved_boxes(counts_ref)
    copies = []
    for f in range(FIELDS):
        for c in range(COLUMN):
            slot = jnp.maximum(c - moved, 0)
            copies.append(pltpu.make_async_copy(old_ref.at[f, slot], boxes.at[f, c], sems.at[f, c]))
    for copy in copies:
        copy.start()
    lane = iota((EDGE, LANES), 1)
    half = lane < 2 * EDGE
    even = (lane // EDGE) % 2 == 0
    low = iota((8, LANES), 0) < 4
    for f in range(FIELDS):
        for c in range(COLUMN):
            copies[f * COLUMN + c].wait()
        for g in range(GROUPS):
            v = [boxes[f, c, :, lane_group(g)] for c in range(COLUMN)]
            w = [pltpu.roll(a, 2 * EDGE, 1) for a in v]
            a0, a1 = jnp.where(half, v[0], w[2]), jnp.where(half, v[1], w[3])
            a2, a3 = jnp.where(half, w[0], v[2]), jnp.where(half, w[1], v[3])
            rows = []
            for a, b in ((a0, a1), (a2, a3)):
                rows.append(jnp.where(even, a, pltpu.roll(b, EDGE, 1)))
                rows.append(jnp.where(even, pltpu.roll(a, LANES - EDGE, 1), b))
            for r, row in enumerate(rows):
                out[f, 4 * g + r] = row
                edge_out[f, 4 * g + r] = jnp.where(low, row[0:8], row[24:32])


def unmix(kinds, f):
    if f == 0:
        a = b = kinds[0]
    else:
        a, b = kinds[2 * f - 1], kinds[2 * f]
    return [a, pltpu.roll(b, LANES - EDGE, 1), pltpu.roll(a, 2 * EDGE, 1), pltpu.roll(b, EDGE, 1)]


def wire_rows(shell, core, k, g):
    low = iota((8, LANES), 0) < 4
    edge = shell[k, g]
    if g in (0, GROUPS - 1):
        base = GROUPS + (3 if g else 0)
        mid = [shell[k, base + which] for which in range(3)]
    else:
        mid = [core[k, 3 * (g - 1) + which] for which in range(3)]
    return jnp.concatenate([jnp.where(low, edge, mid[0]), mid[1], mid[2], jnp.where(low, mid[0], edge)], axis=0)


def pack_x(pressure, right_side, coefficient):
    row = iota((8, LANES), 0)
    high = jnp.where(
        row >= 5, coefficient, jnp.where(row >= 2, pltpu.roll(pressure, 5, 0), pltpu.roll(right_side, 2, 0))
    )
    low = jnp.where(
        row < 3, coefficient, jnp.where(row < 6, pltpu.roll(pressure, 3, 0), pltpu.roll(right_side, 6, 0))
    )
    return high, low


def make_faces(counts_ref, shell, own, own_edge, y_up, y_down, x_up, x_down, slabs, sems):
    copies = []
    for f in range(FIELDS):
        for side in range(2):
            copies.append(pltpu.make_async_copy(own.at[f, pl.ds(28 * side, 4)], slabs.at[f, side], sems.at[f, side]))
    for copy in copies:
        copy.start()
    limit = moved_boxes(counts_ref) * EDGE
    taken = iota((8, LANES), 1) < limit
    for g in range(GROUPS):
        kinds = [shell[k, g] for k in range(KINDS)]
        rows = [unmix(kinds, f) for f in range(FIELDS)]
        for r in range(4):
            y = 4 * g + r
            edge = [jnp.where(taken, rows[f][r], own_edge[f, y]) for f in range(FIELDS)]
            x_up[y + 2], x_down[y + 2] = pack_x(*edge)
    for copy in copies:
        copy.wait()
    taken = iota((EDGE, LANES), 1) < limit
    for side, g in enumerate((0, GROUPS - 1)):
        out = y_up if side else y_down
        kinds = [wire_rows(shell, None, k, g) for k in range(KINDS)]
        for f, at, depth in ((2, 0, 3), (0, 3, 3), (1, 6, 2)):
            rows = unmix(kinds, f)
            for j in range(depth):
                r = 4 - depth + j if side else j
                out[at + j] = jnp.where(taken, rows[r], slabs[f, side, r])


def add_corners(before, after, x_up_in, x_down_in, x_up, x_down, tiles, sems):
    del x_up_in, x_down_in
    low = iota((8, LANES), 0) < 4
    places = ((before, 1, 4, 6), (before, 2, 5, 7), (after, 0, 3, 6), (after, 1, 4, 7))
    for at, (ref, b, p, f) in enumerate(places):
        edge = [jnp.where(low, ref[i, 0:8], ref[i, 24:32]) for i in (p, f, b)]
        tiles[0, at], tiles[1, at] = pack_x(*edge)
    copies = []
    for way, out in enumerate((x_up, x_down)):
        for side in range(2):
            copies.append(
                pltpu.make_async_copy(
                    tiles.at[way, pl.ds(2 * side, 2)], out.at[pl.ds((XMSG - 2) * side, 2)], sems.at[way, side]
                )
            )
    for copy in copies:
        copy.start()
    for copy in copies:
        copy.wait()


def plane_sum(value):
    lane = iota(value.shape, 1)
    rows = value.shape[0]
    below = jnp.where(lane == 0, 0.0, pltpu.roll(value, 1, 1))
    above = jnp.where(lane == LANES - 1, 0.0, pltpu.roll(value, LANES - 1, 1))
    return (pltpu.roll(value, 1, 0) + pltpu.roll(value, rows - 1, 0)) + (below + above)


def sweep(counts_ref, own, shell, core, y_before, y_after, x_before, x_after, out_p, out_r, prs, rhs, cof, mid, tot, inv):
    grp, dev = lax.axis_index("grp"), lax.axis_index("dev")
    limit = moved_boxes(counts_ref) * EDGE
    taken = iota((EDGE, LANES), 1) < limit
    fields = (prs, rhs, cof)
    for g in range(GROUPS):
        kinds = [wire_rows(shell, core, k, g) for k in range(KINDS)]
        for f, ref in enumerate(fields):
            rows = unmix(kinds, f)
            for r in range(4):
                y = 4 * g + r
                ref[y + 3, 0:EDGE] = jnp.where(taken, rows[r], own[f, y])
    for j in range(3):
        cof[j, 0:EDGE] = y_before[j]
        prs[j, 0:EDGE] = y_before[3 + j]
        cof[EDGE + 3 + j, 0:EDGE] = y_after[j]
        prs[EDGE + 3 + j, 0:EDGE] = y_after[3 + j]
    for j in range(2):
        rhs[1 + j, 0:EDGE] = y_before[6 + j]
        rhs[EDGE + 3 + j, 0:EDGE] = y_after[6 + j]
    row8 = iota((8, LANES), 0)
    zero = jnp.zeros((8, LANES), F32)
    for ref in fields:
        ref[0, EDGE:TALL] = zero
        ref[SLABS - 1, EDGE:TALL] = zero

    def halo(i, carry):
        low, high = x_before[i], x_after[i]
        at = i + 1
        cof[at, EDGE:TALL] = jnp.where(row8 < 4, high, low)
        prs[at, EDGE:TALL] = jnp.where(row8 < 4, pltpu.roll(high, 5, 0), pltpu.roll(low, 3, 0))
        rhs[at, EDGE:TALL] = jnp.where(row8 < 4, pltpu.roll(high, 2, 0), pltpu.roll(low, 6, 0))
        return carry

    lax.fori_loop(0, XMSG, halo, 0)

    shape = (TALL, LANES)
    row, lane = iota(shape, 0), iota(shape, 1)
    base = row + lane
    near = (row >= EDGE) & (row < EDGE + 4)
    far = row >= EDGE + 4
    has_after = (grp < lax.axis_size("grp") - 1).astype(jnp.int32)
    has_before = (grp > 0).astype(jnp.int32)
    inside_x = jnp.where(near, has_after, jnp.where(far, has_before, 1))
    y_low = (dev > 0).astype(jnp.int32)
    y_high = (dev < lax.axis_size("dev") - 1).astype(jnp.int32)

    def colour(at, which):
        y_ok = jnp.where(at < 3, y_low, jnp.where(at >= EDGE + 3, y_high, 1))
        return ((base + at + which) % 2) * inside_x * y_ok > 0

    def flows(ref, at):
        b, p, pm, pp = cof[at], ref[at], ref[at - 1], ref[at + 1]
        near_p = plane_sum(p) + (pm + pp)
        near_q = plane_sum(b * p) + (cof[at - 1] * pm + cof[at + 1] * pp)
        return p, 0.5 * (b * near_p + near_q)

    def red(at, carry):
        b = cof[at]
        total = 3.0 * b + 0.5 * (plane_sum(b) + (cof[at - 1] + cof[at + 1]))
        inverse = 1.0 / total
        tot[at] = total
        inv[at] = inverse
        p, flow = flows(prs, at)
        mid[at] = jnp.where(colour(at, 0), (rhs[at] + flow) * inverse, p)
        return carry

    def black(at, carry):
        p, flow = flows(mid, at)
        prs[at] = jnp.where(colour(at, 1), (rhs[at] + flow) * inv[at], p)
        return carry

    def finish(at, carry):
        p, flow = flows(prs, at)
        rest = rhs[at] - (tot[at] * p - flow)
        rows = pl.ds(at - 3, EDGE, stride=EDGE)
        out_p[rows, :] = p[0:EDGE]
        out_r[rows, :] = rest[0:EDGE]
        return carry

    lax.fori_loop(1, SLABS - 1, red, 0)
    lax.fori_loop(2, SLABS - 2, black, 0)
    lax.fori_loop(3, SLABS - 3, finish, 0)


def call(body, inputs, outputs, scratch, flops, moved, aliases=None, anywhere=(), out_anywhere=False):
    vmem, place = pl.BlockSpec(memory_space=pltpu.VMEM), pl.BlockSpec(memory_space=pl.ANY)
    hbm = pl.BlockSpec(memory_space=pltpu.HBM)
    out_specs = [place if out_anywhere else vmem for _ in outputs]
    out_shape = [jax.ShapeDtypeStruct(shape, F32) for shape in outputs]
    return pl.pallas_call(
        body,
        out_shape=out_shape,
        in_specs=[hbm if x.ndim == 4 and x.shape[1] == 2 * COLUMN else place if i in anywhere else vmem for i, x in enumerate(inputs)],
        out_specs=out_specs,
        scratch_shapes=scratch,
        input_output_aliases=aliases or {},
        cost_estimate=pl.CostEstimate(flops=flops, bytes_accessed=moved, transcendentals=0),
        compiler_params=pltpu.CompilerParams(vmem_limit_bytes=40 * 2**20),
        name=body.__name__,
    )(*inputs)


def per_device(old_fields, old_counts):
    groups, columns = lax.axis_size("grp"), lax.axis_size("dev")
    devices = groups * columns
    counts = jnp.pad(old_counts, (0, -devices % LANES)).reshape(-1, LANES)
    chain = [(i, i + 1) for i in range(devices - 1)]

    def ends(count):
        up = [(i, i + 1) for i in range(count - 1)]
        return up, [(j, i) for i, j in up]

    y_ways, x_ways = ends(columns), ends(groups)
    pair = [VMEM((FIELDS, MOVED, EDGE, EDGE * EDGE), F32), pltpu.SemaphoreType.DMA((FIELDS, MOVED))]
    (shell,) = call(pack_shell, (counts, old_fields), [(KINDS, SHELL, 8, LANES)], pair, 10**6, 2 * 10**6, anywhere=(1,))
    shell = lax.ppermute(shell, ("grp", "dev"), chain)
    (core,) = call(pack_core, (counts, old_fields), [(KINDS, CORE, 8, LANES)], pair, 10**6, 2 * 10**6, anywhere=(1,))
    core = lax.ppermute(core, ("grp", "dev"), chain)
    own, own_edge = call(
        relayout,
        (counts, old_fields),
        [(FIELDS, EDGE, EDGE, LANES), (FIELDS, EDGE, 8, LANES)],
        [VMEM((FIELDS, COLUMN, EDGE, EDGE * EDGE), F32), pltpu.SemaphoreType.DMA((FIELDS, COLUMN))],
        10**6,
        4 * 10**6,
        anywhere=(1,),
    )
    face, strip = (8, EDGE, LANES), (XMSG, 8, LANES)
    y_up, y_down, x_up, x_down = call(
        make_faces,
        (counts, shell, own, own_edge),
        [face, face, strip, strip],
        [VMEM((FIELDS, 2, 4, EDGE, LANES), F32), pltpu.SemaphoreType.DMA((FIELDS, 2))],
        10**6,
        10**6,
        anywhere=(2,),
    )
    y_before = lax.ppermute(y_up, "dev", y_ways[0])
    y_after = lax.ppermute(y_down, "dev", y_ways[1])
    x_up, x_down = call(
        add_corners,
        (y_before, y_after, x_up, x_down),
        [strip, strip],
        [VMEM((2, 4, 8, LANES), F32), pltpu.SemaphoreType.DMA((2, 2))],
        10**4,
        10**5,
        aliases={2: 0, 3: 1},
        anywhere=(2, 3),
        out_anywhere=True,
    )
    x_before = lax.ppermute(x_up, "grp", x_ways[0])
    x_after = lax.ppermute(x_down, "grp", x_ways[1])
    tall = VMEM((SLABS, TALL, LANES), F32)
    flat = (EDGE * EDGE, LANES)
    outs = call(
        sweep,
        (counts, own, shell, core, y_before, y_after, x_before, x_after),
        [flat, flat],
        [tall] * 6,
        10**8,
        5 * 10**6,
    )
    return tuple(out.reshape(EDGE, EDGE, LANES) for out in outs)


def solution(mesh):
    placed = (P(None, ("grp", "dev"), None, None), P())
    return jax.shard_map(
        per_device,
        mesh=mesh,
        in_specs=placed,
        out_specs=(P("grp", "dev", None), P("grp", "dev", None)),
        check_vma=False,
    )
```

```python
import jax
import jax.numpy as jnp
from jax import lax
from jax.experimental import pallas as pl
from jax.experimental.pallas import tpu as pltpu
from jax.sharding import PartitionSpec as P

EDGE = 32
LANES = 128
GROUPS = EDGE * EDGE // LANES
COLUMN = 4
FIELDS = 3
MOVED = 2
KINDS = 5
SHELL = GROUPS + 6
CORE = 3 * (GROUPS - 2)
ROWS = EDGE + 16
DEEP = EDGE + 8
XMSG = EDGE + 4
F32 = jnp.float32
VMEM = pltpu.VMEM


def iota(shape, dim):
    return lax.broadcasted_iota(jnp.int32, shape, dim)


def moved_boxes(counts_ref):
    device = lax.axis_index("grp") * lax.axis_size("dev") + lax.axis_index("dev")
    counts = counts_ref[...]
    index = iota(counts.shape, 0) * LANES + iota(counts.shape, 1)
    start = jnp.sum(jnp.where(index < device, counts, 0))
    return jnp.clip(start - device * COLUMN, 0, MOVED)


def lane_group(g):
    return pl.ds(g * LANES, LANES)


def fetch(counts_ref, old_ref, counts, boxes, sems, first):
    copies = [pltpu.make_async_copy(counts_ref, counts, sems.at[FIELDS])]
    for f in range(FIELDS):
        copies.append(pltpu.make_async_copy(old_ref.at[f, pl.ds(first, COLUMN)], boxes.at[f], sems.at[f]))
    for copy in copies:
        copy.start()
    copies[0].wait()
    return copies[1:], moved_boxes(counts)


def box_tiles(boxes, f, c, g, which):
    low = iota((8, LANES), 0) < 4
    if which == "edge":
        return jnp.where(low, boxes[f, c, 0:8, lane_group(g)], boxes[f, c, 24:32, lane_group(g)])
    if which == 0:
        return jnp.where(low, boxes[f, c, 24:32, lane_group(g)], boxes[f, c, 0:8, lane_group(g)])
    return boxes[f, c, 8 * which : 8 * which + 8, lane_group(g)]


def pack(boxes, moved, out, at, g, which):
    shape = (8, LANES)
    lane = iota(shape, 1)
    block = lane // EDGE
    black = (iota(shape, 0) + block + lane) % 2 == 1
    even = block % 2 == 0
    first, second = [
        [box_tiles(boxes, f, MOVED + c - moved, g, which) for f in range(FIELDS)] for c in range(MOVED)
    ]
    turned = [pltpu.roll(v, EDGE, 1) for v in second]
    out[0, at] = jnp.where(black, first[0], turned[0])
    for f in (1, 2):
        out[2 * f - 1, at] = jnp.where(even, first[f], turned[f])
        out[2 * f, at] = jnp.where(even, turned[f], first[f])


def pack_shell(counts_ref, old_ref, out, counts, boxes, sems):
    copies, moved = fetch(counts_ref, old_ref, counts, boxes, sems, MOVED)
    for copy in copies:
        copy.wait()
    for g in range(GROUPS):
        pack(boxes, moved, out, g, g, "edge")
    for side, g in enumerate((0, GROUPS - 1)):
        for which in range(3):
            pack(boxes, moved, out, GROUPS + 3 * side + which, g, which)


def pack_core(counts_ref, old_ref, out, counts, boxes, sems):
    copies, moved = fetch(counts_ref, old_ref, counts, boxes, sems, MOVED)
    for copy in copies:
        copy.wait()
    for g in range(1, GROUPS - 1):
        for which in range(3):
            pack(boxes, moved, out, 3 * (g - 1) + which, g, which)


def interleave(v):
    lane = iota(v[0].shape, 1)
    half = lane < 2 * EDGE
    even = (lane // EDGE) % 2 == 0
    w = [pltpu.roll(a, 2 * EDGE, 1) for a in v]
    a0, a1 = jnp.where(half, v[0], w[2]), jnp.where(half, v[1], w[3])
    a2, a3 = jnp.where(half, w[0], v[2]), jnp.where(half, w[1], v[3])
    rows = []
    for a, b in ((a0, a1), (a2, a3)):
        rows.append(jnp.where(even, a, pltpu.roll(b, EDGE, 1)))
        rows.append(jnp.where(even, pltpu.roll(a, LANES - EDGE, 1), b))
    return rows


def relayout_edges(counts_ref, old_ref, edges, slabs, counts, boxes, sems):
    copies, moved = fetch(counts_ref, old_ref, counts, boxes, sems, 0)
    slots = [jnp.maximum(c - moved, 0) for c in range(COLUMN)]
    for f in range(FIELDS):
        copies[f].wait()
        for g in range(GROUPS):
            for r, row in enumerate(interleave([box_tiles(boxes, f, slot, g, "edge") for slot in slots])):
                edges[f, 4 * g + r] = row
        for side, g in enumerate((0, GROUPS - 1)):
            for r, row in enumerate(interleave([boxes[f, slot, :, lane_group(g)] for slot in slots])):
                slabs[f, side, r] = row


def relayout(counts_ref, old_ref, out, counts, boxes, sems):
    copies, moved = fetch(counts_ref, old_ref, counts, boxes, sems, 0)
    slots = [jnp.maximum(c - moved, 0) for c in range(COLUMN)]
    for f in range(FIELDS):
        copies[f].wait()
        for g in range(GROUPS):
            for r, row in enumerate(interleave([boxes[f, slot, :, lane_group(g)] for slot in slots])):
                out[f, 4 * g + r] = row


def unmix(kinds, f):
    if f == 0:
        a = b = kinds[0]
    else:
        a, b = kinds[2 * f - 1], kinds[2 * f]
    return [a, pltpu.roll(b, LANES - EDGE, 1), pltpu.roll(a, 2 * EDGE, 1), pltpu.roll(b, EDGE, 1)]


def wire_rows(shell, core, k, g):
    low = iota((8, LANES), 0) < 4
    edge = shell[k, g]
    if g in (0, GROUPS - 1):
        base = GROUPS + (3 if g else 0)
        mid = [shell[k, base + which] for which in range(3)]
    else:
        mid = [core[k, 3 * (g - 1) + which] for which in range(3)]
    return jnp.concatenate([jnp.where(low, edge, mid[0]), mid[1], mid[2], jnp.where(low, mid[0], edge)], axis=0)


def pack_x(pressure, right_side, coefficient):
    row = iota((8, LANES), 0)
    high = jnp.where(
        row >= 5, coefficient, jnp.where(row >= 2, pltpu.roll(pressure, 5, 0), pltpu.roll(right_side, 2, 0))
    )
    low = jnp.where(
        row < 3, coefficient, jnp.where(row < 6, pltpu.roll(pressure, 3, 0), pltpu.roll(right_side, 6, 0))
    )
    return high, low


def make_faces(counts_ref, shell, edges, slabs, y_up, y_down, x_up, x_down):
    limit = moved_boxes(counts_ref) * EDGE
    taken = iota((EDGE, LANES), 1) < limit
    for side, g in enumerate((0, GROUPS - 1)):
        out = y_up if side else y_down
        kinds = [wire_rows(shell, None, k, g) for k in range(KINDS)]
        for f, at, depth in ((2, 0, 3), (0, 3, 3), (1, 6, 2)):
            rows = unmix(kinds, f)
            for j in range(depth):
                r = 4 - depth + j if side else j
                out[at + j] = jnp.where(taken, rows[r], slabs[f, side, r])
    taken = iota((8, LANES), 1) < limit
    for g in range(GROUPS):
        kinds = [shell[k, g] for k in range(KINDS)]
        rows = [unmix(kinds, f) for f in range(FIELDS)]
        for r in range(4):
            y = 4 * g + r
            edge = [jnp.where(taken, rows[f][r], edges[f, y]) for f in range(FIELDS)]
            x_up[y + 2], x_down[y + 2] = pack_x(*edge)


def add_corners(before, after, x_up_in, x_down_in, x_up, x_down, tiles, sems):
    del x_up_in, x_down_in
    low = iota((8, LANES), 0) < 4
    places = ((before, 1, 4, 6), (before, 2, 5, 7), (after, 0, 3, 6), (after, 1, 4, 7))
    for at, (ref, b, p, f) in enumerate(places):
        edge = [jnp.where(low, ref[i, 0:8], ref[i, 24:32]) for i in (p, f, b)]
        tiles[0, at], tiles[1, at] = pack_x(*edge)
    copies = []
    for way, out in enumerate((x_up, x_down)):
        for side in range(2):
            copies.append(
                pltpu.make_async_copy(
                    tiles.at[way, pl.ds(2 * side, 2)], out.at[pl.ds((XMSG - 2) * side, 2)], sems.at[way, side]
                )
            )
    for copy in copies:
        copy.start()
    for copy in copies:
        copy.wait()


def is_red(shape, shift):
    return (iota(shape, 0) + iota(shape, 1) + shift) & 1 == 0


def assemble(counts_ref, own, shell, core, half, mix, rhs):
    limit = moved_boxes(counts_ref) * EDGE
    taken = iota((EDGE, LANES), 1) < limit
    reds = [is_red((EDGE, LANES), y) for y in range(2)]
    before = None
    for g in range(GROUPS):
        kinds = [wire_rows(shell, core, k, g) for k in range(KINDS)]
        parts = [unmix(kinds, f) for f in range(FIELDS)]
        for r in range(4):
            y = 4 * g + r
            p, f, b = [jnp.where(taken, parts[i][r], own[i, y]) for i in range(FIELDS)]
            h = 0.5 * b
            half[y] = h
            rhs[y] = f
            if y:
                mix[y - 1] = jnp.where(reds[(y - 1) % 2], h * p, before)
            before = p
    mix[EDGE - 1] = before


def tile(row):
    return pl.ds(row, 8)


def sweep(
    half_in,
    mix_in,
    rhs_in,
    y_before,
    y_after,
    x_before,
    x_after,
    out_p,
    out_r,
    half,
    mix,
    rhs,
    mix2,
    mix3,
    new1,
    new2,
    inv,
    tot,
    rest,
):
    grp, dev = lax.axis_index("grp"), lax.axis_index("dev")
    inner = pl.ds(8, EDGE)
    red_rows = [is_red((EDGE, LANES), y) for y in range(2)]
    reds = [is_red((8, LANES), y) for y in range(2)]
    pressures, flux = {}, {}
    for y in (-3, -2, -1, 32, 33, 34):
        ref, k = (y_before, y + 3) if y < 0 else (y_after, y - 32)
        h = 0.5 * ref[k]
        half[y + 4, inner] = h
        pressures[y] = ref[3 + k]
        flux[y] = h * ref[3 + k]
        k = k - 1 if y < 0 else k
        if 0 <= k < 2:
            rhs[y + 4, inner] = ref[6 + k]
    flux[0] = half_in[0] * mix_in[0]
    pressures[EDGE - 1] = mix_in[EDGE - 1]

    def take_in(k, carry):
        for d in range(4):
            y = 4 * k + d
            half[y + 4, inner] = half_in[y]
            mix[y + 4, inner] = mix_in[y]
            rhs[y + 4, inner] = rhs_in[y]
        return carry

    lax.fori_loop(0, EDGE // 4, take_in, 0)
    zero = jnp.zeros((EDGE, LANES), F32)
    for y in (-4, -3, -2, -1, 31, 32, 33, 34):
        mix[y + 4, inner] = jnp.where(red_rows[y % 2], flux.get(y + 1, zero), pressures.get(y, zero))

    def strip(i, odd, last):
        j = i + 2
        rows = []
        for ref, at, turn_p, turn_f, kept in ((x_before, 0, 3, 6, last[0]), (x_after, ROWS - 8, 5, 2, last[1])):
            v = ref[i]
            h = 0.5 * v
            p = pltpu.roll(v, turn_p, 0)
            half[j, tile(at)] = h
            rhs[j, tile(at)] = pltpu.roll(v, turn_f, 0)
            mix[j, tile(at)] = jnp.where(reds[odd], kept, p)
            rows.append(h * p)
        return rows

    def strips(k, carry):
        i = XMSG - 1 - 4 * k
        for d in range(4):
            carry = strip(i - d, (1 + d) % 2, carry)
        return tuple(carry)

    nothing = jnp.zeros((8, LANES), F32)
    last = lax.fori_loop(0, XMSG // 4, strips, (nothing, nothing))
    mix[1, tile(0)], mix[1, tile(ROWS - 8)] = last

    lane = iota((8, LANES), 1)
    row = iota((8, LANES), 0)
    first_lane, last_lane = lane == 0, lane == LANES - 1

    def six(ref, j, top, count):
        sums = []
        for t in range(count):
            r = top + 8 * t
            v = ref[j, tile(r)]
            z = jnp.where(first_lane, 0.0, pltpu.roll(v, 1, 1)) + jnp.where(last_lane, 0.0, pltpu.roll(v, LANES - 1, 1))
            x = ref[j, tile(r - 1)] + ref[j, tile(r + 1)]
            sums.append((z + x) + (ref[j - 1, tile(r)] + ref[j + 1, tile(r)]))
        return sums

    open_x = [row >= 2 * (grp == 0).astype(jnp.int32), None, None, None]
    open_x.append(row < 8 - 6 * (grp == lax.axis_size("grp") - 1).astype(jnp.int32))

    def red(j, odd, carry, shut=None):
        flow_before, new_before = carry
        around = six(half, j, 6, 5)
        flow = six(mix, j, 6, 5)
        news = []
        for t in range(5):
            r = tile(6 + 8 * t)
            h = half[j, r]
            total = 6.0 * h + around[t]
            inverse = 1.0 / total
            if open_x[t] is not None:
                inverse = jnp.where(open_x[t], inverse, 0.0)
            if shut is not None:
                inverse = jnp.where(row >= 8 * shut, inverse, 0.0)
            new = (rhs[j, r] + (h * flow[t] + flow_before[t])) * inverse
            new1[j, r] = new
            inv[j, r] = inverse
            tot[j, r] = total
            mix2[j - 1, r] = jnp.where(reds[1 - odd], new_before[t], h * new)
            news.append(new)
        return flow, news

    def black(j, odd, carry):
        flow_before, new_before = carry
        flow = six(mix2, j, 7, 5)
        news = []
        for t in range(5):
            r = tile(7 + 8 * t)
            h = half[j, r]
            full = rhs[j, r] + (h * flow[t] + flow_before[t])
            new = full * inv[j, r]
            new2[j, r] = new
            rest[j, r] = full - tot[j, r] * new
            mix3[j - 1, r] = jnp.where(reds[1 - odd], new_before[t], h * new)
            news.append(new)
        return flow, news

    def finish(j, odd, flow_before):
        flow = six(mix3, j, 8, 4)
        for t in range(4):
            r = tile(8 + 8 * t)
            mine = new1[j, r]
            left = (rhs[j, r] + (half[j, r] * flow[t] + flow_before[t])) - tot[j, r] * mine
            rows = pl.ds(j - 4 + 8 * t * EDGE, 8, stride=EDGE)
            out_p[rows, :] = jnp.where(reds[odd], mine, new2[j, r])
            out_r[rows, :] = jnp.where(reds[odd], left, rest[j, r])
        return flow

    low_shut = (dev == 0).astype(jnp.int32)
    high_shut = (dev == lax.axis_size("dev") - 1).astype(jnp.int32)

    def reds_step(k, carry):
        for d in range(4):
            carry = red(4 + 4 * k + d, d % 2, carry)
        return carry

    carry = (six(mix, 1, 6, 5), [nothing] * 5)
    carry = red(2, 0, carry, low_shut)
    carry = red(3, 1, carry, low_shut)
    carry = lax.fori_loop(0, EDGE // 4, reds_step, carry)
    carry = red(EDGE + 4, 0, carry, high_shut)
    carry = red(EDGE + 5, 1, carry, high_shut)
    for t in range(5):
        mix2[EDGE + 5, tile(6 + 8 * t)] = carry[1][t]

    def blacks_step(k, carry):
        for d in range(4):
            carry = black(4 + 4 * k + d, d % 2, carry)
        return carry

    carry = (six(mix2, 2, 7, 5), [nothing] * 5)
    carry = black(3, 1, carry)
    carry = lax.fori_loop(0, EDGE // 4, blacks_step, carry)
    carry = black(EDGE + 4, 0, carry)
    for t in range(5):
        mix3[EDGE + 4, tile(7 + 8 * t)] = carry[1][t]

    def finish_step(k, flow):
        for d in range(4):
            flow = finish(4 + 4 * k + d, d % 2, flow)
        return flow

    lax.fori_loop(0, EDGE // 4, finish_step, six(mix3, 3, 8, 4))


def call(body, inputs, outputs, scratch, flops, moved, aliases=None, hbm=(), anywhere=False, limit=40 * 2**20):
    vmem, place, far = [pl.BlockSpec(memory_space=m) for m in (pltpu.VMEM, pl.ANY, pltpu.HBM)]
    kept = set(aliases or {}) if anywhere else ()
    return pl.pallas_call(
        body,
        out_shape=[jax.ShapeDtypeStruct(shape, F32) for shape in outputs],
        in_specs=[far if i in hbm else place if i in kept else vmem for i in range(len(inputs))],
        out_specs=[place if anywhere else vmem for _ in outputs],
        scratch_shapes=scratch,
        input_output_aliases=aliases or {},
        cost_estimate=pl.CostEstimate(flops=flops, bytes_accessed=moved, transcendentals=0),
        compiler_params=pltpu.CompilerParams(vmem_limit_bytes=limit),
        name=body.__name__,
    )(*inputs)


def per_device(old_fields, old_counts):
    groups, columns = lax.axis_size("grp"), lax.axis_size("dev")
    devices = groups * columns
    counts = jnp.pad(old_counts, (0, -devices % LANES)).reshape(-1, LANES)
    chain = [(i, i + 1) for i in range(devices - 1)]

    def ends(count):
        up = [(i, i + 1) for i in range(count - 1)]
        return up, [(j, i) for i, j in up]

    y_ways, x_ways = ends(columns), ends(groups)

    def read(body, outputs, after=None):
        table = counts if after is None else lax.optimization_barrier((counts, after))[0]
        scratch = [
            VMEM(counts.shape, jnp.int32),
            VMEM((FIELDS, COLUMN, EDGE, EDGE * EDGE), F32),
            pltpu.SemaphoreType.DMA((FIELDS + 1,)),
        ]
        return call(body, (table, old_fields), outputs, scratch, 10**6, 2 * 10**6, hbm=(0, 1), limit=40 * 2**20 if after is not None else 54400000)

    face, strip = (8, EDGE, LANES), (XMSG, 8, LANES)
    deep = (DEEP, ROWS, LANES)
    (shell,) = read(pack_shell, [(KINDS, SHELL, 8, LANES)])
    shell = lax.ppermute(shell, ("grp", "dev"), chain)
    (core,) = read(pack_core, [(KINDS, CORE, 8, LANES)])
    core = lax.ppermute(core, ("grp", "dev"), chain)
    edges, slabs = read(relayout_edges, [(FIELDS, EDGE, 8, LANES), (FIELDS, 2, 4, EDGE, LANES)])
    y_up, y_down, x_up, x_down = call(
        make_faces, (counts, shell, edges, slabs), [face, face, strip, strip], [], 10**6, 10**6
    )
    (own,) = read(relayout, [(FIELDS, EDGE, EDGE, LANES)], y_up)
    y_before = lax.ppermute(y_up, "dev", y_ways[0])
    y_after = lax.ppermute(y_down, "dev", y_ways[1])
    x_up, x_down = call(
        add_corners,
        (y_before, y_after, x_up, x_down),
        [strip, strip],
        [VMEM((2, 4, 8, LANES), F32), pltpu.SemaphoreType.DMA((2, 2))],
        10**4,
        10**5,
        aliases={2: 0, 3: 1},
        anywhere=True,
    )
    x_before = lax.ppermute(x_up, "grp", x_ways[0])
    x_after = lax.ppermute(x_down, "grp", x_ways[1])
    table = lax.optimization_barrier((counts, x_up))[0]
    half, mix, rhs = call(assemble, (table, own, shell, core), [(EDGE, EDGE, LANES)] * 3, [], 10**6, 10**6)
    flat = (EDGE * EDGE, LANES)
    outs = call(
        sweep,
        (half, mix, rhs, y_before, y_after, x_before, x_after),
        [flat, flat],
        [VMEM(deep, F32)] * 10,
        10**8,
        5 * 10**6,
    )
    return tuple(out.reshape(EDGE, EDGE, LANES) for out in outs)


def solution(mesh):
    placed = (P(None, ("grp", "dev"), None, None), P())
    return jax.shard_map(
        per_device,
        mesh=mesh,
        in_specs=placed,
        out_specs=(P("grp", "dev", None), P("grp", "dev", None)),
        check_vma=False,
    )
```

```python
import jax
import jax.numpy as jnp
from jax import lax
from jax.experimental import pallas as pl
from jax.experimental.pallas import tpu as pltpu
from jax.sharding import PartitionSpec as P


EDGE = 32
LANES = 128
GROUPS = EDGE * EDGE // LANES
COLUMN = 4
FIELDS = 3
MOVED = 2
KINDS = 5
CORE = 3 * GROUPS
ROWS = EDGE + 16
DEEP = EDGE + 8
YMSG = 8 * EDGE + 32
F32 = jnp.float32
VMEM = pltpu.VMEM


def iota(shape, dim):
    return lax.broadcasted_iota(jnp.int32, shape, dim)


def moved_boxes(counts_ref):
    device = lax.axis_index("grp") * lax.axis_size("dev") + lax.axis_index("dev")
    counts = counts_ref[...]
    index = iota(counts.shape, 0) * LANES + iota(counts.shape, 1)
    start = jnp.sum(jnp.where(index < device, counts, 0))
    return jnp.clip(start - device * COLUMN, 0, MOVED)


def lane_group(g):
    return pl.ds(g * LANES, LANES)


def fetch(counts_ref, old_ref, counts, boxes, sems, first):
    copies = [pltpu.make_async_copy(counts_ref, counts, sems.at[FIELDS])]
    for f in range(FIELDS):
        copies.append(pltpu.make_async_copy(old_ref.at[f, pl.ds(first, COLUMN)], boxes.at[f], sems.at[f]))
    for copy in copies:
        copy.start()
    copies[0].wait()
    return copies[1:], moved_boxes(counts)


def box_tiles(boxes, f, c, g, which):
    low = iota((8, LANES), 0) < 4
    if which == "edge":
        return jnp.where(low, boxes[f, c, 0:8, lane_group(g)], boxes[f, c, 24:32, lane_group(g)])
    if which == 0:
        return jnp.where(low, boxes[f, c, 24:32, lane_group(g)], boxes[f, c, 0:8, lane_group(g)])
    return boxes[f, c, 8 * which : 8 * which + 8, lane_group(g)]


def pack(boxes, moved, out, at, g, which):
    shape = (8, LANES)
    lane = iota(shape, 1)
    block = lane // EDGE
    black = (iota(shape, 0) + block + lane) % 2 == 1
    even = block % 2 == 0
    first, second = [
        [box_tiles(boxes, f, MOVED + c - moved, g, which) for f in range(FIELDS)] for c in range(MOVED)
    ]
    turned = [pltpu.roll(v, EDGE, 1) for v in second]
    out[0, at] = jnp.where(black, first[0], turned[0])
    for f in (1, 2):
        out[2 * f - 1, at] = jnp.where(even, first[f], turned[f])
        out[2 * f, at] = jnp.where(even, turned[f], first[f])


def pack_shell(counts_ref, old_ref, out, counts, boxes, sems):
    copies, moved = fetch(counts_ref, old_ref, counts, boxes, sems, MOVED)
    for copy in copies:
        copy.wait()
    for g in range(GROUPS):
        pack(boxes, moved, out, g, g, "edge")


def pack_core(counts_ref, old_ref, out, counts, boxes, sems):
    copies, moved = fetch(counts_ref, old_ref, counts, boxes, sems, MOVED)
    for copy in copies:
        copy.wait()
    for g in range(GROUPS):
        for which in range(3):
            pack(boxes, moved, out, 3 * g + which, g, which)


def interleave(v):
    lane = iota(v[0].shape, 1)
    half = lane < 2 * EDGE
    even = (lane // EDGE) % 2 == 0
    w = [pltpu.roll(a, 2 * EDGE, 1) for a in v]
    a0, a1 = jnp.where(half, v[0], w[2]), jnp.where(half, v[1], w[3])
    a2, a3 = jnp.where(half, w[0], v[2]), jnp.where(half, w[1], v[3])
    rows = []
    for a, b in ((a0, a1), (a2, a3)):
        rows.append(jnp.where(even, a, pltpu.roll(b, EDGE, 1)))
        rows.append(jnp.where(even, pltpu.roll(a, LANES - EDGE, 1), b))
    return rows


def relayout_edges(counts_ref, old_ref, edges, counts, boxes, sems):
    copies, moved = fetch(counts_ref, old_ref, counts, boxes, sems, 0)
    slots = [jnp.maximum(c - moved, 0) for c in range(COLUMN)]
    for f in range(FIELDS):
        copies[f].wait()
        for g in range(GROUPS):
            for r, row in enumerate(interleave([box_tiles(boxes, f, slot, g, "edge") for slot in slots])):
                edges[f, 4 * g + r] = row


def relayout(counts_ref, old_ref, out, counts, boxes, sems):
    copies, moved = fetch(counts_ref, old_ref, counts, boxes, sems, 0)
    slots = [jnp.maximum(c - moved, 0) for c in range(COLUMN)]
    for f in range(FIELDS):
        copies[f].wait()
        for g in range(GROUPS):
            for r, row in enumerate(interleave([boxes[f, slot, :, lane_group(g)] for slot in slots])):
                out[f, 4 * g + r] = row


def unmix(kinds, f):
    if f == 0:
        a = b = kinds[0]
    else:
        a, b = kinds[2 * f - 1], kinds[2 * f]
    return [a, pltpu.roll(b, LANES - EDGE, 1), pltpu.roll(a, 2 * EDGE, 1), pltpu.roll(b, EDGE, 1)]


def wire_rows(shell, core, k, g):
    low = iota((8, LANES), 0) < 4
    edge = shell[k, g]
    mid = [core[k, 3 * g + which] for which in range(3)]
    return jnp.concatenate([jnp.where(low, edge, mid[0]), mid[1], mid[2], jnp.where(low, mid[0], edge)], axis=0)


def pack_x(pressure, right_side, coefficient):
    row = iota((8, LANES), 0)
    high = jnp.where(
        row >= 5, coefficient, jnp.where(row >= 2, pltpu.roll(pressure, 5, 0), pltpu.roll(right_side, 2, 0))
    )
    low = jnp.where(
        row < 3, coefficient, jnp.where(row < 6, pltpu.roll(pressure, 3, 0), pltpu.roll(right_side, 6, 0))
    )
    return high, low


def make_faces(counts_ref, shell, edges, x_up, x_down):
    limit = moved_boxes(counts_ref) * EDGE
    taken = iota((8, LANES), 1) < limit
    for g in range(GROUPS):
        kinds = [shell[k, g] for k in range(KINDS)]
        rows = [unmix(kinds, f) for f in range(FIELDS)]
        for r in range(4):
            y = 4 * g + r
            edge = [jnp.where(taken, rows[f][r], edges[f, y]) for f in range(FIELDS)]
            x_up[y], x_down[y] = pack_x(*edge)


def add_corners(before, after, y_up_in, y_down_in, y_up, y_down, sems):
    del y_up_in, y_down_in
    copies = []
    for way, (out, first) in enumerate(((y_up, EDGE - 2), (y_down, 0))):
        for d in range(2):
            for side, ref in enumerate((before, after)):
                at = 8 * EDGE + 8 * (2 * d + side)
                copies.append(pltpu.make_async_copy(ref.at[first + d], out.at[pl.ds(at, 8)], sems.at[way, d, side]))
    for copy in copies:
        copy.start()
    for copy in copies:
        copy.wait()


def is_red(shape, shift):
    return (iota(shape, 0) + iota(shape, 1) + shift) & 1 == 0


def assemble(counts_ref, own, shell, core, half, mix, rhs, y_up, y_down):
    limit = moved_boxes(counts_ref) * EDGE
    taken = iota((EDGE, LANES), 1) < limit
    reds = [is_red((EDGE, LANES), y) for y in range(2)]
    before = None
    for g in range(GROUPS):
        kinds = [wire_rows(shell, core, k, g) for k in range(KINDS)]
        parts = [unmix(kinds, f) for f in range(FIELDS)]
        for r in range(4):
            y = 4 * g + r
            p, f, b = [jnp.where(taken, parts[i][r], own[i, y]) for i in range(FIELDS)]
            h = 0.5 * b
            half[y] = h
            rhs[y] = f
            if y:
                mix[y - 1] = jnp.where(reds[(y - 1) % 2], h * p, before)
            before = p
    mix[EDGE - 1] = before
    for out, first, thin in ((y_up, EDGE - 3, EDGE - 2), (y_down, 0, 0)):
        for i in range(3):
            out[EDGE * i : EDGE * (i + 1)] = half[first + i]
            out[EDGE * (3 + i) : EDGE * (4 + i)] = mix[first + i]
        for i in range(2):
            out[EDGE * (6 + i) : EDGE * (7 + i)] = rhs[thin + i]


def tile(row):
    return pl.ds(row, 8)


def sweep(
    half_in,
    mix_in,
    rhs_in,
    y_before,
    y_after,
    x_before,
    x_after,
    out_p,
    out_r,
    half,
    mix,
    rhs,
    mix2,
    mix3,
    new1,
    new2,
    inv,
    tot,
    rest,
):
    grp, dev = lax.axis_index("grp"), lax.axis_index("dev")
    inner = pl.ds(8, EDGE)
    red_rows = [is_red((EDGE, LANES), y) for y in range(2)]
    reds = [is_red((8, LANES), y) for y in range(2)]
    pressures, flux = {}, {}
    for y in (-3, -2, -1, 32, 33, 34):
        ref, k = (y_before, y + 3) if y < 0 else (y_after, y - 32)
        h, p = [ref[EDGE * i : EDGE * (i + 1)] for i in (k, 3 + k)]
        half[y + 4, inner] = h
        pressures[y] = p
        flux[y] = h * p
        k = k - 1 if y < 0 else k
        if 0 <= k < 2:
            rhs[y + 4, inner] = ref[EDGE * (6 + k) : EDGE * (7 + k)]
    flux[0] = half_in[0] * mix_in[0]
    pressures[EDGE - 1] = mix_in[EDGE - 1]

    def take_in(k, carry):
        for d in range(4):
            y = 4 * k + d
            half[y + 4, inner] = half_in[y]
            mix[y + 4, inner] = mix_in[y]
            rhs[y + 4, inner] = rhs_in[y]
        return carry

    lax.fori_loop(0, EDGE // 4, take_in, 0)
    zero = jnp.zeros((EDGE, LANES), F32)
    for y in (-4, -3, -2, -1, 31, 32, 33, 34):
        mix[y + 4, inner] = jnp.where(red_rows[y % 2], flux.get(y + 1, zero), pressures.get(y, zero))

    def strip(j, odd, values, last):
        rows = []
        for v, at, turn_p, turn_f, kept in zip(values, (0, ROWS - 8), (3, 5), (6, 2), last):
            h = 0.5 * v
            p = pltpu.roll(v, turn_p, 0)
            half[j, tile(at)] = h
            rhs[j, tile(at)] = pltpu.roll(v, turn_f, 0)
            mix[j, tile(at)] = jnp.where(reds[odd], kept, p)
            rows.append(h * p)
        return tuple(rows)

    def strips(k, carry):
        for d in range(4):
            y = EDGE - 1 - 4 * k - d
            carry = strip(y + 4, (1 + d) % 2, (x_before[y], x_after[y]), carry)
        return carry

    def corners(ref, d):
        return [ref[pl.ds(8 * EDGE + 8 * (2 * d + side), 8)] for side in range(2)]

    nothing = jnp.zeros((8, LANES), F32)
    last = (nothing, nothing)
    for d in (1, 0):
        last = strip(EDGE + 4 + d, d, corners(y_after, d), last)
    last = lax.fori_loop(0, EDGE // 4, strips, last)
    for d in (1, 0):
        last = strip(2 + d, d, corners(y_before, d), last)
    mix[1, tile(0)], mix[1, tile(ROWS - 8)] = last

    lane = iota((8, LANES), 1)
    row = iota((8, LANES), 0)
    first_lane, last_lane = lane == 0, lane == LANES - 1

    def six(ref, j, top, count):
        sums = []
        for t in range(count):
            r = top + 8 * t
            v = ref[j, tile(r)]
            z = jnp.where(first_lane, 0.0, pltpu.roll(v, 1, 1)) + jnp.where(last_lane, 0.0, pltpu.roll(v, LANES - 1, 1))
            x = ref[j, tile(r - 1)] + ref[j, tile(r + 1)]
            sums.append((z + x) + (ref[j - 1, tile(r)] + ref[j + 1, tile(r)]))
        return sums

    open_x = [row >= 2 * (grp == 0).astype(jnp.int32), None, None, None]
    open_x.append(row < 8 - 6 * (grp == lax.axis_size("grp") - 1).astype(jnp.int32))

    def red(j, odd, carry, shut=None):
        flow_before, new_before = carry
        around = six(half, j, 6, 5)
        flow = six(mix, j, 6, 5)
        news = []
        for t in range(5):
            r = tile(6 + 8 * t)
            h = half[j, r]
            total = 6.0 * h + around[t]
            inverse = 1.0 / total
            if open_x[t] is not None:
                inverse = jnp.where(open_x[t], inverse, 0.0)
            if shut is not None:
                inverse = jnp.where(row >= 8 * shut, inverse, 0.0)
            new = (rhs[j, r] + (h * flow[t] + flow_before[t])) * inverse
            new1[j, r] = new
            inv[j, r] = inverse
            tot[j, r] = total
            mix2[j - 1, r] = jnp.where(reds[1 - odd], new_before[t], h * new)
            news.append(new)
        return flow, news

    def black(j, odd, carry):
        flow_before, new_before = carry
        flow = six(mix2, j, 7, 5)
        news = []
        for t in range(5):
            r = tile(7 + 8 * t)
            h = half[j, r]
            full = rhs[j, r] + (h * flow[t] + flow_before[t])
            new = full * inv[j, r]
            new2[j, r] = new
            rest[j, r] = full - tot[j, r] * new
            mix3[j - 1, r] = jnp.where(reds[1 - odd], new_before[t], h * new)
            news.append(new)
        return flow, news

    def finish(j, odd, flow_before):
        flow = six(mix3, j, 8, 4)
        for t in range(4):
            r = tile(8 + 8 * t)
            mine = new1[j, r]
            left = (rhs[j, r] + (half[j, r] * flow[t] + flow_before[t])) - tot[j, r] * mine
            rows = pl.ds(j - 4 + 8 * t * EDGE, 8, stride=EDGE)
            out_p[rows, :] = jnp.where(reds[odd], mine, new2[j, r])
            out_r[rows, :] = jnp.where(reds[odd], left, rest[j, r])
        return flow

    low_shut = (dev == 0).astype(jnp.int32)
    high_shut = (dev == lax.axis_size("dev") - 1).astype(jnp.int32)

    def reds_step(k, carry):
        for d in range(4):
            carry = red(4 + 4 * k + d, d % 2, carry)
        return carry

    carry = (six(mix, 1, 6, 5), [nothing] * 5)
    carry = red(2, 0, carry, low_shut)
    carry = red(3, 1, carry, low_shut)
    carry = lax.fori_loop(0, EDGE // 4, reds_step, carry)
    carry = red(EDGE + 4, 0, carry, high_shut)
    carry = red(EDGE + 5, 1, carry, high_shut)
    for t in range(5):
        mix2[EDGE + 5, tile(6 + 8 * t)] = carry[1][t]

    def blacks_step(k, carry):
        for d in range(4):
            carry = black(4 + 4 * k + d, d % 2, carry)
        return carry

    carry = (six(mix2, 2, 7, 5), [nothing] * 5)
    carry = black(3, 1, carry)
    carry = lax.fori_loop(0, EDGE // 4, blacks_step, carry)
    carry = black(EDGE + 4, 0, carry)
    for t in range(5):
        mix3[EDGE + 4, tile(7 + 8 * t)] = carry[1][t]

    def finish_step(k, flow):
        for d in range(4):
            flow = finish(4 + 4 * k + d, d % 2, flow)
        return flow

    lax.fori_loop(0, EDGE // 4, finish_step, six(mix3, 3, 8, 4))


def call(body, inputs, outputs, scratch, flops, moved, aliases=None, hbm=(), anywhere=False, limit=40 * 2**20):
    vmem, place, far = [pl.BlockSpec(memory_space=m) for m in (pltpu.VMEM, pl.ANY, pltpu.HBM)]
    kept = range(len(inputs)) if anywhere else ()
    return pl.pallas_call(
        body,
        out_shape=[jax.ShapeDtypeStruct(shape, F32) for shape in outputs],
        in_specs=[far if i in hbm else place if i in kept else vmem for i in range(len(inputs))],
        out_specs=[place if anywhere else vmem for _ in outputs],
        scratch_shapes=scratch,
        input_output_aliases=aliases or {},
        cost_estimate=pl.CostEstimate(flops=flops, bytes_accessed=moved, transcendentals=0),
        compiler_params=pltpu.CompilerParams(vmem_limit_bytes=limit),
    )(*inputs)


def per_device(old_fields, old_counts):
    groups, columns = lax.axis_size("grp"), lax.axis_size("dev")
    devices = groups * columns
    counts = jnp.pad(old_counts, (0, -devices % LANES)).reshape(-1, LANES)
    chain = [(i, i + 1) for i in range(devices - 1)]

    def ends(count):
        up = [(i, i + 1) for i in range(count - 1)]
        return up, [(j, i) for i, j in up]

    y_ways, x_ways = ends(columns), ends(groups)

    def read(body, outputs, after=None, limit=54400000):
        table = counts if after is None else lax.optimization_barrier((counts, after))[0]
        scratch = [
            VMEM(counts.shape, jnp.int32),
            VMEM((FIELDS, COLUMN, EDGE, EDGE * EDGE), F32),
            pltpu.SemaphoreType.DMA((FIELDS + 1,)),
        ]
        return call(body, (table, old_fields), outputs, scratch, 10**6, 2 * 10**6, hbm=(0, 1), limit=limit)

    strip, message = (EDGE, 8, LANES), (YMSG, LANES)
    deep, block = (DEEP, ROWS, LANES), (EDGE, EDGE, LANES)
    (shell,) = read(pack_shell, [(KINDS, GROUPS, 8, LANES)])
    (core,) = read(pack_core, [(KINDS, CORE, 8, LANES)], shell)
    shell = lax.ppermute(shell, ("grp", "dev"), chain)
    core = lax.ppermute(core, ("grp", "dev"), chain)
    (edges,) = read(relayout_edges, [(FIELDS, EDGE, 8, LANES)])
    x_up, x_down = call(make_faces, (counts, shell, edges), [strip, strip], [], 10**6, 10**6)
    x_before = lax.ppermute(x_up, "grp", x_ways[0])
    x_after = lax.ppermute(x_down, "grp", x_ways[1])
    (own,) = read(relayout, [(FIELDS, EDGE, EDGE, LANES)], x_up, 40 * 2**20)
    half, mix, rhs, y_up, y_down = call(
        assemble, (counts, own, shell, core), [block, block, block, message, message], [], 10**6, 10**6
    )
    y_up, y_down = call(
        add_corners,
        (x_before, x_after, y_up, y_down),
        [message, message],
        [pltpu.SemaphoreType.DMA((2, 2, 2))],
        10**4,
        10**5,
        aliases={2: 0, 3: 1},
        anywhere=True,
    )
    y_before = lax.ppermute(y_up, "dev", y_ways[0])
    y_after = lax.ppermute(y_down, "dev", y_ways[1])
    flat = (EDGE * EDGE, LANES)
    outs = call(
        sweep,
        (half, mix, rhs, y_before, y_after, x_before, x_after),
        [flat, flat],
        [VMEM(deep, F32)] * 10,
        10**8,
        5 * 10**6,
    )
    return tuple(out.reshape(EDGE, EDGE, LANES) for out in outs)


def solution(mesh):
    placed = (P(None, ("grp", "dev"), None, None), P())
    return jax.shard_map(
        per_device,
        mesh=mesh,
        in_specs=placed,
        out_specs=(P("grp", "dev", None), P("grp", "dev", None)),
        check_vma=False,
    )
```

```python
import jax
import jax.numpy as jnp
from jax import lax
from jax.experimental import pallas as pl
from jax.experimental.pallas import tpu as pltpu
from jax.sharding import PartitionSpec as P


EDGE = 32
LANES = 128
GROUPS = EDGE * EDGE // LANES
COLUMN = 4
FIELDS = 3
MOVED = 2
KINDS = 5
RIM = 6
CORE = 3 * (GROUPS - 2)
ROWS = EDGE + 16
DEEP = EDGE + 8
YMSG = 8 * EDGE + 32
F32 = jnp.float32
VMEM = pltpu.VMEM


def iota(shape, dim):
    return lax.broadcasted_iota(jnp.int32, shape, dim)


def moved_boxes(counts_ref):
    device = lax.axis_index("grp") * lax.axis_size("dev") + lax.axis_index("dev")
    counts = counts_ref[...]
    index = iota(counts.shape, 0) * LANES + iota(counts.shape, 1)
    start = jnp.sum(jnp.where(index < device, counts, 0))
    return jnp.clip(start - device * COLUMN, 0, MOVED)


def lane_group(g):
    return pl.ds(g * LANES, LANES)


def fetch(counts_ref, old_ref, counts, boxes, sems, first):
    copies = [pltpu.make_async_copy(counts_ref, counts, sems.at[FIELDS])]
    for f in range(FIELDS):
        copies.append(pltpu.make_async_copy(old_ref.at[f, pl.ds(first, COLUMN)], boxes.at[f], sems.at[f]))
    for copy in copies:
        copy.start()
    copies[0].wait()
    return copies[1:], moved_boxes(counts)


def box_tiles(boxes, f, c, g, which):
    low = iota((8, LANES), 0) < 4
    if which == "edge":
        return jnp.where(low, boxes[f, c, 0:8, lane_group(g)], boxes[f, c, 24:32, lane_group(g)])
    if which == 0:
        return jnp.where(low, boxes[f, c, 24:32, lane_group(g)], boxes[f, c, 0:8, lane_group(g)])
    return boxes[f, c, 8 * which : 8 * which + 8, lane_group(g)]


def pack(boxes, moved, out, at, g, which):
    shape = (8, LANES)
    lane = iota(shape, 1)
    block = lane // EDGE
    black = (iota(shape, 0) + block + lane) % 2 == 1
    even = block % 2 == 0
    first, second = [
        [box_tiles(boxes, f, MOVED + c - moved, g, which) for f in range(FIELDS)] for c in range(MOVED)
    ]
    turned = [pltpu.roll(v, EDGE, 1) for v in second]
    out[0, at] = jnp.where(black, first[0], turned[0])
    for f in (1, 2):
        out[2 * f - 1, at] = jnp.where(even, first[f], turned[f])
        out[2 * f, at] = jnp.where(even, turned[f], first[f])


def pack_shell(counts_ref, old_ref, out, counts, boxes, sems):
    copies, moved = fetch(counts_ref, old_ref, counts, boxes, sems, MOVED)
    for copy in copies:
        copy.wait()
    for g in range(GROUPS):
        pack(boxes, moved, out, g, g, "edge")


def pack_rest(counts_ref, old_ref, rim, core, counts, boxes, sems):
    copies, moved = fetch(counts_ref, old_ref, counts, boxes, sems, MOVED)
    for copy in copies:
        copy.wait()
    for g in range(GROUPS):
        for which in range(3):
            if g in (0, GROUPS - 1):
                pack(boxes, moved, rim, (3 if g else 0) + which, g, which)
            else:
                pack(boxes, moved, core, 3 * (g - 1) + which, g, which)


def interleave(v):
    lane = iota(v[0].shape, 1)
    half = lane < 2 * EDGE
    even = (lane // EDGE) % 2 == 0
    w = [pltpu.roll(a, 2 * EDGE, 1) for a in v]
    a0, a1 = jnp.where(half, v[0], w[2]), jnp.where(half, v[1], w[3])
    a2, a3 = jnp.where(half, w[0], v[2]), jnp.where(half, w[1], v[3])
    rows = []
    for a, b in ((a0, a1), (a2, a3)):
        rows.append(jnp.where(even, a, pltpu.roll(b, EDGE, 1)))
        rows.append(jnp.where(even, pltpu.roll(a, LANES - EDGE, 1), b))
    return rows


def relayout_edges(counts_ref, old_ref, edges, slabs, counts, boxes, sems):
    copies, moved = fetch(counts_ref, old_ref, counts, boxes, sems, 0)
    slots = [jnp.maximum(c - moved, 0) for c in range(COLUMN)]
    for f in range(FIELDS):
        copies[f].wait()
        for g in range(GROUPS):
            for r, row in enumerate(interleave([box_tiles(boxes, f, slot, g, "edge") for slot in slots])):
                edges[f, 4 * g + r] = row
        for side, g in enumerate((0, GROUPS - 1)):
            for r, row in enumerate(interleave([boxes[f, slot, :, lane_group(g)] for slot in slots])):
                slabs[f, side, r] = row


def relayout(counts_ref, old_ref, out, counts, boxes, sems):
    copies, moved = fetch(counts_ref, old_ref, counts, boxes, sems, 0)
    slots = [jnp.maximum(c - moved, 0) for c in range(COLUMN)]
    for f in range(FIELDS):
        copies[f].wait()
        for g in range(GROUPS):
            for r, row in enumerate(interleave([boxes[f, slot, :, lane_group(g)] for slot in slots])):
                out[f, 4 * g + r] = row


def unmix(kinds, f):
    if f == 0:
        a = b = kinds[0]
    else:
        a, b = kinds[2 * f - 1], kinds[2 * f]
    return [a, pltpu.roll(b, LANES - EDGE, 1), pltpu.roll(a, 2 * EDGE, 1), pltpu.roll(b, EDGE, 1)]


def wire_rows(shell, rim, core, k, g):
    low = iota((8, LANES), 0) < 4
    edge = shell[k, g]
    if g in (0, GROUPS - 1):
        mid = [rim[k, (3 if g else 0) + which] for which in range(3)]
    else:
        mid = [core[k, 3 * (g - 1) + which] for which in range(3)]
    return jnp.concatenate([jnp.where(low, edge, mid[0]), mid[1], mid[2], jnp.where(low, mid[0], edge)], axis=0)


def pack_x(pressure, right_side, coefficient):
    row = iota((8, LANES), 0)
    high = jnp.where(
        row >= 5, coefficient, jnp.where(row >= 2, pltpu.roll(pressure, 5, 0), pltpu.roll(right_side, 2, 0))
    )
    low = jnp.where(
        row < 3, coefficient, jnp.where(row < 6, pltpu.roll(pressure, 3, 0), pltpu.roll(right_side, 6, 0))
    )
    return high, low


def make_faces(counts_ref, shell, edges, x_up, x_down):
    limit = moved_boxes(counts_ref) * EDGE
    taken = iota((8, LANES), 1) < limit
    for g in range(GROUPS):
        kinds = [shell[k, g] for k in range(KINDS)]
        rows = [unmix(kinds, f) for f in range(FIELDS)]
        for r in range(4):
            y = 4 * g + r
            edge = [jnp.where(taken, rows[f][r], edges[f, y]) for f in range(FIELDS)]
            x_up[y], x_down[y] = pack_x(*edge)


def make_slabs(counts_ref, shell, rim, slabs, y_up, y_down):
    taken = iota((EDGE, LANES), 1) < moved_boxes(counts_ref) * EDGE
    for side, g in enumerate((0, GROUPS - 1)):
        out = y_up if side else y_down
        kinds = [wire_rows(shell, rim, None, k, g) for k in range(KINDS)]
        for f, at, depth in ((2, 0, 3), (0, 3, 3), (1, 6, 2)):
            rows = unmix(kinds, f)
            for j in range(depth):
                r = 4 - depth + j if side else j
                slab = jnp.where(taken, rows[r], slabs[f, side, r])
                out[EDGE * (at + j) : EDGE * (at + j + 1)] = 0.5 * slab if f == 2 else slab


def add_corners(before, after, y_up_in, y_down_in, y_up, y_down, sems):
    del y_up_in, y_down_in
    copies = []
    for way, (out, first) in enumerate(((y_up, EDGE - 2), (y_down, 0))):
        for d in range(2):
            for side, ref in enumerate((before, after)):
                at = 8 * EDGE + 8 * (2 * d + side)
                copies.append(pltpu.make_async_copy(ref.at[first + d], out.at[pl.ds(at, 8)], sems.at[way, d, side]))
    for copy in copies:
        copy.start()
    for copy in copies:
        copy.wait()


def is_red(shape, shift):
    return (iota(shape, 0) + iota(shape, 1) + shift) & 1 == 0


def assemble(counts_ref, own, shell, rim, core, half, mix, rhs):
    limit = moved_boxes(counts_ref) * EDGE
    taken = iota((EDGE, LANES), 1) < limit
    reds = [is_red((EDGE, LANES), y) for y in range(2)]
    before = None
    for g in range(GROUPS):
        kinds = [wire_rows(shell, rim, core, k, g) for k in range(KINDS)]
        parts = [unmix(kinds, f) for f in range(FIELDS)]
        for r in range(4):
            y = 4 * g + r
            p, f, b = [jnp.where(taken, parts[i][r], own[i, y]) for i in range(FIELDS)]
            h = 0.5 * b
            half[y] = h
            rhs[y] = f
            if y:
                mix[y - 1] = jnp.where(reds[(y - 1) % 2], h * p, before)
            before = p
    mix[EDGE - 1] = before


def tile(row):
    return pl.ds(row, 8)


class Sweep:
    def __init__(self, shift, out_p, out_r, half, mix, rhs, mix2, mix3, new1, new2, inv, tot, rest):
        self.shift, self.out_p, self.out_r = shift, out_p, out_r
        self.half, self.mix, self.rhs, self.mix2, self.mix3 = half, mix, rhs, mix2, mix3
        self.new1, self.new2, self.inv, self.tot, self.rest = new1, new2, inv, tot, rest
        shape = (8, LANES)
        lane, self.row = iota(shape, 1), iota(shape, 0)
        self.first_lane, self.last_lane = lane == 0, lane == LANES - 1
        self.reds = [is_red(shape, y) for y in range(2)]
        self.nothing = jnp.zeros(shape, F32)
        grp = lax.axis_index("grp")
        low = self.row >= 2 * (grp == 0).astype(jnp.int32)
        high = self.row < 8 - 6 * (grp == lax.axis_size("grp") - 1).astype(jnp.int32)
        self.open_x = [low, None, None, None, high]

    def six(self, ref, y, top, count):
        j = y + self.shift
        sums = []
        for t in range(count):
            r = top + 8 * t
            v = ref[j, tile(r)]
            below = jnp.where(self.first_lane, 0.0, pltpu.roll(v, 1, 1))
            above = jnp.where(self.last_lane, 0.0, pltpu.roll(v, LANES - 1, 1))
            x = ref[j, tile(r - 1)] + ref[j, tile(r + 1)]
            sums.append(((below + above) + x) + (ref[j - 1, tile(r)] + ref[j + 1, tile(r)]))
        return sums

    def red(self, y, odd, carry, shut=None):
        flow_before, new_before = carry
        around = self.six(self.half, y, 6, 5)
        flow = self.six(self.mix, y, 6, 5)
        news = []
        j = y + self.shift
        for t in range(5):
            r = tile(6 + 8 * t)
            h = self.half[j, r]
            total = 6.0 * h + around[t]
            inverse = 1.0 / total
            if self.open_x[t] is not None:
                inverse = jnp.where(self.open_x[t], inverse, 0.0)
            if shut is not None:
                inverse = jnp.where(self.row >= 8 * shut, inverse, 0.0)
            new = (self.rhs[j, r] + (h * flow[t] + flow_before[t])) * inverse
            self.new1[j, r] = new
            self.inv[j, r] = inverse
            self.tot[j, r] = total
            self.mix2[j - 1, r] = jnp.where(self.reds[1 - odd], new_before[t], h * new)
            news.append(new)
        return flow, news

    def black(self, y, odd, carry):
        flow_before, new_before = carry
        flow = self.six(self.mix2, y, 7, 5)
        news = []
        j = y + self.shift
        for t in range(5):
            r = tile(7 + 8 * t)
            h = self.half[j, r]
            full = self.rhs[j, r] + (h * flow[t] + flow_before[t])
            new = full * self.inv[j, r]
            self.new2[j, r] = new
            self.rest[j, r] = full - self.tot[j, r] * new
            self.mix3[j - 1, r] = jnp.where(self.reds[1 - odd], new_before[t], h * new)
            news.append(new)
        return flow, news

    def finish(self, y, odd, flow_before):
        flow = self.six(self.mix3, y, 8, 4)
        j = y + self.shift
        for t in range(4):
            r = tile(8 + 8 * t)
            mine = self.new1[j, r]
            left = (self.rhs[j, r] + (self.half[j, r] * flow[t] + flow_before[t])) - self.tot[j, r] * mine
            rows = pl.ds(y + 8 * t * EDGE, 8, stride=EDGE)
            self.out_p[rows, :] = jnp.where(self.reds[odd], mine, self.new2[j, r])
            self.out_r[rows, :] = jnp.where(self.reds[odd], left, self.rest[j, r])
        return flow

    def strip(self, y, odd, values, last):
        rows = []
        j = y + self.shift
        for v, at, turn_p, turn_f, kept in zip(values, (0, ROWS - 8), (3, 5), (6, 2), last):
            h = 0.5 * v
            p = pltpu.roll(v, turn_p, 0)
            self.half[j, tile(at)] = h
            self.rhs[j, tile(at)] = pltpu.roll(v, turn_f, 0)
            self.mix[j, tile(at)] = jnp.where(self.reds[odd], kept, p)
            rows.append(h * p)
        return tuple(rows)


def fours(first, count, step, carry):
    def body(k, carry):
        for d in range(4):
            carry = step(first + 4 * k + d, (first + d) % 2, carry)
        return carry

    return lax.fori_loop(0, count // 4, body, carry)


INNER = pl.ds(8, EDGE)


def sweep_inner(half_in, mix_in, rhs_in, x_before, x_after, *refs):
    w = Sweep(4, *refs)
    w.mix[3, INNER] = half_in[0] * mix_in[0]

    def take_in(y, odd, carry):
        w.half[y + 4, INNER] = half_in[y]
        w.mix[y + 4, INNER] = mix_in[y]
        w.rhs[y + 4, INNER] = rhs_in[y]
        return carry

    fours(0, EDGE, take_in, 0)

    def strips(k, odd, carry):
        y = EDGE - 1 - k
        return w.strip(y, 1 - odd, (x_before[y], x_after[y]), carry)

    last = fours(0, EDGE, strips, (w.nothing, w.nothing))
    w.mix[3, tile(0)], w.mix[3, tile(ROWS - 8)] = last
    carry = w.red(1, 1, (w.six(w.mix, 0, 6, 5), [w.nothing] * 5))
    carry = fours(2, EDGE - 4, w.red, carry)
    carry = w.red(EDGE - 2, 0, carry)
    for t in range(5):
        w.mix2[EDGE + 2, tile(6 + 8 * t)] = carry[1][t]
    carry = fours(2, EDGE - 4, w.black, (w.six(w.mix2, 1, 7, 5), [w.nothing] * 5))
    for t in range(5):
        w.mix3[EDGE + 1, tile(7 + 8 * t)] = carry[1][t]
    flow = w.finish(3, 1, w.six(w.mix3, 2, 8, 4))
    flow = fours(4, EDGE - 8, w.finish, flow)
    w.finish(EDGE - 4, 0, flow)


KEPT = ("half", "mix", "rhs", "mix2", "mix3", "new1", "new2", "inv", "tot", "rest")
NEAR = (
    ((0, 3), (0, 2), (0, 3), (1, 3), (2, 4), (1, 3), (2, 3), (1, 2), (1, 3), (2, 3)),
    ((29, 32), (29, 32), (29, 32), (28, 30), (27, 29), (29, 31), (29, 30), (30, 31), (29, 31), (29, 30)),
)


def sweep_outer(y_before, y_after, x_before, x_after, part_p, part_r, *refs):
    n = len(KEPT)
    old, (out_p, out_r), new = refs[:n], refs[n : n + 2], refs[n + 2 :]
    out_p[...] = part_p[...]
    out_r[...] = part_r[...]
    dev = lax.axis_index("dev")
    red_rows = [is_red((EDGE, LANES), y) for y in range(2)]
    zero = jnp.zeros((EDGE, LANES), F32)
    sides = [Sweep(shift, out_p, out_r, *[ref.at[i] for ref in new]) for i, shift in enumerate((4, -26))]
    for side, (w, spans) in enumerate(zip(sides, NEAR)):
        for name, ref, (first, end) in zip(KEPT, old, spans):
            for y in range(first, end):
                getattr(w, name)[y + w.shift] = ref[y + 4]
        source = y_after if side else y_before
        pressures, flux = {}, {}
        for k, y in enumerate(range(EDGE, EDGE + 3) if side else range(-3, 0)):
            h, p = [source[EDGE * i : EDGE * (i + 1)] for i in (k, 3 + k)]
            w.half[y + w.shift, INNER] = h
            pressures[y] = p
            flux[y] = h * p
            k = k if side else k - 1
            if 0 <= k < 2:
                w.rhs[y + w.shift, INNER] = source[EDGE * (6 + k) : EDGE * (7 + k)]
        edge = (EDGE - 1 if side else 0) + w.shift
        if side:
            pressures[EDGE - 1] = w.mix[edge, INNER]
        else:
            flux[0] = w.half[edge, INNER] * w.mix[edge, INNER]
        for y in range(EDGE - 1, EDGE + 3) if side else range(-4, 0):
            w.mix[y + w.shift, INNER] = jnp.where(red_rows[y % 2], flux.get(y + 1, zero), pressures.get(y, zero))

    def corners(ref, d):
        return [ref[pl.ds(8 * EDGE + 8 * (2 * d + side), 8)] for side in range(2)]

    low, high = sides
    last = (low.nothing, low.nothing)
    for d in (1, 0):
        last = high.strip(EDGE + d, d, corners(y_after, d), last)
    high.strip(EDGE - 1, 1, (x_before[EDGE - 1], x_after[EDGE - 1]), last)
    v = (x_before[0], x_after[0])
    last = tuple(0.5 * a * pltpu.roll(a, turn, 0) for a, turn in zip(v, (3, 5)))
    for d in (1, 0):
        last = low.strip(d - 2, d, corners(y_before, d), last)
    low.mix[1, tile(0)], low.mix[1, tile(ROWS - 8)] = last

    low_shut = (dev == 0).astype(jnp.int32)
    high_shut = (dev == lax.axis_size("dev") - 1).astype(jnp.int32)
    carry = (low.six(low.mix, -3, 6, 5), [low.nothing] * 5)
    carry = low.red(-2, 0, carry, low_shut)
    carry = low.red(-1, 1, carry, low_shut)
    carry = low.red(0, 0, carry)
    for t in range(5):
        r = tile(6 + 8 * t)
        low.mix2[4, r] = jnp.where(low.reds[0], carry[1][t], low.half[5, r] * low.new1[5, r])
    top = EDGE - 2
    carry = (high.six(high.mix, top, 6, 5), [high.new1[top + high.shift, tile(6 + 8 * t)] for t in range(5)])
    carry = high.red(top + 1, 1, carry)
    carry = high.red(top + 2, 0, carry, high_shut)
    carry = high.red(top + 3, 1, carry, high_shut)
    for t in range(5):
        high.mix2[top + 3 + high.shift, tile(6 + 8 * t)] = carry[1][t]

    carry = (low.six(low.mix2, -2, 7, 5), [low.nothing] * 5)
    for y in (-1, 0, 1):
        carry = low.black(y, y % 2, carry)
    for t in range(5):
        r = tile(7 + 8 * t)
        low.mix3[5, r] = jnp.where(low.reds[1], carry[1][t], low.half[6, r] * low.new2[6, r])
    top = EDGE - 3
    carry = (high.six(high.mix2, top, 7, 5), [high.new2[top + high.shift, tile(7 + 8 * t)] for t in range(5)])
    for y in range(top + 1, top + 4):
        carry = high.black(y, y % 2, carry)
    for t in range(5):
        high.mix3[top + 3 + high.shift, tile(7 + 8 * t)] = carry[1][t]

    flow = low.six(low.mix3, -1, 8, 4)
    for y in (0, 1, 2):
        flow = low.finish(y, y % 2, flow)
    flow = high.six(high.mix3, EDGE - 4, 8, 4)
    for y in range(EDGE - 3, EDGE):
        flow = high.finish(y, y % 2, flow)


def call(body, inputs, outputs, scratch, flops, moved, aliases=None, hbm=(), anywhere=False, limit=40 * 2**20):
    vmem, place, far = [pl.BlockSpec(memory_space=m) for m in (pltpu.VMEM, pl.ANY, pltpu.HBM)]
    kept = range(len(inputs)) if anywhere else ()
    return pl.pallas_call(
        body,
        out_shape=[jax.ShapeDtypeStruct(shape, F32) for shape in outputs],
        in_specs=[far if i in hbm else place if i in kept else vmem for i in range(len(inputs))],
        out_specs=[place if anywhere else vmem for _ in outputs],
        scratch_shapes=scratch,
        input_output_aliases=aliases or {},
        cost_estimate=pl.CostEstimate(flops=flops, bytes_accessed=moved, transcendentals=0),
        compiler_params=pltpu.CompilerParams(vmem_limit_bytes=limit),
    )(*inputs)


def per_device(old_fields, old_counts):
    groups, columns = lax.axis_size("grp"), lax.axis_size("dev")
    devices = groups * columns
    counts = jnp.pad(old_counts, (0, -devices % LANES)).reshape(-1, LANES)
    chain = [(i, i + 1) for i in range(devices - 1)]

    def ends(count):
        up = [(i, i + 1) for i in range(count - 1)]
        return up, [(j, i) for i, j in up]

    y_ways, x_ways = ends(columns), ends(groups)

    def read(body, outputs, after=None, limit=54400000):
        table = counts if after is None else lax.optimization_barrier((counts, after))[0]
        scratch = [
            VMEM(counts.shape, jnp.int32),
            VMEM((FIELDS, COLUMN, EDGE, EDGE * EDGE), F32),
            pltpu.SemaphoreType.DMA((FIELDS + 1,)),
        ]
        return call(body, (table, old_fields), outputs, scratch, 10**6, 2 * 10**6, hbm=(0, 1), limit=limit)

    strip, message = (EDGE, 8, LANES), (YMSG, LANES)
    deep, block = (DEEP, ROWS, LANES), (EDGE, EDGE, LANES)
    (shell,) = read(pack_shell, [(KINDS, GROUPS, 8, LANES)])
    rim, core = read(pack_rest, [(KINDS, RIM, 8, LANES), (KINDS, CORE, 8, LANES)], shell)
    shell = lax.ppermute(shell, ("grp", "dev"), chain)
    rim = lax.ppermute(rim, ("grp", "dev"), chain)
    core = lax.ppermute(core, ("grp", "dev"), chain)
    edges, slabs = read(relayout_edges, [(FIELDS, EDGE, 8, LANES), (FIELDS, 2, 4, EDGE, LANES)])
    x_up, x_down = call(make_faces, (counts, shell, edges), [strip, strip], [], 10**6, 10**6)
    x_before = lax.ppermute(x_up, "grp", x_ways[0])
    x_after = lax.ppermute(x_down, "grp", x_ways[1])
    table = lax.optimization_barrier((counts, x_up))[0]
    y_up, y_down = call(make_slabs, (table, shell, rim, slabs), [message, message], [], 10**6, 10**6)
    y_up, y_down = call(
        add_corners,
        (x_before, x_after, y_up, y_down),
        [message, message],
        [pltpu.SemaphoreType.DMA((2, 2, 2))],
        10**4,
        10**5,
        aliases={2: 0, 3: 1},
        anywhere=True,
    )
    y_before = lax.ppermute(y_up, "dev", y_ways[0])
    y_after = lax.ppermute(y_down, "dev", y_ways[1])
    (own,) = read(relayout, [(FIELDS, EDGE, EDGE, LANES)], y_up, 40 * 2**20)
    half, mix, rhs = call(assemble, (counts, own, shell, rim, core), [block] * 3, [], 10**6, 10**6)
    flat = (EDGE * EDGE, LANES)
    part_p, part_r, *kept = call(
        sweep_inner,
        (half, mix, rhs, x_before, x_after),
        [flat, flat] + [deep] * len(KEPT),
        [],
        10**8,
        5 * 10**6,
    )
    outs = call(
        sweep_outer,
        (y_before, y_after, x_before, x_after, part_p, part_r, *kept),
        [flat, flat],
        [VMEM((2, 10, ROWS, LANES), F32)] * len(KEPT),
        10**7,
        10**6,
    )
    return tuple(out.reshape(EDGE, EDGE, LANES) for out in outs)


def solution(mesh):
    placed = (P(None, ("grp", "dev"), None, None), P())
    return jax.shard_map(
        per_device,
        mesh=mesh,
        in_specs=placed,
        out_specs=(P("grp", "dev", None), P("grp", "dev", None)),
        check_vma=False,
    )
```

```python
import jax
import jax.numpy as jnp
from jax import lax
from jax.experimental import pallas as pl
from jax.experimental.pallas import tpu as pltpu
from jax.sharding import PartitionSpec as P


EDGE = 32
LANES = 128
GROUPS = EDGE * EDGE // LANES
COLUMN = 4
FIELDS = 3
MOVED = 2
KINDS = 5
SHELL = GROUPS + 6
CORE = 3 * (GROUPS - 2)
ROWS = EDGE + 16
DEEP = EDGE + 8
CORNERS = 6 * EDGE
YMSG = CORNERS + 32
F32 = jnp.float32
VMEM = pltpu.VMEM


def iota(shape, dim):
    return lax.broadcasted_iota(jnp.int32, shape, dim)


def moved_boxes(counts_ref):
    device = lax.axis_index("grp") * lax.axis_size("dev") + lax.axis_index("dev")
    counts = counts_ref[...]
    index = iota(counts.shape, 0) * LANES + iota(counts.shape, 1)
    start = jnp.sum(jnp.where(index < device, counts, 0))
    return jnp.clip(start - device * COLUMN, 0, MOVED)


def lane_group(g):
    return pl.ds(g * LANES, LANES)


def fetch(counts_ref, old_ref, counts, boxes, sems, first):
    copies = [pltpu.make_async_copy(counts_ref, counts, sems.at[FIELDS])]
    for f in range(FIELDS):
        copies.append(pltpu.make_async_copy(old_ref.at[f, pl.ds(first, COLUMN)], boxes.at[f], sems.at[f]))
    for copy in copies:
        copy.start()
    copies[0].wait()
    return copies[1:], moved_boxes(counts)


def box_tiles(boxes, f, c, g, which):
    low = iota((8, LANES), 0) < 4
    if which == "edge":
        return jnp.where(low, boxes[f, c, 0:8, lane_group(g)], boxes[f, c, 24:32, lane_group(g)])
    if which == 0:
        return jnp.where(low, boxes[f, c, 24:32, lane_group(g)], boxes[f, c, 0:8, lane_group(g)])
    return boxes[f, c, 8 * which : 8 * which + 8, lane_group(g)]


def pack(boxes, moved, out, at, g, which):
    shape = (8, LANES)
    lane = iota(shape, 1)
    block = lane // EDGE
    black = (iota(shape, 0) + block + lane) % 2 == 1
    even = block % 2 == 0
    first, second = [
        [box_tiles(boxes, f, MOVED + c - moved, g, which) for f in range(FIELDS)] for c in range(MOVED)
    ]
    turned = [pltpu.roll(v, EDGE, 1) for v in second]
    out[0, at] = jnp.where(black, first[0], turned[0])
    for f in (1, 2):
        out[2 * f - 1, at] = jnp.where(even, first[f], turned[f])
        out[2 * f, at] = jnp.where(even, turned[f], first[f])


def pack_shell(counts_ref, old_ref, out, counts, boxes, sems):
    copies, moved = fetch(counts_ref, old_ref, counts, boxes, sems, MOVED)
    for copy in copies:
        copy.wait()
    for g in range(GROUPS):
        pack(boxes, moved, out, g, g, "edge")
    for side, g in enumerate((0, GROUPS - 1)):
        for which in range(3):
            pack(boxes, moved, out, GROUPS + 3 * side + which, g, which)


def pack_core(counts_ref, old_ref, out, counts, boxes, sems):
    copies, moved = fetch(counts_ref, old_ref, counts, boxes, sems, MOVED)
    for copy in copies:
        copy.wait()
    for g in range(1, GROUPS - 1):
        for which in range(3):
            pack(boxes, moved, out, 3 * (g - 1) + which, g, which)


def interleave(v):
    lane = iota(v[0].shape, 1)
    half = lane < 2 * EDGE
    even = (lane // EDGE) % 2 == 0
    w = [pltpu.roll(a, 2 * EDGE, 1) for a in v]
    a0, a1 = jnp.where(half, v[0], w[2]), jnp.where(half, v[1], w[3])
    a2, a3 = jnp.where(half, w[0], v[2]), jnp.where(half, w[1], v[3])
    rows = []
    for a, b in ((a0, a1), (a2, a3)):
        rows.append(jnp.where(even, a, pltpu.roll(b, EDGE, 1)))
        rows.append(jnp.where(even, pltpu.roll(a, LANES - EDGE, 1), b))
    return rows


def relayout_edges(counts_ref, old_ref, edges, slabs, counts, boxes, sems):
    copies, moved = fetch(counts_ref, old_ref, counts, boxes, sems, 0)
    slots = [jnp.maximum(c - moved, 0) for c in range(COLUMN)]
    for f in range(FIELDS):
        copies[f].wait()
        for g in range(GROUPS):
            for r, row in enumerate(interleave([box_tiles(boxes, f, slot, g, "edge") for slot in slots])):
                edges[f, 4 * g + r] = row
        for side, g in enumerate((0, GROUPS - 1)):
            for r, row in enumerate(interleave([boxes[f, slot, :, lane_group(g)] for slot in slots])):
                slabs[f, side, r] = row


def relayout(counts_ref, old_ref, out, counts, boxes, sems):
    copies, moved = fetch(counts_ref, old_ref, counts, boxes, sems, 0)
    slots = [jnp.maximum(c - moved, 0) for c in range(COLUMN)]
    for f in range(FIELDS):
        copies[f].wait()
        for g in range(GROUPS):
            for r, row in enumerate(interleave([boxes[f, slot, :, lane_group(g)] for slot in slots])):
                out[f, 4 * g + r] = row


def unmix(kinds, f):
    if f == 0:
        a = b = kinds[0]
    else:
        a, b = kinds[2 * f - 1], kinds[2 * f]
    return [a, pltpu.roll(b, LANES - EDGE, 1), pltpu.roll(a, 2 * EDGE, 1), pltpu.roll(b, EDGE, 1)]


def wire_rows(shell, core, k, g):
    low = iota((8, LANES), 0) < 4
    edge = shell[k, g]
    if g in (0, GROUPS - 1):
        mid = [shell[k, GROUPS + (3 if g else 0) + which] for which in range(3)]
    else:
        mid = [core[k, 3 * (g - 1) + which] for which in range(3)]
    return jnp.concatenate([jnp.where(low, edge, mid[0]), mid[1], mid[2], jnp.where(low, mid[0], edge)], axis=0)


def pack_x(pressure, right_side, coefficient):
    row = iota((8, LANES), 0)
    high = jnp.where(
        row >= 5, coefficient, jnp.where(row >= 2, pltpu.roll(pressure, 5, 0), pltpu.roll(right_side, 2, 0))
    )
    low = jnp.where(
        row < 3, coefficient, jnp.where(row < 6, pltpu.roll(pressure, 3, 0), pltpu.roll(right_side, 6, 0))
    )
    return high, low


def is_odd(axis):
    return lax.axis_index(axis) % 2 == 1


def make_faces(counts_ref, shell, edges, first, second):
    limit = moved_boxes(counts_ref) * EDGE
    taken = iota((8, LANES), 1) < limit
    odd = is_odd("grp")
    for g in range(GROUPS):
        kinds = [shell[k, g] for k in range(KINDS)]
        rows = [unmix(kinds, f) for f in range(FIELDS)]
        for r in range(4):
            y = 4 * g + r
            edge = [jnp.where(taken, rows[f][r], edges[f, y]) for f in range(FIELDS)]
            up, down = pack_x(*edge)
            first[y] = jnp.where(odd, down, up)
            second[y] = jnp.where(odd, up, down)


def make_slabs(counts_ref, shell, slabs, first, second):
    taken = iota((EDGE, LANES), 1) < moved_boxes(counts_ref) * EDGE
    blacks = [~is_red((EDGE, LANES), y) for y in range(2)]
    sides = []
    for side, g in enumerate((0, GROUPS - 1)):
        kinds = [wire_rows(shell, None, k, g) for k in range(KINDS)]
        p, f, b = [[jnp.where(taken, row, slabs[i, side, r]) for r, row in enumerate(unmix(kinds, i))] for i in range(FIELDS)]
        near, next_, far = (3, 2, 1) if side else (0, 1, 2)
        sides.append(
            [
                0.5 * b[near],
                0.5 * b[next_],
                jnp.where(blacks[far % 2], 0.5 * b[far], pltpu.roll(p[far], 1, 1)),
                jnp.where(blacks[near % 2], p[near], p[next_]),
                f[near],
                f[next_],
            ]
        )
    odd = is_odd("dev")
    for i, (down, up) in enumerate(zip(*sides)):
        first[EDGE * i : EDGE * (i + 1)] = jnp.where(odd, down, up)
        second[EDGE * i : EDGE * (i + 1)] = jnp.where(odd, up, down)


def add_corners(x_first, x_second, first_in, second_in, first, second, sems):
    del first_in, second_in
    odd = lax.axis_index("dev") % 2
    copies = []
    for way, out in enumerate((first, second)):
        top = (EDGE - 2) * (odd if way else 1 - odd)
        for d in range(2):
            for side, ref in enumerate((x_first, x_second)):
                at = CORNERS + 8 * (2 * d + side)
                copies.append(pltpu.make_async_copy(ref.at[top + d], out.at[pl.ds(at, 8)], sems.at[way, d, side]))
    for copy in copies:
        copy.start()
    for copy in copies:
        copy.wait()


def is_red(shape, shift):
    return (iota(shape, 0) + iota(shape, 1) + shift) & 1 == 0


def assemble(counts_ref, own, shell, core, half, mix, rhs):
    limit = moved_boxes(counts_ref) * EDGE
    taken = iota((EDGE, LANES), 1) < limit
    reds = [is_red((EDGE, LANES), y) for y in range(2)]
    before = None
    for g in range(GROUPS):
        kinds = [wire_rows(shell, core, k, g) for k in range(KINDS)]
        parts = [unmix(kinds, f) for f in range(FIELDS)]
        for r in range(4):
            y = 4 * g + r
            p, f, b = [jnp.where(taken, parts[i][r], own[i, y]) for i in range(FIELDS)]
            h = 0.5 * b
            half[y] = h
            rhs[y] = f
            if y:
                mix[y - 1] = jnp.where(reds[(y - 1) % 2], h * p, before)
            before = p
    mix[EDGE - 1] = before


def tile(row):
    return pl.ds(row, 8)


class Sweep:
    def __init__(self, shift, out_p, out_r, half, mix, rhs, mix2, mix3, new1, new2, inv, tot, rest):
        self.shift, self.out_p, self.out_r = shift, out_p, out_r
        self.half, self.mix, self.rhs, self.mix2, self.mix3 = half, mix, rhs, mix2, mix3
        self.new1, self.new2, self.inv, self.tot, self.rest = new1, new2, inv, tot, rest
        shape = (8, LANES)
        lane, self.row = iota(shape, 1), iota(shape, 0)
        self.first_lane, self.last_lane = lane == 0, lane == LANES - 1
        self.reds = [is_red(shape, y) for y in range(2)]
        self.nothing = jnp.zeros(shape, F32)
        grp = lax.axis_index("grp")
        low = self.row >= 2 * (grp == 0).astype(jnp.int32)
        high = self.row < 8 - 6 * (grp == lax.axis_size("grp") - 1).astype(jnp.int32)
        self.open_x = [low, None, None, None, high]

    def six(self, ref, y, top, count):
        j = y + self.shift
        sums = []
        for t in range(count):
            r = top + 8 * t
            v = ref[j, tile(r)]
            below = jnp.where(self.first_lane, 0.0, pltpu.roll(v, 1, 1))
            above = jnp.where(self.last_lane, 0.0, pltpu.roll(v, LANES - 1, 1))
            x = ref[j, tile(r - 1)] + ref[j, tile(r + 1)]
            sums.append(((below + above) + x) + (ref[j - 1, tile(r)] + ref[j + 1, tile(r)]))
        return sums

    def red(self, y, odd, carry, shut=None):
        flow_before, new_before = carry
        around = self.six(self.half, y, 6, 5)
        flow = self.six(self.mix, y, 6, 5)
        news = []
        j = y + self.shift
        for t in range(5):
            r = tile(6 + 8 * t)
            h = self.half[j, r]
            total = 6.0 * h + around[t]
            inverse = 1.0 / total
            if self.open_x[t] is not None:
                inverse = jnp.where(self.open_x[t], inverse, 0.0)
            if shut is not None:
                inverse = jnp.where(self.row >= 8 * shut, inverse, 0.0)
            new = (self.rhs[j, r] + (h * flow[t] + flow_before[t])) * inverse
            self.new1[j, r] = new
            self.inv[j, r] = inverse
            self.tot[j, r] = total
            self.mix2[j - 1, r] = jnp.where(self.reds[1 - odd], new_before[t], h * new)
            news.append(new)
        return flow, news

    def black(self, y, odd, carry):
        flow_before, new_before = carry
        flow = self.six(self.mix2, y, 7, 5)
        news = []
        j = y + self.shift
        for t in range(5):
            r = tile(7 + 8 * t)
            h = self.half[j, r]
            full = self.rhs[j, r] + (h * flow[t] + flow_before[t])
            new = full * self.inv[j, r]
            self.new2[j, r] = new
            self.rest[j, r] = full - self.tot[j, r] * new
            self.mix3[j - 1, r] = jnp.where(self.reds[1 - odd], new_before[t], h * new)
            news.append(new)
        return flow, news

    def finish(self, y, odd, flow_before):
        flow = self.six(self.mix3, y, 8, 4)
        j = y + self.shift
        for t in range(4):
            r = tile(8 + 8 * t)
            mine = self.new1[j, r]
            left = (self.rhs[j, r] + (self.half[j, r] * flow[t] + flow_before[t])) - self.tot[j, r] * mine
            rows = pl.ds(y + 8 * t * EDGE, 8, stride=EDGE)
            self.out_p[rows, :] = jnp.where(self.reds[odd], mine, self.new2[j, r])
            self.out_r[rows, :] = jnp.where(self.reds[odd], left, self.rest[j, r])
        return flow

    def strip(self, y, odd, values, last):
        rows = []
        j = y + self.shift
        for v, at, turn_p, turn_f, kept in zip(values, (0, ROWS - 8), (3, 5), (6, 2), last):
            h = 0.5 * v
            p = pltpu.roll(v, turn_p, 0)
            self.half[j, tile(at)] = h
            self.rhs[j, tile(at)] = pltpu.roll(v, turn_f, 0)
            self.mix[j, tile(at)] = jnp.where(self.reds[odd], kept, p)
            rows.append(h * p)
        return tuple(rows)


def fours(first, count, step, carry):
    def body(k, carry):
        for d in range(4):
            carry = step(first + 4 * k + d, (first + d) % 2, carry)
        return carry

    return lax.fori_loop(0, count // 4, body, carry)


INNER = pl.ds(8, EDGE)


def order(axis, first, second):
    odd = is_odd(axis)
    return jnp.where(odd, first, second), jnp.where(odd, second, first)


def sweep_inner(half_in, mix_in, rhs_in, x_first, x_second, *refs):
    w = Sweep(4, *refs)
    w.mix[3, INNER] = half_in[0] * mix_in[0]

    def take_in(y, odd, carry):
        w.half[y + 4, INNER] = half_in[y]
        w.mix[y + 4, INNER] = mix_in[y]
        w.rhs[y + 4, INNER] = rhs_in[y]
        return carry

    fours(0, EDGE, take_in, 0)

    def strips(k, odd, carry):
        y = EDGE - 1 - k
        return w.strip(y, 1 - odd, order("grp", x_first[y], x_second[y]), carry)

    last = fours(0, EDGE, strips, (w.nothing, w.nothing))
    w.mix[3, tile(0)], w.mix[3, tile(ROWS - 8)] = last
    carry = w.red(1, 1, (w.six(w.mix, 0, 6, 5), [w.nothing] * 5))
    carry = fours(2, EDGE - 4, w.red, carry)
    carry = w.red(EDGE - 2, 0, carry)
    for t in range(5):
        w.mix2[EDGE + 2, tile(6 + 8 * t)] = carry[1][t]
    carry = fours(2, EDGE - 4, w.black, (w.six(w.mix2, 1, 7, 5), [w.nothing] * 5))
    for t in range(5):
        w.mix3[EDGE + 1, tile(7 + 8 * t)] = carry[1][t]
    flow = w.finish(3, 1, w.six(w.mix3, 2, 8, 4))
    flow = fours(4, EDGE - 8, w.finish, flow)
    w.finish(EDGE - 4, 0, flow)


KEPT = ("half", "mix", "rhs", "mix2", "mix3", "new1", "new2", "inv", "tot", "rest")
NEAR = (
    ((0, 3), (0, 2), (0, 3), (1, 3), (2, 4), (1, 3), (2, 3), (1, 2), (1, 3), (2, 3)),
    ((29, 32), (29, 32), (29, 32), (28, 30), (27, 29), (29, 31), (29, 30), (30, 31), (29, 31), (29, 30)),
)


def sweep_outer(y_first, y_second, x_first, x_second, part_p, part_r, *refs):
    n = len(KEPT)
    old, (out_p, out_r), new = refs[:n], refs[n : n + 2], refs[n + 2 :]
    out_p[...] = part_p[...]
    out_r[...] = part_r[...]
    dev = lax.axis_index("dev")
    red_rows = [is_red((EDGE, LANES), y) for y in range(2)]
    zero = jnp.zeros((EDGE, LANES), F32)

    def message(side, row, rows):
        return order("dev", y_first[row : row + rows], y_second[row : row + rows])[side]

    sides = [Sweep(shift, out_p, out_r, *[ref.at[i] for ref in new]) for i, shift in enumerate((4, -26))]
    for side, (w, spans) in enumerate(zip(sides, NEAR)):
        for name, ref, (first, end) in zip(KEPT, old, spans):
            for y in range(first, end):
                getattr(w, name)[y + w.shift] = ref[y + 4]
        h1, h2, far, mixed, f1, f2 = [message(side, EDGE * i, EDGE) for i in range(6)]
        place = (EDGE, EDGE + 1, EDGE + 2) if side else (-1, -2, -3)
        for y, h in zip(place, (h1, h2, far)):
            w.half[y + w.shift, INNER] = h
        for y, f in zip(place, (f1, f2)):
            w.rhs[y + w.shift, INNER] = f
        pressures = dict(zip(place, (mixed, mixed, pltpu.roll(far, LANES - 1, 1))))
        flux = {y: h * pressures[y] for y, h in zip(place, (h1, h2, far))}
        edge = (EDGE - 1 if side else 0) + w.shift
        if side:
            pressures[EDGE - 1] = w.mix[edge, INNER]
        else:
            flux[0] = w.half[edge, INNER] * w.mix[edge, INNER]
        for y in range(EDGE - 1, EDGE + 3) if side else range(-4, 0):
            w.mix[y + w.shift, INNER] = jnp.where(red_rows[y % 2], flux.get(y + 1, zero), pressures.get(y, zero))

    def corners(side, d):
        return order("grp", *[message(side, CORNERS + 8 * (2 * d + i), 8) for i in range(2)])

    low, high = sides
    last = (low.nothing, low.nothing)
    for d in (1, 0):
        last = high.strip(EDGE + d, d, corners(1, d), last)
    high.strip(EDGE - 1, 1, order("grp", x_first[EDGE - 1], x_second[EDGE - 1]), last)
    v = order("grp", x_first[0], x_second[0])
    last = tuple(0.5 * a * pltpu.roll(a, turn, 0) for a, turn in zip(v, (3, 5)))
    for d in (1, 0):
        last = low.strip(d - 2, d, corners(0, d), last)
    low.mix[1, tile(0)], low.mix[1, tile(ROWS - 8)] = last

    low_shut = (dev == 0).astype(jnp.int32)
    high_shut = (dev == lax.axis_size("dev") - 1).astype(jnp.int32)
    carry = (low.six(low.mix, -3, 6, 5), [low.nothing] * 5)
    carry = low.red(-2, 0, carry, low_shut)
    carry = low.red(-1, 1, carry, low_shut)
    carry = low.red(0, 0, carry)
    for t in range(5):
        r = tile(6 + 8 * t)
        low.mix2[4, r] = jnp.where(low.reds[0], carry[1][t], low.half[5, r] * low.new1[5, r])
    top = EDGE - 2
    carry = (high.six(high.mix, top, 6, 5), [high.new1[top + high.shift, tile(6 + 8 * t)] for t in range(5)])
    carry = high.red(top + 1, 1, carry)
    carry = high.red(top + 2, 0, carry, high_shut)
    carry = high.red(top + 3, 1, carry, high_shut)
    for t in range(5):
        high.mix2[top + 3 + high.shift, tile(6 + 8 * t)] = carry[1][t]

    carry = (low.six(low.mix2, -2, 7, 5), [low.nothing] * 5)
    for y in (-1, 0, 1):
        carry = low.black(y, y % 2, carry)
    for t in range(5):
        r = tile(7 + 8 * t)
        low.mix3[5, r] = jnp.where(low.reds[1], carry[1][t], low.half[6, r] * low.new2[6, r])
    top = EDGE - 3
    carry = (high.six(high.mix2, top, 7, 5), [high.new2[top + high.shift, tile(7 + 8 * t)] for t in range(5)])
    for y in range(top + 1, top + 4):
        carry = high.black(y, y % 2, carry)
    for t in range(5):
        high.mix3[top + 3 + high.shift, tile(7 + 8 * t)] = carry[1][t]

    flow = low.six(low.mix3, -1, 8, 4)
    for y in (0, 1, 2):
        flow = low.finish(y, y % 2, flow)
    flow = high.six(high.mix3, EDGE - 4, 8, 4)
    for y in range(EDGE - 3, EDGE):
        flow = high.finish(y, y % 2, flow)


def call(body, inputs, outputs, scratch, flops, moved, aliases=None, hbm=(), anywhere=False, limit=40 * 2**20):
    vmem, place, far = [pl.BlockSpec(memory_space=m) for m in (pltpu.VMEM, pl.ANY, pltpu.HBM)]
    kept = range(len(inputs)) if anywhere else ()
    return pl.pallas_call(
        body,
        out_shape=[jax.ShapeDtypeStruct(shape, F32) for shape in outputs],
        in_specs=[far if i in hbm else place if i in kept else vmem for i in range(len(inputs))],
        out_specs=[place if anywhere else vmem for _ in outputs],
        scratch_shapes=scratch,
        input_output_aliases=aliases or {},
        cost_estimate=pl.CostEstimate(flops=flops, bytes_accessed=moved, transcendentals=0),
        compiler_params=pltpu.CompilerParams(vmem_limit_bytes=limit),
    )(*inputs)


def per_device(old_fields, old_counts):
    groups, columns = lax.axis_size("grp"), lax.axis_size("dev")
    devices = groups * columns
    counts = jnp.pad(old_counts, (0, -devices % LANES)).reshape(-1, LANES)
    chain = [(i, i + 1) for i in range(devices - 1)]

    def swaps(count):
        ways = []
        for first in range(2):
            pairs = [(i, i + 1) for i in range(first, count - 1, 2)]
            ways.append(pairs + [(j, i) for i, j in pairs])
        return ways

    y_ways, x_ways = swaps(columns), swaps(groups)

    def read(body, outputs, after=None, limit=54400000):
        table = counts if after is None else lax.optimization_barrier((counts, after))[0]
        scratch = [
            VMEM(counts.shape, jnp.int32),
            VMEM((FIELDS, COLUMN, EDGE, EDGE * EDGE), F32),
            pltpu.SemaphoreType.DMA((FIELDS + 1,)),
        ]
        return call(body, (table, old_fields), outputs, scratch, 10**6, 2 * 10**6, hbm=(0, 1), limit=limit)

    strip, message = (EDGE, 8, LANES), (YMSG, LANES)
    deep, block = (DEEP, ROWS, LANES), (EDGE, EDGE, LANES)
    (shell,) = read(pack_shell, [(KINDS, SHELL, 8, LANES)])
    (core,) = read(pack_core, [(KINDS, CORE, 8, LANES)], shell)
    shell = lax.ppermute(shell, ("grp", "dev"), chain)
    core = lax.ppermute(core, ("grp", "dev"), chain)
    edges, slabs = read(relayout_edges, [(FIELDS, EDGE, 8, LANES), (FIELDS, 2, 4, EDGE, LANES)])
    x_first, x_second = call(make_faces, (counts, shell, edges), [strip, strip], [], 10**6, 10**6)
    table = lax.optimization_barrier((counts, x_first))[0]
    x_first = lax.ppermute(x_first, "grp", x_ways[0])
    x_second = lax.ppermute(x_second, "grp", x_ways[1])
    y_first, y_second = call(make_slabs, (table, shell, slabs), [message, message], [], 10**6, 10**6)
    y_first, y_second = call(
        add_corners,
        (x_first, x_second, y_first, y_second),
        [message, message],
        [pltpu.SemaphoreType.DMA((2, 2, 2))],
        10**4,
        10**5,
        aliases={2: 0, 3: 1},
        anywhere=True,
    )
    after = y_first
    y_first = lax.ppermute(y_first, "dev", y_ways[0])
    y_second = lax.ppermute(y_second, "dev", y_ways[1])
    (own,) = read(relayout, [(FIELDS, EDGE, EDGE, LANES)], after, 40 * 2**20)
    half, mix, rhs = call(assemble, (counts, own, shell, core), [block] * 3, [], 10**6, 10**6)
    flat = (EDGE * EDGE, LANES)
    part_p, part_r, *kept = call(
        sweep_inner,
        (half, mix, rhs, x_first, x_second),
        [flat, flat] + [deep] * len(KEPT),
        [],
        10**8,
        5 * 10**6,
    )
    outs = call(
        sweep_outer,
        (y_first, y_second, x_first, x_second, part_p, part_r, *kept),
        [flat, flat],
        [VMEM((2, 10, ROWS, LANES), F32)] * len(KEPT),
        10**7,
        10**6,
    )
    return tuple(out.reshape(EDGE, EDGE, LANES) for out in outs)


def solution(mesh):
    placed = (P(None, ("grp", "dev"), None, None), P())
    return jax.shard_map(
        per_device,
        mesh=mesh,
        in_specs=placed,
        out_specs=(P("grp", "dev", None), P("grp", "dev", None)),
        check_vma=False,
    )
```

```python
import jax
import jax.numpy as jnp
from jax import lax
from jax.experimental import pallas as pl
from jax.experimental.pallas import tpu as pltpu
from jax.sharding import PartitionSpec as P


EDGE = 32
LANES = 128
GROUPS = EDGE * EDGE // LANES
COLUMN = 4
FIELDS = 3
MOVED = 2
KINDS = 5
SHELL = GROUPS + 6
CORE = 3 * (GROUPS - 2)
ROWS = EDGE + 16
DEEP = EDGE + 8
CORNERS = 6 * EDGE
YMSG = CORNERS + 32
F32 = jnp.float32
INNER = pl.ds(8, EDGE)
VMEM = pltpu.VMEM


def iota(shape, dim):
    return lax.broadcasted_iota(jnp.int32, shape, dim)


def moved_boxes(counts_ref):
    device = lax.axis_index("grp") * lax.axis_size("dev") + lax.axis_index("dev")
    counts = counts_ref[...]
    index = iota(counts.shape, 0) * LANES + iota(counts.shape, 1)
    start = jnp.sum(jnp.where(index < device, counts, 0))
    return jnp.clip(start - device * COLUMN, 0, MOVED)


def lane_group(g):
    return pl.ds(g * LANES, LANES)


def fetch(counts_ref, old_ref, counts, boxes, sems, first):
    copies = [pltpu.make_async_copy(counts_ref, counts, sems.at[FIELDS])]
    for f in range(FIELDS):
        copies.append(pltpu.make_async_copy(old_ref.at[f, pl.ds(first, COLUMN)], boxes.at[f], sems.at[f]))
    for copy in copies:
        copy.start()
    copies[0].wait()
    return copies[1:], moved_boxes(counts)


def box_tiles(boxes, f, c, g, which):
    low = iota((8, LANES), 0) < 4
    if which == "edge":
        return jnp.where(low, boxes[f, c, 0:8, lane_group(g)], boxes[f, c, 24:32, lane_group(g)])
    if which == 0:
        return jnp.where(low, boxes[f, c, 24:32, lane_group(g)], boxes[f, c, 0:8, lane_group(g)])
    return boxes[f, c, 8 * which : 8 * which + 8, lane_group(g)]


def pack(boxes, moved, out, at, g, which):
    shape = (8, LANES)
    lane = iota(shape, 1)
    block = lane // EDGE
    black = (iota(shape, 0) + block + lane) % 2 == 1
    even = block % 2 == 0
    first, second = [
        [box_tiles(boxes, f, MOVED + c - moved, g, which) for f in range(FIELDS)] for c in range(MOVED)
    ]
    turned = [pltpu.roll(v, EDGE, 1) for v in second]
    out[0, at] = jnp.where(black, first[0], turned[0])
    for f in (1, 2):
        out[2 * f - 1, at] = jnp.where(even, first[f], turned[f])
        out[2 * f, at] = jnp.where(even, turned[f], first[f])


def pack_shell(counts_ref, old_ref, out, counts, boxes, sems):
    copies, moved = fetch(counts_ref, old_ref, counts, boxes, sems, MOVED)
    for copy in copies:
        copy.wait()
    for g in range(GROUPS):
        pack(boxes, moved, out, g, g, "edge")
    for side, g in enumerate((0, GROUPS - 1)):
        for which in range(3):
            pack(boxes, moved, out, GROUPS + 3 * side + which, g, which)


def pack_core(counts_ref, old_ref, out, counts, boxes, sems):
    copies, moved = fetch(counts_ref, old_ref, counts, boxes, sems, MOVED)
    for copy in copies:
        copy.wait()
    for g in range(1, GROUPS - 1):
        for which in range(3):
            pack(boxes, moved, out, 3 * (g - 1) + which, g, which)


def interleave(v):
    lane = iota(v[0].shape, 1)
    half = lane < 2 * EDGE
    even = (lane // EDGE) % 2 == 0
    outer = (lane < EDGE) | (lane >= 3 * EDGE)
    pairs = []
    for a, b in ((v[0], v[1]), (v[2], v[3])):
        turned = pltpu.roll(jnp.where(even, b, a), EDGE, 1)
        pairs.append((jnp.where(even, a, turned), jnp.where(even, turned, b)))
    (a0, a1), (b0, b1) = pairs
    turned = pltpu.roll(jnp.where(half, b0, a0), 2 * EDGE, 1)
    crossed = pltpu.roll(jnp.where(half, b1, a1), 2 * EDGE, 1)
    kept = jnp.where(half, a1, b1)
    return [
        jnp.where(half, a0, turned),
        jnp.where(outer, crossed, kept),
        jnp.where(half, turned, b0),
        jnp.where(outer, kept, crossed),
    ]


def relayout(counts_ref, old_ref, out, edges, counts, boxes, sems):
    copies, moved = fetch(counts_ref, old_ref, counts, boxes, sems, 0)
    slots = [jnp.maximum(c - moved, 0) for c in range(COLUMN)]
    low = iota((8, LANES), 0) < 4
    for f in range(FIELDS):
        copies[f].wait()
        for g in range(GROUPS):
            for r, row in enumerate(interleave([boxes[f, slot, :, lane_group(g)] for slot in slots])):
                out[f, 4 * g + r] = row
                edges[f, 4 * g + r] = jnp.where(low, row[0:8], row[24:32])


def unmix(kinds, f):
    if f == 0:
        a = b = kinds[0]
    else:
        a, b = kinds[2 * f - 1], kinds[2 * f]
    return [a, pltpu.roll(b, LANES - EDGE, 1), pltpu.roll(a, 2 * EDGE, 1), pltpu.roll(b, EDGE, 1)]


def wire_rows(shell, core, k, g):
    low = iota((8, LANES), 0) < 4
    edge = shell[k, g]
    if g in (0, GROUPS - 1):
        mid = [shell[k, GROUPS + (3 if g else 0) + which] for which in range(3)]
    else:
        mid = [core[k, 3 * (g - 1) + which] for which in range(3)]
    return jnp.concatenate([jnp.where(low, edge, mid[0]), mid[1], mid[2], jnp.where(low, mid[0], edge)], axis=0)


def pack_x(pressure, right_side, coefficient):
    row = iota((8, LANES), 0)
    high = jnp.where(
        row >= 5, coefficient, jnp.where(row >= 2, pltpu.roll(pressure, 5, 0), pltpu.roll(right_side, 2, 0))
    )
    low = jnp.where(
        row < 3, coefficient, jnp.where(row < 6, pltpu.roll(pressure, 3, 0), pltpu.roll(right_side, 6, 0))
    )
    return high, low


def is_odd(axis):
    return lax.axis_index(axis) % 2 == 1


def make_faces(counts_ref, shell, edges, first, second):
    limit = moved_boxes(counts_ref) * EDGE
    taken = iota((8, LANES), 1) < limit
    odd = is_odd("grp")
    for g in range(GROUPS):
        kinds = [shell[k, g] for k in range(KINDS)]
        rows = [unmix(kinds, f) for f in range(FIELDS)]
        for r in range(4):
            y = 4 * g + r
            edge = [jnp.where(taken, rows[f][r], edges[f, y]) for f in range(FIELDS)]
            up, down = pack_x(*edge)
            first[y] = jnp.where(odd, down, up)
            second[y] = jnp.where(odd, up, down)


def make_slabs(counts_ref, shell, own, first, second):
    taken = iota((EDGE, LANES), 1) < moved_boxes(counts_ref) * EDGE
    blacks = [~is_red((EDGE, LANES), y) for y in range(2)]
    sides = []
    for side, g in enumerate((0, GROUPS - 1)):
        kinds = [wire_rows(shell, None, k, g) for k in range(KINDS)]
        p, f, b = [[jnp.where(taken, row, own[i, 4 * g + r]) for r, row in enumerate(unmix(kinds, i))] for i in range(FIELDS)]
        near, next_, far = (3, 2, 1) if side else (0, 1, 2)
        sides.append(
            [
                0.5 * b[near],
                0.5 * b[next_],
                jnp.where(blacks[far % 2], 0.5 * b[far], pltpu.roll(p[far], 1, 1)),
                jnp.where(blacks[near % 2], p[near], p[next_]),
                f[near],
                f[next_],
            ]
        )
    odd = is_odd("dev")
    for i, (down, up) in enumerate(zip(*sides)):
        first[EDGE * i : EDGE * (i + 1)] = jnp.where(odd, down, up)
        second[EDGE * i : EDGE * (i + 1)] = jnp.where(odd, up, down)


def add_corners(x_first, x_second, first_in, second_in, first, second, sems):
    del first_in, second_in
    odd = lax.axis_index("dev") % 2
    copies = []
    for way, out in enumerate((first, second)):
        top = (EDGE - 2) * (odd if way else 1 - odd)
        for d in range(2):
            for side, ref in enumerate((x_first, x_second)):
                at = CORNERS + 8 * (2 * d + side)
                copies.append(pltpu.make_async_copy(ref.at[top + d], out.at[pl.ds(at, 8)], sems.at[way, d, side]))
    for copy in copies:
        copy.start()
    for copy in copies:
        copy.wait()


def is_red(shape, shift):
    return (iota(shape, 0) + iota(shape, 1) + shift) & 1 == 0


def assemble(counts_ref, own, shell, core, half, mix, rhs):
    limit = moved_boxes(counts_ref) * EDGE
    taken = iota((EDGE, LANES), 1) < limit
    reds = [is_red((EDGE, LANES), y) for y in range(2)]
    before = jnp.zeros((EDGE, LANES), F32)
    for g in range(GROUPS):
        kinds = [wire_rows(shell, core, k, g) for k in range(KINDS)]
        parts = [unmix(kinds, f) for f in range(FIELDS)]
        for r in range(4):
            y = 4 * g + r
            p, f, b = [jnp.where(taken, parts[i][r], own[i, y]) for i in range(FIELDS)]
            h = 0.5 * b
            half[y + 4, INNER] = h
            rhs[y + 4, INNER] = f
            mix[y + 3, INNER] = jnp.where(reds[(y - 1) % 2], h * p, before)
            before = p
    mix[EDGE + 3, INNER] = before


def tile(row):
    return pl.ds(row, 8)


class Sweep:
    def __init__(self, shift, out_p, out_r, half, mix, rhs, mix2, mix3, new1, new2, inv, tot, rest):
        self.shift, self.out_p, self.out_r = shift, out_p, out_r
        self.half, self.mix, self.rhs, self.mix2, self.mix3 = half, mix, rhs, mix2, mix3
        self.new1, self.new2, self.inv, self.tot, self.rest = new1, new2, inv, tot, rest
        shape = (8, LANES)
        lane, self.row = iota(shape, 1), iota(shape, 0)
        self.first_lane, self.last_lane = lane == 0, lane == LANES - 1
        self.reds = [is_red(shape, y) for y in range(2)]
        self.nothing = jnp.zeros(shape, F32)
        grp = lax.axis_index("grp")
        low = self.row >= 2 * (grp == 0).astype(jnp.int32)
        high = self.row < 8 - 6 * (grp == lax.axis_size("grp") - 1).astype(jnp.int32)
        self.open_x = [low, None, None, None, high]

    def six(self, ref, y, top, count):
        j = y + self.shift
        sums = []
        for t in range(count):
            r = top + 8 * t
            v = ref[j, tile(r)]
            below = jnp.where(self.first_lane, 0.0, pltpu.roll(v, 1, 1))
            above = jnp.where(self.last_lane, 0.0, pltpu.roll(v, LANES - 1, 1))
            x = ref[j, tile(r - 1)] + ref[j, tile(r + 1)]
            sums.append(((below + above) + x) + (ref[j - 1, tile(r)] + ref[j + 1, tile(r)]))
        return sums

    def red(self, y, odd, carry, shut=None):
        flow_before, new_before = carry
        around = self.six(self.half, y, 6, 5)
        flow = self.six(self.mix, y, 6, 5)
        news = []
        j = y + self.shift
        for t in range(5):
            r = tile(6 + 8 * t)
            h = self.half[j, r]
            total = 6.0 * h + around[t]
            inverse = 1.0 / total
            if self.open_x[t] is not None:
                inverse = jnp.where(self.open_x[t], inverse, 0.0)
            if shut is not None:
                inverse = jnp.where(self.row >= 8 * shut, inverse, 0.0)
            new = (self.rhs[j, r] + (h * flow[t] + flow_before[t])) * inverse
            self.new1[j, r] = new
            self.inv[j, r] = inverse
            self.tot[j, r] = total
            self.mix2[j - 1, r] = jnp.where(self.reds[1 - odd], new_before[t], h * new)
            news.append(new)
        return flow, news

    def black(self, y, odd, carry):
        flow_before, new_before = carry
        flow = self.six(self.mix2, y, 7, 5)
        news = []
        j = y + self.shift
        for t in range(5):
            r = tile(7 + 8 * t)
            h = self.half[j, r]
            full = self.rhs[j, r] + (h * flow[t] + flow_before[t])
            new = full * self.inv[j, r]
            self.new2[j, r] = new
            self.rest[j, r] = full - self.tot[j, r] * new
            self.mix3[j - 1, r] = jnp.where(self.reds[1 - odd], new_before[t], h * new)
            news.append(new)
        return flow, news

    def finish(self, y, odd, flow_before):
        flow = self.six(self.mix3, y, 8, 4)
        j = y + self.shift
        for t in range(4):
            r = tile(8 + 8 * t)
            mine = self.new1[j, r]
            left = (self.rhs[j, r] + (self.half[j, r] * flow[t] + flow_before[t])) - self.tot[j, r] * mine
            rows = pl.ds(y + 8 * t * EDGE, 8, stride=EDGE)
            self.out_p[rows, :] = jnp.where(self.reds[odd], mine, self.new2[j, r])
            self.out_r[rows, :] = jnp.where(self.reds[odd], left, self.rest[j, r])
        return flow

    def strip(self, y, odd, values, last):
        rows = []
        j = y + self.shift
        for v, at, turn_p, turn_f, kept in zip(values, (0, ROWS - 8), (3, 5), (6, 2), last):
            h = 0.5 * v
            p = pltpu.roll(v, turn_p, 0)
            self.half[j, tile(at)] = h
            self.rhs[j, tile(at)] = pltpu.roll(v, turn_f, 0)
            self.mix[j, tile(at)] = jnp.where(self.reds[odd], kept, p)
            rows.append(h * p)
        return tuple(rows)


def fours(first, count, step, carry):
    def body(k, carry):
        for d in range(4):
            carry = step(first + 4 * k + d, (first + d) % 2, carry)
        return carry

    return lax.fori_loop(0, count // 4, body, carry)


def order(axis, first, second):
    odd = is_odd(axis)
    return jnp.where(odd, first, second), jnp.where(odd, second, first)


def sweep_inner(counts_ref, own, shell, core, x_first, x_second, *refs):
    w = Sweep(4, *refs)
    assemble(counts_ref, own, shell, core, w.half, w.mix, w.rhs)

    def strips(k, odd, carry):
        y = EDGE - 1 - k
        return w.strip(y, 1 - odd, order("grp", x_first[y], x_second[y]), carry)

    last = fours(0, EDGE, strips, (w.nothing, w.nothing))
    w.mix[3, tile(0)], w.mix[3, tile(ROWS - 8)] = last
    carry = w.red(1, 1, (w.six(w.mix, 0, 6, 5), [w.nothing] * 5))
    carry = fours(2, EDGE - 4, w.red, carry)
    carry = w.red(EDGE - 2, 0, carry)
    for t in range(5):
        w.mix2[EDGE + 2, tile(6 + 8 * t)] = carry[1][t]
    carry = fours(2, EDGE - 4, w.black, (w.six(w.mix2, 1, 7, 5), [w.nothing] * 5))
    for t in range(5):
        w.mix3[EDGE + 1, tile(7 + 8 * t)] = carry[1][t]
    flow = w.finish(3, 1, w.six(w.mix3, 2, 8, 4))
    flow = fours(4, EDGE - 8, w.finish, flow)
    w.finish(EDGE - 4, 0, flow)


KEPT = ("half", "mix", "rhs", "mix2", "mix3", "new1", "new2", "inv", "tot", "rest")
NEAR = (
    ((0, 3), (0, 2), (0, 3), (1, 3), (2, 4), (1, 3), (2, 3), (1, 2), (1, 3), (2, 3)),
    ((29, 32), (29, 32), (29, 32), (28, 30), (27, 29), (29, 31), (29, 30), (30, 31), (29, 31), (29, 30)),
)


def sweep_outer(y_first, y_second, x_first, x_second, part_p, part_r, *refs):
    n = len(KEPT)
    old, (out_p, out_r), new = refs[:n], refs[n : n + 2], refs[n + 2 :]
    out_p[...] = part_p[...]
    out_r[...] = part_r[...]
    dev = lax.axis_index("dev")
    red_rows = [is_red((EDGE, LANES), y) for y in range(2)]
    zero = jnp.zeros((EDGE, LANES), F32)

    def message(side, row, rows):
        return order("dev", y_first[row : row + rows], y_second[row : row + rows])[side]

    sides = [Sweep(shift, out_p, out_r, *[ref.at[i] for ref in new]) for i, shift in enumerate((4, -26))]
    for side, (w, spans) in enumerate(zip(sides, NEAR)):
        for name, ref, (first, end) in zip(KEPT, old, spans):
            for y in range(first, end):
                getattr(w, name)[y + w.shift] = ref[y + 4]
        h1, h2, far, mixed, f1, f2 = [message(side, EDGE * i, EDGE) for i in range(6)]
        place = (EDGE, EDGE + 1, EDGE + 2) if side else (-1, -2, -3)
        for y, h in zip(place, (h1, h2, far)):
            w.half[y + w.shift, INNER] = h
        for y, f in zip(place, (f1, f2)):
            w.rhs[y + w.shift, INNER] = f
        pressures = dict(zip(place, (mixed, mixed, pltpu.roll(far, LANES - 1, 1))))
        flux = {y: h * pressures[y] for y, h in zip(place, (h1, h2, far))}
        edge = (EDGE - 1 if side else 0) + w.shift
        if side:
            pressures[EDGE - 1] = w.mix[edge, INNER]
        else:
            flux[0] = w.half[edge, INNER] * w.mix[edge, INNER]
        for y in range(EDGE - 1, EDGE + 3) if side else range(-4, 0):
            w.mix[y + w.shift, INNER] = jnp.where(red_rows[y % 2], flux.get(y + 1, zero), pressures.get(y, zero))

    def corners(side, d):
        return order("grp", *[message(side, CORNERS + 8 * (2 * d + i), 8) for i in range(2)])

    low, high = sides
    last = (low.nothing, low.nothing)
    for d in (1, 0):
        last = high.strip(EDGE + d, d, corners(1, d), last)
    high.strip(EDGE - 1, 1, order("grp", x_first[EDGE - 1], x_second[EDGE - 1]), last)
    v = order("grp", x_first[0], x_second[0])
    last = tuple(0.5 * a * pltpu.roll(a, turn, 0) for a, turn in zip(v, (3, 5)))
    for d in (1, 0):
        last = low.strip(d - 2, d, corners(0, d), last)
    low.mix[1, tile(0)], low.mix[1, tile(ROWS - 8)] = last

    low_shut = (dev == 0).astype(jnp.int32)
    high_shut = (dev == lax.axis_size("dev") - 1).astype(jnp.int32)
    carry = (low.six(low.mix, -3, 6, 5), [low.nothing] * 5)
    carry = low.red(-2, 0, carry, low_shut)
    carry = low.red(-1, 1, carry, low_shut)
    carry = low.red(0, 0, carry)
    for t in range(5):
        r = tile(6 + 8 * t)
        low.mix2[4, r] = jnp.where(low.reds[0], carry[1][t], low.half[5, r] * low.new1[5, r])
    top = EDGE - 2
    carry = (high.six(high.mix, top, 6, 5), [high.new1[top + high.shift, tile(6 + 8 * t)] for t in range(5)])
    carry = high.red(top + 1, 1, carry)
    carry = high.red(top + 2, 0, carry, high_shut)
    carry = high.red(top + 3, 1, carry, high_shut)
    for t in range(5):
        high.mix2[top + 3 + high.shift, tile(6 + 8 * t)] = carry[1][t]

    carry = (low.six(low.mix2, -2, 7, 5), [low.nothing] * 5)
    for y in (-1, 0, 1):
        carry = low.black(y, y % 2, carry)
    for t in range(5):
        r = tile(7 + 8 * t)
        low.mix3[5, r] = jnp.where(low.reds[1], carry[1][t], low.half[6, r] * low.new2[6, r])
    top = EDGE - 3
    carry = (high.six(high.mix2, top, 7, 5), [high.new2[top + high.shift, tile(7 + 8 * t)] for t in range(5)])
    for y in range(top + 1, top + 4):
        carry = high.black(y, y % 2, carry)
    for t in range(5):
        high.mix3[top + 3 + high.shift, tile(7 + 8 * t)] = carry[1][t]

    flow = low.six(low.mix3, -1, 8, 4)
    for y in (0, 1, 2):
        flow = low.finish(y, y % 2, flow)
    flow = high.six(high.mix3, EDGE - 4, 8, 4)
    for y in range(EDGE - 3, EDGE):
        flow = high.finish(y, y % 2, flow)


def call(body, inputs, outputs, scratch, flops, moved, aliases=None, hbm=(), anywhere=False, limit=40 * 2**20):
    vmem, place, far = [pl.BlockSpec(memory_space=m) for m in (pltpu.VMEM, pl.ANY, pltpu.HBM)]
    kept = range(len(inputs)) if anywhere else ()
    return pl.pallas_call(
        body,
        out_shape=[jax.ShapeDtypeStruct(shape, F32) for shape in outputs],
        in_specs=[far if i in hbm else place if i in kept else vmem for i in range(len(inputs))],
        out_specs=[place if anywhere else vmem for _ in outputs],
        scratch_shapes=scratch,
        input_output_aliases=aliases or {},
        cost_estimate=pl.CostEstimate(flops=flops, bytes_accessed=moved, transcendentals=0),
        compiler_params=pltpu.CompilerParams(vmem_limit_bytes=limit),
    )(*inputs)


def per_device(old_fields, old_counts):
    groups, columns = lax.axis_size("grp"), lax.axis_size("dev")
    devices = groups * columns
    counts = jnp.pad(old_counts, (0, -devices % LANES)).reshape(-1, LANES)
    chain = [(i, i + 1) for i in range(devices - 1)]

    def swaps(count):
        ways = []
        for first in range(2):
            pairs = [(i, i + 1) for i in range(first, count - 1, 2)]
            ways.append(pairs + [(j, i) for i, j in pairs])
        return ways

    y_ways, x_ways = swaps(columns), swaps(groups)

    def read(body, outputs, after=None, limit=54400000):
        table = counts if after is None else lax.optimization_barrier((counts, after))[0]
        scratch = [
            VMEM(counts.shape, jnp.int32),
            VMEM((FIELDS, COLUMN, EDGE, EDGE * EDGE), F32),
            pltpu.SemaphoreType.DMA((FIELDS + 1,)),
        ]
        return call(body, (table, old_fields), outputs, scratch, 10**6, 2 * 10**6, hbm=(0, 1), limit=limit)

    strip, message = (EDGE, 8, LANES), (YMSG, LANES)
    deep = (DEEP, ROWS, LANES)
    (shell,) = read(pack_shell, [(KINDS, SHELL, 8, LANES)])
    (core,) = read(pack_core, [(KINDS, CORE, 8, LANES)], shell)
    shell = lax.ppermute(shell, ("grp", "dev"), chain)
    core = lax.ppermute(core, ("grp", "dev"), chain)
    own, edges = read(relayout, [(FIELDS, EDGE, EDGE, LANES), (FIELDS, EDGE, 8, LANES)])
    x_first, x_second = call(make_faces, (counts, shell, edges), [strip, strip], [], 10**6, 10**6)
    table = lax.optimization_barrier((counts, x_first))[0]
    x_first = lax.ppermute(x_first, "grp", x_ways[0])
    x_second = lax.ppermute(x_second, "grp", x_ways[1])
    y_first, y_second = call(make_slabs, (table, shell, own), [message, message], [], 10**6, 10**6)
    y_first, y_second = call(
        add_corners,
        (x_first, x_second, y_first, y_second),
        [message, message],
        [pltpu.SemaphoreType.DMA((2, 2, 2))],
        10**4,
        10**5,
        aliases={2: 0, 3: 1},
        anywhere=True,
    )
    y_first = lax.ppermute(y_first, "dev", y_ways[0])
    y_second = lax.ppermute(y_second, "dev", y_ways[1])
    flat = (EDGE * EDGE, LANES)
    part_p, part_r, *kept = call(
        sweep_inner,
        (counts, own, shell, core, x_first, x_second),
        [flat, flat] + [deep] * len(KEPT),
        [],
        10**8,
        5 * 10**6,
    )
    outs = call(
        sweep_outer,
        (y_first, y_second, x_first, x_second, part_p, part_r, *kept),
        [flat, flat],
        [VMEM((2, 10, ROWS, LANES), F32)] * len(KEPT),
        10**7,
        10**6,
    )
    return tuple(out.reshape(EDGE, EDGE, LANES) for out in outs)


def solution(mesh):
    placed = (P(None, ("grp", "dev"), None, None), P())
    return jax.shard_map(
        per_device,
        mesh=mesh,
        in_specs=placed,
        out_specs=(P("grp", "dev", None), P("grp", "dev", None)),
        check_vma=False,
    )
```

```python
import jax
import jax.numpy as jnp
from jax import lax
from jax.experimental import pallas as pl
from jax.experimental.pallas import tpu as pltpu
from jax.sharding import PartitionSpec as P


EDGE = 32
LANES = 128
GROUPS = EDGE * EDGE // LANES
COLUMN = 4
FIELDS = 3
MOVED = 2
KINDS = 5
RIM = 6
CORE = 3 * (GROUPS - 2)
ROWS = EDGE + 16
DEEP = EDGE + 8
CORNERS = 6 * EDGE
YMSG = CORNERS + 32
F32 = jnp.float32
INNER = pl.ds(8, EDGE)
VMEM = pltpu.VMEM


def iota(shape, dim):
    return lax.broadcasted_iota(jnp.int32, shape, dim)


def moved_boxes(counts_ref):
    device = lax.axis_index("grp") * lax.axis_size("dev") + lax.axis_index("dev")
    counts = counts_ref[...]
    index = iota(counts.shape, 0) * LANES + iota(counts.shape, 1)
    start = jnp.sum(jnp.where(index < device, counts, 0))
    return jnp.clip(start - device * COLUMN, 0, MOVED)


def lane_group(g):
    return pl.ds(g * LANES, LANES)


def fetch(counts_ref, old_ref, counts, boxes, sems, first):
    copies = [pltpu.make_async_copy(counts_ref, counts, sems.at[FIELDS])]
    for f in range(FIELDS):
        copies.append(pltpu.make_async_copy(old_ref.at[f, pl.ds(first, COLUMN)], boxes.at[f], sems.at[f]))
    for copy in copies:
        copy.start()
    copies[0].wait()
    return copies[1:], moved_boxes(counts)


def box_tiles(boxes, f, c, g, which):
    low = iota((8, LANES), 0) < 4
    if which == "edge":
        return jnp.where(low, boxes[f, c, 0:8, lane_group(g)], boxes[f, c, 24:32, lane_group(g)])
    if which == 0:
        return jnp.where(low, boxes[f, c, 24:32, lane_group(g)], boxes[f, c, 0:8, lane_group(g)])
    return boxes[f, c, 8 * which : 8 * which + 8, lane_group(g)]


def pack(boxes, moved, out, at, g, which):
    shape = (8, LANES)
    lane = iota(shape, 1)
    block = lane // EDGE
    black = (iota(shape, 0) + block + lane) % 2 == 1
    even = block % 2 == 0
    first, second = [
        [box_tiles(boxes, f, MOVED + c - moved, g, which) for f in range(FIELDS)] for c in range(MOVED)
    ]
    turned = [pltpu.roll(v, EDGE, 1) for v in second]
    out[0, at] = jnp.where(black, first[0], turned[0])
    for f in (1, 2):
        out[2 * f - 1, at] = jnp.where(even, first[f], turned[f])
        out[2 * f, at] = jnp.where(even, turned[f], first[f])


def pack_all(counts_ref, old_ref, shell, rim, core, counts, boxes, sems):
    copies, moved = fetch(counts_ref, old_ref, counts, boxes, sems, MOVED)
    for copy in copies:
        copy.wait()
    for g in range(GROUPS):
        pack(boxes, moved, shell, g, g, "edge")
    for g in range(GROUPS):
        for which in range(3):
            if g in (0, GROUPS - 1):
                pack(boxes, moved, rim, (3 if g else 0) + which, g, which)
            else:
                pack(boxes, moved, core, 3 * (g - 1) + which, g, which)


def interleave(v):
    lane = iota(v[0].shape, 1)
    half = lane < 2 * EDGE
    even = (lane // EDGE) % 2 == 0
    outer = (lane < EDGE) | (lane >= 3 * EDGE)
    pairs = []
    for a, b in ((v[0], v[1]), (v[2], v[3])):
        turned = pltpu.roll(jnp.where(even, b, a), EDGE, 1)
        pairs.append((jnp.where(even, a, turned), jnp.where(even, turned, b)))
    (a0, a1), (b0, b1) = pairs
    turned = pltpu.roll(jnp.where(half, b0, a0), 2 * EDGE, 1)
    crossed = pltpu.roll(jnp.where(half, b1, a1), 2 * EDGE, 1)
    kept = jnp.where(half, a1, b1)
    return [
        jnp.where(half, a0, turned),
        jnp.where(outer, crossed, kept),
        jnp.where(half, turned, b0),
        jnp.where(outer, kept, crossed),
    ]


def relayout_edges(counts_ref, old_ref, edges, slabs, counts, boxes, sems):
    copies, moved = fetch(counts_ref, old_ref, counts, boxes, sems, 0)
    slots = [jnp.maximum(c - moved, 0) for c in range(COLUMN)]
    for f in range(FIELDS):
        copies[f].wait()
        for g in range(GROUPS):
            for r, row in enumerate(interleave([box_tiles(boxes, f, slot, g, "edge") for slot in slots])):
                edges[f, 4 * g + r] = row
        for side, g in enumerate((0, GROUPS - 1)):
            for r, row in enumerate(interleave([boxes[f, slot, :, lane_group(g)] for slot in slots])):
                slabs[f, side, r] = row


def relayout(counts_ref, old_ref, out, counts, boxes, sems):
    copies, moved = fetch(counts_ref, old_ref, counts, boxes, sems, 0)
    slots = [jnp.maximum(c - moved, 0) for c in range(COLUMN)]
    for f in range(FIELDS):
        copies[f].wait()
        for g in range(GROUPS):
            for r, row in enumerate(interleave([boxes[f, slot, :, lane_group(g)] for slot in slots])):
                out[f, 4 * g + r] = row


def unmix(kinds, f):
    if f == 0:
        a = b = kinds[0]
    else:
        a, b = kinds[2 * f - 1], kinds[2 * f]
    return [a, pltpu.roll(b, LANES - EDGE, 1), pltpu.roll(a, 2 * EDGE, 1), pltpu.roll(b, EDGE, 1)]


def wire_rows(shell, rim, core, k, g):
    low = iota((8, LANES), 0) < 4
    edge = shell[k, g]
    if g in (0, GROUPS - 1):
        mid = [rim[k, (3 if g else 0) + which] for which in range(3)]
    else:
        mid = [core[k, 3 * (g - 1) + which] for which in range(3)]
    return jnp.concatenate([jnp.where(low, edge, mid[0]), mid[1], mid[2], jnp.where(low, mid[0], edge)], axis=0)


def pack_x(pressure, right_side, coefficient):
    row = iota((8, LANES), 0)
    high = jnp.where(
        row >= 5, coefficient, jnp.where(row >= 2, pltpu.roll(pressure, 5, 0), pltpu.roll(right_side, 2, 0))
    )
    low = jnp.where(
        row < 3, coefficient, jnp.where(row < 6, pltpu.roll(pressure, 3, 0), pltpu.roll(right_side, 6, 0))
    )
    return high, low


def is_odd(axis):
    return lax.axis_index(axis) % 2 == 1


def make_faces(counts_ref, shell, edges, first, second):
    limit = moved_boxes(counts_ref) * EDGE
    taken = iota((8, LANES), 1) < limit
    odd = is_odd("grp")
    for g in range(GROUPS):
        kinds = [shell[k, g] for k in range(KINDS)]
        rows = [unmix(kinds, f) for f in range(FIELDS)]
        for r in range(4):
            y = 4 * g + r
            edge = [jnp.where(taken, rows[f][r], edges[f, y]) for f in range(FIELDS)]
            up, down = pack_x(*edge)
            first[y] = jnp.where(odd, down, up)
            second[y] = jnp.where(odd, up, down)


def make_slabs(counts_ref, shell, rim, slabs, first, second):
    taken = iota((EDGE, LANES), 1) < moved_boxes(counts_ref) * EDGE
    blacks = [~is_red((EDGE, LANES), y) for y in range(2)]
    sides = []
    for side, g in enumerate((0, GROUPS - 1)):
        kinds = [wire_rows(shell, rim, None, k, g) for k in range(KINDS)]
        p, f, b = [[jnp.where(taken, row, slabs[i, side, r]) for r, row in enumerate(unmix(kinds, i))] for i in range(FIELDS)]
        near, next_, far = (3, 2, 1) if side else (0, 1, 2)
        sides.append(
            [
                0.5 * b[near],
                0.5 * b[next_],
                jnp.where(blacks[far % 2], 0.5 * b[far], pltpu.roll(p[far], 1, 1)),
                jnp.where(blacks[near % 2], p[near], p[next_]),
                f[near],
                f[next_],
            ]
        )
    odd = is_odd("dev")
    for i, (down, up) in enumerate(zip(*sides)):
        first[EDGE * i : EDGE * (i + 1)] = jnp.where(odd, down, up)
        second[EDGE * i : EDGE * (i + 1)] = jnp.where(odd, up, down)


def add_corners(x_first, x_second, first_in, second_in, first, second, sems):
    del first_in, second_in
    odd = lax.axis_index("dev") % 2
    copies = []
    for way, out in enumerate((first, second)):
        top = (EDGE - 2) * (odd if way else 1 - odd)
        for d in range(2):
            for side, ref in enumerate((x_first, x_second)):
                at = CORNERS + 8 * (2 * d + side)
                copies.append(pltpu.make_async_copy(ref.at[top + d], out.at[pl.ds(at, 8)], sems.at[way, d, side]))
    for copy in copies:
        copy.start()
    for copy in copies:
        copy.wait()


def is_red(shape, shift):
    return (iota(shape, 0) + iota(shape, 1) + shift) & 1 == 0


def assemble(counts_ref, own, shell, rim, core, half, mix, rhs):
    limit = moved_boxes(counts_ref) * EDGE
    taken = iota((EDGE, LANES), 1) < limit
    reds = [is_red((EDGE, LANES), y) for y in range(2)]
    before = jnp.zeros((EDGE, LANES), F32)
    for g in range(GROUPS):
        kinds = [wire_rows(shell, rim, core, k, g) for k in range(KINDS)]
        parts = [unmix(kinds, f) for f in range(FIELDS)]
        for r in range(4):
            y = 4 * g + r
            p, f, b = [jnp.where(taken, parts[i][r], own[i, y]) for i in range(FIELDS)]
            h = 0.5 * b
            half[y + 4, INNER] = h
            rhs[y + 4, INNER] = f
            mix[y + 3, INNER] = jnp.where(reds[(y - 1) % 2], h * p, before)
            before = p
    mix[EDGE + 3, INNER] = before


def tile(row):
    return pl.ds(row, 8)


class Sweep:
    def __init__(self, shift, out_p, out_r, half, mix, rhs, mix2, mix3, new1, new2, inv, tot, rest):
        self.shift, self.out_p, self.out_r = shift, out_p, out_r
        self.half, self.mix, self.rhs, self.mix2, self.mix3 = half, mix, rhs, mix2, mix3
        self.new1, self.new2, self.inv, self.tot, self.rest = new1, new2, inv, tot, rest
        shape = (8, LANES)
        lane, self.row = iota(shape, 1), iota(shape, 0)
        self.first_lane, self.last_lane = lane == 0, lane == LANES - 1
        self.reds = [is_red(shape, y) for y in range(2)]
        self.nothing = jnp.zeros(shape, F32)
        grp = lax.axis_index("grp")
        low = self.row >= 2 * (grp == 0).astype(jnp.int32)
        high = self.row < 8 - 6 * (grp == lax.axis_size("grp") - 1).astype(jnp.int32)
        self.open_x = [low, None, None, None, high]

    def six(self, ref, y, top, count):
        j = y + self.shift
        sums = []
        for t in range(count):
            r = top + 8 * t
            v = ref[j, tile(r)]
            below = jnp.where(self.first_lane, 0.0, pltpu.roll(v, 1, 1))
            above = jnp.where(self.last_lane, 0.0, pltpu.roll(v, LANES - 1, 1))
            x = ref[j, tile(r - 1)] + ref[j, tile(r + 1)]
            sums.append(((below + above) + x) + (ref[j - 1, tile(r)] + ref[j + 1, tile(r)]))
        return sums

    def red(self, y, odd, carry, shut=None):
        flow_before, new_before = carry
        around = self.six(self.half, y, 6, 5)
        flow = self.six(self.mix, y, 6, 5)
        news = []
        j = y + self.shift
        for t in range(5):
            r = tile(6 + 8 * t)
            h = self.half[j, r]
            total = 6.0 * h + around[t]
            inverse = 1.0 / total
            if self.open_x[t] is not None:
                inverse = jnp.where(self.open_x[t], inverse, 0.0)
            if shut is not None:
                inverse = jnp.where(self.row >= 8 * shut, inverse, 0.0)
            new = (self.rhs[j, r] + (h * flow[t] + flow_before[t])) * inverse
            self.new1[j, r] = new
            self.inv[j, r] = inverse
            self.tot[j, r] = total
            self.mix2[j - 1, r] = jnp.where(self.reds[1 - odd], new_before[t], h * new)
            news.append(new)
        return flow, news

    def black(self, y, odd, carry):
        flow_before, new_before = carry
        flow = self.six(self.mix2, y, 7, 5)
        news = []
        j = y + self.shift
        for t in range(5):
            r = tile(7 + 8 * t)
            h = self.half[j, r]
            full = self.rhs[j, r] + (h * flow[t] + flow_before[t])
            new = full * self.inv[j, r]
            self.new2[j, r] = new
            self.rest[j, r] = full - self.tot[j, r] * new
            self.mix3[j - 1, r] = jnp.where(self.reds[1 - odd], new_before[t], h * new)
            news.append(new)
        return flow, news

    def finish(self, y, odd, flow_before):
        flow = self.six(self.mix3, y, 8, 4)
        j = y + self.shift
        for t in range(4):
            r = tile(8 + 8 * t)
            mine = self.new1[j, r]
            left = (self.rhs[j, r] + (self.half[j, r] * flow[t] + flow_before[t])) - self.tot[j, r] * mine
            rows = pl.ds(y + 8 * t * EDGE, 8, stride=EDGE)
            self.out_p[rows, :] = jnp.where(self.reds[odd], mine, self.new2[j, r])
            self.out_r[rows, :] = jnp.where(self.reds[odd], left, self.rest[j, r])
        return flow

    def strip(self, y, odd, values, last):
        rows = []
        j = y + self.shift
        for v, at, turn_p, turn_f, kept in zip(values, (0, ROWS - 8), (3, 5), (6, 2), last):
            h = 0.5 * v
            p = pltpu.roll(v, turn_p, 0)
            self.half[j, tile(at)] = h
            self.rhs[j, tile(at)] = pltpu.roll(v, turn_f, 0)
            self.mix[j, tile(at)] = jnp.where(self.reds[odd], kept, p)
            rows.append(h * p)
        return tuple(rows)


def fours(first, count, step, carry):
    def body(k, carry):
        for d in range(4):
            carry = step(first + 4 * k + d, (first + d) % 2, carry)
        return carry

    return lax.fori_loop(0, count // 4, body, carry)


def order(axis, first, second):
    odd = is_odd(axis)
    return jnp.where(odd, first, second), jnp.where(odd, second, first)


def sweep_inner(counts_ref, own, shell, rim, core, x_first, x_second, *refs):
    w = Sweep(4, *refs)
    assemble(counts_ref, own, shell, rim, core, w.half, w.mix, w.rhs)

    def strips(k, odd, carry):
        y = EDGE - 1 - k
        return w.strip(y, 1 - odd, order("grp", x_first[y], x_second[y]), carry)

    last = fours(0, EDGE, strips, (w.nothing, w.nothing))
    w.mix[3, tile(0)], w.mix[3, tile(ROWS - 8)] = last
    carry = w.red(1, 1, (w.six(w.mix, 0, 6, 5), [w.nothing] * 5))
    carry = fours(2, EDGE - 4, w.red, carry)
    carry = w.red(EDGE - 2, 0, carry)
    for t in range(5):
        w.mix2[EDGE + 2, tile(6 + 8 * t)] = carry[1][t]
    carry = fours(2, EDGE - 4, w.black, (w.six(w.mix2, 1, 7, 5), [w.nothing] * 5))
    for t in range(5):
        w.mix3[EDGE + 1, tile(7 + 8 * t)] = carry[1][t]
    flow = w.finish(3, 1, w.six(w.mix3, 2, 8, 4))
    flow = fours(4, EDGE - 8, w.finish, flow)
    w.finish(EDGE - 4, 0, flow)


KEPT = ("half", "mix", "rhs", "mix2", "mix3", "new1", "new2", "inv", "tot", "rest")
NEAR = (
    ((0, 3), (0, 2), (0, 3), (1, 3), (2, 4), (1, 3), (2, 3), (1, 2), (1, 3), (2, 3)),
    ((29, 32), (29, 32), (29, 32), (28, 30), (27, 29), (29, 31), (29, 30), (30, 31), (29, 31), (29, 30)),
)


def sweep_outer(y_first, y_second, x_first, x_second, part_p, part_r, *refs):
    n = len(KEPT)
    old, (out_p, out_r), new = refs[:n], refs[n : n + 2], refs[n + 2 :]
    out_p[...] = part_p[...]
    out_r[...] = part_r[...]
    dev = lax.axis_index("dev")
    red_rows = [is_red((EDGE, LANES), y) for y in range(2)]
    zero = jnp.zeros((EDGE, LANES), F32)

    def message(side, row, rows):
        return order("dev", y_first[row : row + rows], y_second[row : row + rows])[side]

    sides = [Sweep(shift, out_p, out_r, *[ref.at[i] for ref in new]) for i, shift in enumerate((4, -26))]
    for side, (w, spans) in enumerate(zip(sides, NEAR)):
        for name, ref, (first, end) in zip(KEPT, old, spans):
            for y in range(first, end):
                getattr(w, name)[y + w.shift] = ref[y + 4]
        h1, h2, far, mixed, f1, f2 = [message(side, EDGE * i, EDGE) for i in range(6)]
        place = (EDGE, EDGE + 1, EDGE + 2) if side else (-1, -2, -3)
        for y, h in zip(place, (h1, h2, far)):
            w.half[y + w.shift, INNER] = h
        for y, f in zip(place, (f1, f2)):
            w.rhs[y + w.shift, INNER] = f
        pressures = dict(zip(place, (mixed, mixed, pltpu.roll(far, LANES - 1, 1))))
        flux = {y: h * pressures[y] for y, h in zip(place, (h1, h2, far))}
        edge = (EDGE - 1 if side else 0) + w.shift
        if side:
            pressures[EDGE - 1] = w.mix[edge, INNER]
        else:
            flux[0] = w.half[edge, INNER] * w.mix[edge, INNER]
        for y in range(EDGE - 1, EDGE + 3) if side else range(-4, 0):
            w.mix[y + w.shift, INNER] = jnp.where(red_rows[y % 2], flux.get(y + 1, zero), pressures.get(y, zero))

    def corners(side, d):
        return order("grp", *[message(side, CORNERS + 8 * (2 * d + i), 8) for i in range(2)])

    low, high = sides
    last = (low.nothing, low.nothing)
    for d in (1, 0):
        last = high.strip(EDGE + d, d, corners(1, d), last)
    high.strip(EDGE - 1, 1, order("grp", x_first[EDGE - 1], x_second[EDGE - 1]), last)
    v = order("grp", x_first[0], x_second[0])
    last = tuple(0.5 * a * pltpu.roll(a, turn, 0) for a, turn in zip(v, (3, 5)))
    for d in (1, 0):
        last = low.strip(d - 2, d, corners(0, d), last)
    low.mix[1, tile(0)], low.mix[1, tile(ROWS - 8)] = last

    low_shut = (dev == 0).astype(jnp.int32)
    high_shut = (dev == lax.axis_size("dev") - 1).astype(jnp.int32)
    carry = (low.six(low.mix, -3, 6, 5), [low.nothing] * 5)
    carry = low.red(-2, 0, carry, low_shut)
    carry = low.red(-1, 1, carry, low_shut)
    carry = low.red(0, 0, carry)
    for t in range(5):
        r = tile(6 + 8 * t)
        low.mix2[4, r] = jnp.where(low.reds[0], carry[1][t], low.half[5, r] * low.new1[5, r])
    top = EDGE - 2
    carry = (high.six(high.mix, top, 6, 5), [high.new1[top + high.shift, tile(6 + 8 * t)] for t in range(5)])
    carry = high.red(top + 1, 1, carry)
    carry = high.red(top + 2, 0, carry, high_shut)
    carry = high.red(top + 3, 1, carry, high_shut)
    for t in range(5):
        high.mix2[top + 3 + high.shift, tile(6 + 8 * t)] = carry[1][t]

    carry = (low.six(low.mix2, -2, 7, 5), [low.nothing] * 5)
    for y in (-1, 0, 1):
        carry = low.black(y, y % 2, carry)
    for t in range(5):
        r = tile(7 + 8 * t)
        low.mix3[5, r] = jnp.where(low.reds[1], carry[1][t], low.half[6, r] * low.new2[6, r])
    top = EDGE - 3
    carry = (high.six(high.mix2, top, 7, 5), [high.new2[top + high.shift, tile(7 + 8 * t)] for t in range(5)])
    for y in range(top + 1, top + 4):
        carry = high.black(y, y % 2, carry)
    for t in range(5):
        high.mix3[top + 3 + high.shift, tile(7 + 8 * t)] = carry[1][t]

    flow = low.six(low.mix3, -1, 8, 4)
    for y in (0, 1, 2):
        flow = low.finish(y, y % 2, flow)
    flow = high.six(high.mix3, EDGE - 4, 8, 4)
    for y in range(EDGE - 3, EDGE):
        flow = high.finish(y, y % 2, flow)


def call(body, inputs, outputs, scratch, flops, moved, aliases=None, hbm=(), anywhere=False, limit=40 * 2**20):
    vmem, place, far = [pl.BlockSpec(memory_space=m) for m in (pltpu.VMEM, pl.ANY, pltpu.HBM)]
    kept = range(len(inputs)) if anywhere else ()
    return pl.pallas_call(
        body,
        out_shape=[jax.ShapeDtypeStruct(shape, F32) for shape in outputs],
        in_specs=[far if i in hbm else place if i in kept else vmem for i in range(len(inputs))],
        out_specs=[place if anywhere else vmem for _ in outputs],
        scratch_shapes=scratch,
        input_output_aliases=aliases or {},
        cost_estimate=pl.CostEstimate(flops=flops, bytes_accessed=moved, transcendentals=0),
        compiler_params=pltpu.CompilerParams(vmem_limit_bytes=limit),
    )(*inputs)


def per_device(old_fields, old_counts):
    groups, columns = lax.axis_size("grp"), lax.axis_size("dev")
    devices = groups * columns
    counts = jnp.pad(old_counts, (0, -devices % LANES)).reshape(-1, LANES)
    chain = [(i, i + 1) for i in range(devices - 1)]

    def swaps(count):
        ways = []
        for first in range(2):
            pairs = [(i, i + 1) for i in range(first, count - 1, 2)]
            ways.append(pairs + [(j, i) for i, j in pairs])
        return ways

    y_ways, x_ways = swaps(columns), swaps(groups)

    def read(body, outputs, after=None, limit=54400000):
        table = counts if after is None else lax.optimization_barrier((counts, after))[0]
        scratch = [
            VMEM(counts.shape, jnp.int32),
            VMEM((FIELDS, COLUMN, EDGE, EDGE * EDGE), F32),
            pltpu.SemaphoreType.DMA((FIELDS + 1,)),
        ]
        return call(body, (table, old_fields), outputs, scratch, 10**6, 2 * 10**6, hbm=(0, 1), limit=limit)

    strip, message = (EDGE, 8, LANES), (YMSG, LANES)
    deep = (DEEP, ROWS, LANES)
    shell, rim, core = read(pack_all, [(KINDS, n, 8, LANES) for n in (GROUPS, RIM, CORE)])
    shell = lax.ppermute(shell, ("grp", "dev"), chain)
    rim = lax.ppermute(rim, ("grp", "dev"), chain)
    core = lax.ppermute(core, ("grp", "dev"), chain)
    edges, slabs = read(relayout_edges, [(FIELDS, EDGE, 8, LANES), (FIELDS, 2, 4, EDGE, LANES)])
    x_first, x_second = call(make_faces, (counts, shell, edges), [strip, strip], [], 10**6, 10**6)
    table = lax.optimization_barrier((counts, x_first))[0]
    x_first = lax.ppermute(x_first, "grp", x_ways[0])
    x_second = lax.ppermute(x_second, "grp", x_ways[1])
    y_first, y_second = call(make_slabs, (table, shell, rim, slabs), [message, message], [], 10**6, 10**6)
    y_first, y_second = call(
        add_corners,
        (x_first, x_second, y_first, y_second),
        [message, message],
        [pltpu.SemaphoreType.DMA((2, 2, 2))],
        10**4,
        10**5,
        aliases={2: 0, 3: 1},
        anywhere=True,
    )
    (own,) = read(relayout, [(FIELDS, EDGE, EDGE, LANES)], y_first)
    y_first = lax.ppermute(y_first, "dev", y_ways[0])
    y_second = lax.ppermute(y_second, "dev", y_ways[1])
    flat = (EDGE * EDGE, LANES)
    part_p, part_r, *kept = call(
        sweep_inner,
        (counts, own, shell, rim, core, x_first, x_second),
        [flat, flat] + [deep] * len(KEPT),
        [],
        10**8,
        5 * 10**6,
    )
    outs = call(
        sweep_outer,
        (y_first, y_second, x_first, x_second, part_p, part_r, *kept),
        [flat, flat],
        [VMEM((2, 10, ROWS, LANES), F32)] * len(KEPT),
        10**7,
        10**6,
    )
    return tuple(out.reshape(EDGE, EDGE, LANES) for out in outs)


def solution(mesh):
    placed = (P(None, ("grp", "dev"), None, None), P())
    return jax.shard_map(
        per_device,
        mesh=mesh,
        in_specs=placed,
        out_specs=(P("grp", "dev", None), P("grp", "dev", None)),
        check_vma=False,
    )
```

```python
import jax
import jax.numpy as jnp
from jax import lax
from jax.experimental import pallas as pl
from jax.experimental.pallas import tpu as pltpu
from jax.sharding import PartitionSpec as P


EDGE = 32
LANES = 128
GROUPS = EDGE * EDGE // LANES
COLUMN = 4
FIELDS = 3
MOVED = 2
KINDS = 5
RIM = 6
CORE = 3 * (GROUPS - 2)
ROWS = EDGE + 16
DEEP = EDGE + 8
CORNERS = 6 * EDGE
YMSG = CORNERS + 32
F32 = jnp.float32
INNER = pl.ds(8, EDGE)
VMEM = pltpu.VMEM


def iota(shape, dim):
    return lax.broadcasted_iota(jnp.int32, shape, dim)


def moved_boxes(counts_ref):
    device = lax.axis_index("grp") * lax.axis_size("dev") + lax.axis_index("dev")
    counts = counts_ref[...]
    index = iota(counts.shape, 0) * LANES + iota(counts.shape, 1)
    start = jnp.sum(jnp.where(index < device, counts, 0))
    return jnp.clip(start - device * COLUMN, 0, MOVED)


def lane_group(g):
    return pl.ds(g * LANES, LANES)


def fetch(counts_ref, old_ref, counts, boxes, sems, first):
    copies = [pltpu.make_async_copy(counts_ref, counts, sems.at[FIELDS])]
    for f in range(FIELDS):
        copies.append(pltpu.make_async_copy(old_ref.at[f, pl.ds(first, COLUMN)], boxes.at[f], sems.at[f]))
    for copy in copies:
        copy.start()
    copies[0].wait()
    return copies[1:], moved_boxes(counts)


def box_tiles(boxes, f, c, g, which):
    low = iota((8, LANES), 0) < 4
    if which == "edge":
        return jnp.where(low, boxes[f, c, 0:8, lane_group(g)], boxes[f, c, 24:32, lane_group(g)])
    if which == 0:
        return jnp.where(low, boxes[f, c, 24:32, lane_group(g)], boxes[f, c, 0:8, lane_group(g)])
    return boxes[f, c, 8 * which : 8 * which + 8, lane_group(g)]


def pack(boxes, moved, out, at, g, which):
    shape = (8, LANES)
    lane = iota(shape, 1)
    block = lane // EDGE
    black = (iota(shape, 0) + block + lane) % 2 == 1
    even = block % 2 == 0
    first, second = [
        [box_tiles(boxes, f, MOVED + c - moved, g, which) for f in range(FIELDS)] for c in range(MOVED)
    ]
    turned = [pltpu.roll(v, EDGE, 1) for v in second]
    out[0, at] = jnp.where(black, first[0], turned[0])
    for f in (1, 2):
        out[2 * f - 1, at] = jnp.where(even, first[f], turned[f])
        out[2 * f, at] = jnp.where(even, turned[f], first[f])


def pack_all(counts_ref, old_ref, shell, rim, core, counts, boxes, sems):
    copies, moved = fetch(counts_ref, old_ref, counts, boxes, sems, MOVED)
    for copy in copies:
        copy.wait()
    for g in range(GROUPS):
        pack(boxes, moved, shell, g, g, "edge")
    for g in range(GROUPS):
        for which in range(3):
            if g in (0, GROUPS - 1):
                pack(boxes, moved, rim, (3 if g else 0) + which, g, which)
            else:
                pack(boxes, moved, core, 3 * (g - 1) + which, g, which)


def interleave(v):
    lane = iota(v[0].shape, 1)
    half = lane < 2 * EDGE
    even = (lane // EDGE) % 2 == 0
    outer = (lane < EDGE) | (lane >= 3 * EDGE)
    pairs = []
    for a, b in ((v[0], v[1]), (v[2], v[3])):
        turned = pltpu.roll(jnp.where(even, b, a), EDGE, 1)
        pairs.append((jnp.where(even, a, turned), jnp.where(even, turned, b)))
    (a0, a1), (b0, b1) = pairs
    turned = pltpu.roll(jnp.where(half, b0, a0), 2 * EDGE, 1)
    crossed = pltpu.roll(jnp.where(half, b1, a1), 2 * EDGE, 1)
    kept = jnp.where(half, a1, b1)
    return [
        jnp.where(half, a0, turned),
        jnp.where(outer, crossed, kept),
        jnp.where(half, turned, b0),
        jnp.where(outer, kept, crossed),
    ]


def relayout(counts_ref, old_ref, out, edges, counts, boxes, sems):
    copies, moved = fetch(counts_ref, old_ref, counts, boxes, sems, 0)
    slots = [jnp.maximum(c - moved, 0) for c in range(COLUMN)]
    low = iota((8, LANES), 0) < 4
    for f in range(FIELDS):
        copies[f].wait()
        for g in range(GROUPS):
            for r, row in enumerate(interleave([boxes[f, slot, :, lane_group(g)] for slot in slots])):
                out[f, 4 * g + r] = row
                edges[f, 4 * g + r] = jnp.where(low, row[0:8], row[24:32])


def unmix(kinds, f):
    if f == 0:
        a = b = kinds[0]
    else:
        a, b = kinds[2 * f - 1], kinds[2 * f]
    return [a, pltpu.roll(b, LANES - EDGE, 1), pltpu.roll(a, 2 * EDGE, 1), pltpu.roll(b, EDGE, 1)]


def wire_rows(shell, rim, core, k, g):
    low = iota((8, LANES), 0) < 4
    edge = shell[k, g]
    if g in (0, GROUPS - 1):
        mid = [rim[k, (3 if g else 0) + which] for which in range(3)]
    else:
        mid = [core[k, 3 * (g - 1) + which] for which in range(3)]
    return jnp.concatenate([jnp.where(low, edge, mid[0]), mid[1], mid[2], jnp.where(low, mid[0], edge)], axis=0)


def pack_x(pressure, right_side, coefficient):
    row = iota((8, LANES), 0)
    high = jnp.where(
        row >= 5, coefficient, jnp.where(row >= 2, pltpu.roll(pressure, 5, 0), pltpu.roll(right_side, 2, 0))
    )
    low = jnp.where(
        row < 3, coefficient, jnp.where(row < 6, pltpu.roll(pressure, 3, 0), pltpu.roll(right_side, 6, 0))
    )
    return high, low


def is_odd(axis):
    return lax.axis_index(axis) % 2 == 1


def make_faces(counts_ref, shell, edges, first, second):
    limit = moved_boxes(counts_ref) * EDGE
    taken = iota((8, LANES), 1) < limit
    odd = is_odd("grp")
    for g in range(GROUPS):
        kinds = [shell[k, g] for k in range(KINDS)]
        rows = [unmix(kinds, f) for f in range(FIELDS)]
        for r in range(4):
            y = 4 * g + r
            edge = [jnp.where(taken, rows[f][r], edges[f, y]) for f in range(FIELDS)]
            up, down = pack_x(*edge)
            first[y] = jnp.where(odd, down, up)
            second[y] = jnp.where(odd, up, down)


def make_slabs(counts_ref, shell, rim, own, first, second):
    taken = iota((EDGE, LANES), 1) < moved_boxes(counts_ref) * EDGE
    blacks = [~is_red((EDGE, LANES), y) for y in range(2)]
    sides = []
    for side, g in enumerate((0, GROUPS - 1)):
        kinds = [wire_rows(shell, rim, None, k, g) for k in range(KINDS)]
        p, f, b = [[jnp.where(taken, row, own[i, 4 * g + r]) for r, row in enumerate(unmix(kinds, i))] for i in range(FIELDS)]
        near, next_, far = (3, 2, 1) if side else (0, 1, 2)
        sides.append(
            [
                0.5 * b[near],
                0.5 * b[next_],
                jnp.where(blacks[far % 2], 0.5 * b[far], pltpu.roll(p[far], 1, 1)),
                jnp.where(blacks[near % 2], p[near], p[next_]),
                f[near],
                f[next_],
            ]
        )
    odd = is_odd("dev")
    for i, (down, up) in enumerate(zip(*sides)):
        first[EDGE * i : EDGE * (i + 1)] = jnp.where(odd, down, up)
        second[EDGE * i : EDGE * (i + 1)] = jnp.where(odd, up, down)


def add_corners(x_first, x_second, first_in, second_in, first, second, sems):
    del first_in, second_in
    odd = lax.axis_index("dev") % 2
    copies = []
    for way, out in enumerate((first, second)):
        top = (EDGE - 2) * (odd if way else 1 - odd)
        for d in range(2):
            for side, ref in enumerate((x_first, x_second)):
                at = CORNERS + 8 * (2 * d + side)
                copies.append(pltpu.make_async_copy(ref.at[top + d], out.at[pl.ds(at, 8)], sems.at[way, d, side]))
    for copy in copies:
        copy.start()
    for copy in copies:
        copy.wait()


def is_red(shape, shift):
    return (iota(shape, 0) + iota(shape, 1) + shift) & 1 == 0


def assemble(counts_ref, own, shell, rim, core, half, mix, rhs):
    limit = moved_boxes(counts_ref) * EDGE
    taken = iota((EDGE, LANES), 1) < limit
    reds = [is_red((EDGE, LANES), y) for y in range(2)]
    before = jnp.zeros((EDGE, LANES), F32)
    for g in range(GROUPS):
        kinds = [wire_rows(shell, rim, core, k, g) for k in range(KINDS)]
        parts = [unmix(kinds, f) for f in range(FIELDS)]
        for r in range(4):
            y = 4 * g + r
            p, f, b = [jnp.where(taken, parts[i][r], own[i, y]) for i in range(FIELDS)]
            h = 0.5 * b
            half[y + 4, INNER] = h
            rhs[y + 4, INNER] = f
            mix[y + 3, INNER] = jnp.where(reds[(y - 1) % 2], h * p, before)
            before = p
    mix[EDGE + 3, INNER] = before


def tile(row):
    return pl.ds(row, 8)


class Sweep:
    def __init__(self, shift, out_p, out_r, half, mix, rhs, mix2, mix3, new1, new2, inv, tot, rest):
        self.shift, self.out_p, self.out_r = shift, out_p, out_r
        self.half, self.mix, self.rhs, self.mix2, self.mix3 = half, mix, rhs, mix2, mix3
        self.new1, self.new2, self.inv, self.tot, self.rest = new1, new2, inv, tot, rest
        shape = (8, LANES)
        lane, self.row = iota(shape, 1), iota(shape, 0)
        self.first_lane, self.last_lane = lane == 0, lane == LANES - 1
        self.reds = [is_red(shape, y) for y in range(2)]
        self.nothing = jnp.zeros(shape, F32)
        grp = lax.axis_index("grp")
        low = self.row >= 2 * (grp == 0).astype(jnp.int32)
        high = self.row < 8 - 6 * (grp == lax.axis_size("grp") - 1).astype(jnp.int32)
        self.open_x = [low, None, None, None, high]

    def six(self, ref, y, top, count):
        j = y + self.shift
        sums = []
        for t in range(count):
            r = top + 8 * t
            v = ref[j, tile(r)]
            below = jnp.where(self.first_lane, 0.0, pltpu.roll(v, 1, 1))
            above = jnp.where(self.last_lane, 0.0, pltpu.roll(v, LANES - 1, 1))
            x = ref[j, tile(r - 1)] + ref[j, tile(r + 1)]
            sums.append(((below + above) + x) + (ref[j - 1, tile(r)] + ref[j + 1, tile(r)]))
        return sums

    def red(self, y, odd, carry, shut=None):
        flow_before, new_before = carry
        around = self.six(self.half, y, 6, 5)
        flow = self.six(self.mix, y, 6, 5)
        news = []
        j = y + self.shift
        for t in range(5):
            r = tile(6 + 8 * t)
            h = self.half[j, r]
            total = 6.0 * h + around[t]
            inverse = 1.0 / total
            if self.open_x[t] is not None:
                inverse = jnp.where(self.open_x[t], inverse, 0.0)
            if shut is not None:
                inverse = jnp.where(self.row >= 8 * shut, inverse, 0.0)
            new = (self.rhs[j, r] + (h * flow[t] + flow_before[t])) * inverse
            self.new1[j, r] = new
            self.inv[j, r] = inverse
            self.tot[j, r] = total
            self.mix2[j - 1, r] = jnp.where(self.reds[1 - odd], new_before[t], h * new)
            news.append(new)
        return flow, news

    def black(self, y, odd, carry):
        flow_before, new_before = carry
        flow = self.six(self.mix2, y, 7, 5)
        news = []
        j = y + self.shift
        for t in range(5):
            r = tile(7 + 8 * t)
            h = self.half[j, r]
            full = self.rhs[j, r] + (h * flow[t] + flow_before[t])
            new = full * self.inv[j, r]
            self.new2[j, r] = new
            self.rest[j, r] = full - self.tot[j, r] * new
            self.mix3[j - 1, r] = jnp.where(self.reds[1 - odd], new_before[t], h * new)
            news.append(new)
        return flow, news

    def finish(self, y, odd, flow_before):
        flow = self.six(self.mix3, y, 8, 4)
        j = y + self.shift
        for t in range(4):
            r = tile(8 + 8 * t)
            mine = self.new1[j, r]
            left = (self.rhs[j, r] + (self.half[j, r] * flow[t] + flow_before[t])) - self.tot[j, r] * mine
            rows = pl.ds(y + 8 * t * EDGE, 8, stride=EDGE)
            self.out_p[rows, :] = jnp.where(self.reds[odd], mine, self.new2[j, r])
            self.out_r[rows, :] = jnp.where(self.reds[odd], left, self.rest[j, r])
        return flow

    def strip(self, y, odd, values, last):
        rows = []
        j = y + self.shift
        for v, at, turn_p, turn_f, kept in zip(values, (0, ROWS - 8), (3, 5), (6, 2), last):
            h = 0.5 * v
            p = pltpu.roll(v, turn_p, 0)
            self.half[j, tile(at)] = h
            self.rhs[j, tile(at)] = pltpu.roll(v, turn_f, 0)
            self.mix[j, tile(at)] = jnp.where(self.reds[odd], kept, p)
            rows.append(h * p)
        return tuple(rows)


def fours(first, count, step, carry):
    def body(k, carry):
        for d in range(4):
            carry = step(first + 4 * k + d, (first + d) % 2, carry)
        return carry

    return lax.fori_loop(0, count // 4, body, carry)


def order(axis, first, second):
    odd = is_odd(axis)
    return jnp.where(odd, first, second), jnp.where(odd, second, first)


def sweep_inner(counts_ref, own, shell, rim, core, x_first, x_second, *refs):
    w = Sweep(4, *refs)
    assemble(counts_ref, own, shell, rim, core, w.half, w.mix, w.rhs)

    def strips(k, odd, carry):
        y = EDGE - 1 - k
        return w.strip(y, 1 - odd, order("grp", x_first[y], x_second[y]), carry)

    last = fours(0, EDGE, strips, (w.nothing, w.nothing))
    w.mix[3, tile(0)], w.mix[3, tile(ROWS - 8)] = last
    carry = w.red(1, 1, (w.six(w.mix, 0, 6, 5), [w.nothing] * 5))
    carry = fours(2, EDGE - 4, w.red, carry)
    carry = w.red(EDGE - 2, 0, carry)
    for t in range(5):
        w.mix2[EDGE + 2, tile(6 + 8 * t)] = carry[1][t]
    carry = fours(2, EDGE - 4, w.black, (w.six(w.mix2, 1, 7, 5), [w.nothing] * 5))
    for t in range(5):
        w.mix3[EDGE + 1, tile(7 + 8 * t)] = carry[1][t]
    flow = w.finish(3, 1, w.six(w.mix3, 2, 8, 4))
    flow = fours(4, EDGE - 8, w.finish, flow)
    w.finish(EDGE - 4, 0, flow)


KEPT = ("half", "mix", "rhs", "mix2", "mix3", "new1", "new2", "inv", "tot", "rest")
NEAR = (
    ((0, 3), (0, 2), (0, 3), (1, 3), (2, 4), (1, 3), (2, 3), (1, 2), (1, 3), (2, 3)),
    ((29, 32), (29, 32), (29, 32), (28, 30), (27, 29), (29, 31), (29, 30), (30, 31), (29, 31), (29, 30)),
)


def sweep_outer(y_first, y_second, x_first, x_second, part_p, part_r, *refs):
    n = len(KEPT)
    old, (out_p, out_r), new = refs[:n], refs[n : n + 2], refs[n + 2 :]
    out_p[...] = part_p[...]
    out_r[...] = part_r[...]
    dev = lax.axis_index("dev")
    red_rows = [is_red((EDGE, LANES), y) for y in range(2)]
    zero = jnp.zeros((EDGE, LANES), F32)

    def message(side, row, rows):
        return order("dev", y_first[row : row + rows], y_second[row : row + rows])[side]

    sides = [Sweep(shift, out_p, out_r, *[ref.at[i] for ref in new]) for i, shift in enumerate((4, -26))]
    for side, (w, spans) in enumerate(zip(sides, NEAR)):
        for name, ref, (first, end) in zip(KEPT, old, spans):
            for y in range(first, end):
                getattr(w, name)[y + w.shift] = ref[y + 4]
        h1, h2, far, mixed, f1, f2 = [message(side, EDGE * i, EDGE) for i in range(6)]
        place = (EDGE, EDGE + 1, EDGE + 2) if side else (-1, -2, -3)
        for y, h in zip(place, (h1, h2, far)):
            w.half[y + w.shift, INNER] = h
        for y, f in zip(place, (f1, f2)):
            w.rhs[y + w.shift, INNER] = f
        pressures = dict(zip(place, (mixed, mixed, pltpu.roll(far, LANES - 1, 1))))
        flux = {y: h * pressures[y] for y, h in zip(place, (h1, h2, far))}
        edge = (EDGE - 1 if side else 0) + w.shift
        if side:
            pressures[EDGE - 1] = w.mix[edge, INNER]
        else:
            flux[0] = w.half[edge, INNER] * w.mix[edge, INNER]
        for y in range(EDGE - 1, EDGE + 3) if side else range(-4, 0):
            w.mix[y + w.shift, INNER] = jnp.where(red_rows[y % 2], flux.get(y + 1, zero), pressures.get(y, zero))

    def corners(side, d):
        return order("grp", *[message(side, CORNERS + 8 * (2 * d + i), 8) for i in range(2)])

    low, high = sides
    last = (low.nothing, low.nothing)
    for d in (1, 0):
        last = high.strip(EDGE + d, d, corners(1, d), last)
    high.strip(EDGE - 1, 1, order("grp", x_first[EDGE - 1], x_second[EDGE - 1]), last)
    v = order("grp", x_first[0], x_second[0])
    last = tuple(0.5 * a * pltpu.roll(a, turn, 0) for a, turn in zip(v, (3, 5)))
    for d in (1, 0):
        last = low.strip(d - 2, d, corners(0, d), last)
    low.mix[1, tile(0)], low.mix[1, tile(ROWS - 8)] = last

    low_shut = (dev == 0).astype(jnp.int32)
    high_shut = (dev == lax.axis_size("dev") - 1).astype(jnp.int32)
    carry = (low.six(low.mix, -3, 6, 5), [low.nothing] * 5)
    carry = low.red(-2, 0, carry, low_shut)
    carry = low.red(-1, 1, carry, low_shut)
    carry = low.red(0, 0, carry)
    for t in range(5):
        r = tile(6 + 8 * t)
        low.mix2[4, r] = jnp.where(low.reds[0], carry[1][t], low.half[5, r] * low.new1[5, r])
    top = EDGE - 2
    carry = (high.six(high.mix, top, 6, 5), [high.new1[top + high.shift, tile(6 + 8 * t)] for t in range(5)])
    carry = high.red(top + 1, 1, carry)
    carry = high.red(top + 2, 0, carry, high_shut)
    carry = high.red(top + 3, 1, carry, high_shut)
    for t in range(5):
        high.mix2[top + 3 + high.shift, tile(6 + 8 * t)] = carry[1][t]

    carry = (low.six(low.mix2, -2, 7, 5), [low.nothing] * 5)
    for y in (-1, 0, 1):
        carry = low.black(y, y % 2, carry)
    for t in range(5):
        r = tile(7 + 8 * t)
        low.mix3[5, r] = jnp.where(low.reds[1], carry[1][t], low.half[6, r] * low.new2[6, r])
    top = EDGE - 3
    carry = (high.six(high.mix2, top, 7, 5), [high.new2[top + high.shift, tile(7 + 8 * t)] for t in range(5)])
    for y in range(top + 1, top + 4):
        carry = high.black(y, y % 2, carry)
    for t in range(5):
        high.mix3[top + 3 + high.shift, tile(7 + 8 * t)] = carry[1][t]

    flow = low.six(low.mix3, -1, 8, 4)
    for y in (0, 1, 2):
        flow = low.finish(y, y % 2, flow)
    flow = high.six(high.mix3, EDGE - 4, 8, 4)
    for y in range(EDGE - 3, EDGE):
        flow = high.finish(y, y % 2, flow)


def call(body, inputs, outputs, scratch, flops, moved, aliases=None, hbm=(), anywhere=False, limit=40 * 2**20):
    vmem, place, far = [pl.BlockSpec(memory_space=m) for m in (pltpu.VMEM, pl.ANY, pltpu.HBM)]
    kept = range(len(inputs)) if anywhere else ()
    return pl.pallas_call(
        body,
        out_shape=[jax.ShapeDtypeStruct(shape, F32) for shape in outputs],
        in_specs=[far if i in hbm else place if i in kept else vmem for i in range(len(inputs))],
        out_specs=[place if anywhere else vmem for _ in outputs],
        scratch_shapes=scratch,
        input_output_aliases=aliases or {},
        cost_estimate=pl.CostEstimate(flops=flops, bytes_accessed=moved, transcendentals=0),
        compiler_params=pltpu.CompilerParams(vmem_limit_bytes=limit),
    )(*inputs)


def per_device(old_fields, old_counts):
    groups, columns = lax.axis_size("grp"), lax.axis_size("dev")
    devices = groups * columns
    counts = jnp.pad(old_counts, (0, -devices % LANES)).reshape(-1, LANES)
    chain = [(i, i + 1) for i in range(devices - 1)]

    def swaps(count):
        ways = []
        for first in range(2):
            pairs = [(i, i + 1) for i in range(first, count - 1, 2)]
            ways.append(pairs + [(j, i) for i, j in pairs])
        return ways

    y_ways, x_ways = swaps(columns), swaps(groups)

    def read(body, outputs, after=None, limit=54400000):
        table = counts if after is None else lax.optimization_barrier((counts, after))[0]
        scratch = [
            VMEM(counts.shape, jnp.int32),
            VMEM((FIELDS, COLUMN, EDGE, EDGE * EDGE), F32),
            pltpu.SemaphoreType.DMA((FIELDS + 1,)),
        ]
        return call(body, (table, old_fields), outputs, scratch, 10**6, 2 * 10**6, hbm=(0, 1), limit=limit)

    strip, message = (EDGE, 8, LANES), (YMSG, LANES)
    deep = (DEEP, ROWS, LANES)
    shell, rim, core = read(pack_all, [(KINDS, n, 8, LANES) for n in (GROUPS, RIM, CORE)])
    shell = lax.ppermute(shell, ("grp", "dev"), chain)
    rim = lax.ppermute(rim, ("grp", "dev"), chain)
    core = lax.ppermute(core, ("grp", "dev"), chain)
    own, edges = read(relayout, [(FIELDS, EDGE, EDGE, LANES), (FIELDS, EDGE, 8, LANES)])
    x_first, x_second = call(make_faces, (counts, shell, edges), [strip, strip], [], 10**6, 10**6)
    table = lax.optimization_barrier((counts, x_first))[0]
    x_first = lax.ppermute(x_first, "grp", x_ways[0])
    x_second = lax.ppermute(x_second, "grp", x_ways[1])
    y_first, y_second = call(make_slabs, (table, shell, rim, own), [message, message], [], 10**6, 10**6)
    y_first, y_second = call(
        add_corners,
        (x_first, x_second, y_first, y_second),
        [message, message],
        [pltpu.SemaphoreType.DMA((2, 2, 2))],
        10**4,
        10**5,
        aliases={2: 0, 3: 1},
        anywhere=True,
    )
    y_first = lax.ppermute(y_first, "dev", y_ways[0])
    y_second = lax.ppermute(y_second, "dev", y_ways[1])
    flat = (EDGE * EDGE, LANES)
    part_p, part_r, *kept = call(
        sweep_inner,
        (counts, own, shell, rim, core, x_first, x_second),
        [flat, flat] + [deep] * len(KEPT),
        [],
        10**8,
        5 * 10**6,
    )
    outs = call(
        sweep_outer,
        (y_first, y_second, x_first, x_second, part_p, part_r, *kept),
        [flat, flat],
        [VMEM((2, 10, ROWS, LANES), F32)] * len(KEPT),
        10**7,
        10**6,
    )
    return tuple(out.reshape(EDGE, EDGE, LANES) for out in outs)


def solution(mesh):
    placed = (P(None, ("grp", "dev"), None, None), P())
    return jax.shard_map(
        per_device,
        mesh=mesh,
        in_specs=placed,
        out_specs=(P("grp", "dev", None), P("grp", "dev", None)),
        check_vma=False,
    )
```

```python
import jax
import jax.numpy as jnp
from jax import lax
from jax.experimental import pallas as pl
from jax.experimental.pallas import tpu as pltpu
from jax.sharding import PartitionSpec as P


EDGE = 32
LANES = 128
GROUPS = EDGE * EDGE // LANES
COLUMN = 4
FIELDS = 3
MOVED = 2
KINDS = 5
CORE = 3 * GROUPS
ROWS = EDGE + 16
DEEP = EDGE + 8
CORNERS = 6 * EDGE
YMSG = CORNERS + 32
F32 = jnp.float32
INNER = pl.ds(8, EDGE)
VMEM = pltpu.VMEM


def iota(shape, dim):
    return lax.broadcasted_iota(jnp.int32, shape, dim)


def moved_boxes(counts_ref):
    device = lax.axis_index("grp") * lax.axis_size("dev") + lax.axis_index("dev")
    counts = counts_ref[...]
    index = iota(counts.shape, 0) * LANES + iota(counts.shape, 1)
    start = jnp.sum(jnp.where(index < device, counts, 0))
    return jnp.clip(start - device * COLUMN, 0, MOVED)


def lane_group(g):
    return pl.ds(g * LANES, LANES)


def fetch(counts_ref, old_ref, counts, boxes, sems, first):
    copies = [pltpu.make_async_copy(counts_ref, counts, sems.at[FIELDS])]
    for f in range(FIELDS):
        copies.append(pltpu.make_async_copy(old_ref.at[f, pl.ds(first, COLUMN)], boxes.at[f], sems.at[f]))
    for copy in copies:
        copy.start()
    copies[0].wait()
    return copies[1:], moved_boxes(counts)


def box_tiles(boxes, f, c, g, which):
    low = iota((8, LANES), 0) < 4
    if which == "edge":
        return jnp.where(low, boxes[f, c, 0:8, lane_group(g)], boxes[f, c, 24:32, lane_group(g)])
    if which == 0:
        return jnp.where(low, boxes[f, c, 24:32, lane_group(g)], boxes[f, c, 0:8, lane_group(g)])
    return boxes[f, c, 8 * which : 8 * which + 8, lane_group(g)]


def pack(boxes, moved, out, at, g, which):
    shape = (8, LANES)
    lane = iota(shape, 1)
    block = lane // EDGE
    black = (iota(shape, 0) + block + lane) % 2 == 1
    even = block % 2 == 0
    first, second = [
        [box_tiles(boxes, f, MOVED + c - moved, g, which) for f in range(FIELDS)] for c in range(MOVED)
    ]
    turned = [pltpu.roll(v, EDGE, 1) for v in second]
    out[0, at] = jnp.where(black, first[0], turned[0])
    for f in (1, 2):
        out[2 * f - 1, at] = jnp.where(even, first[f], turned[f])
        out[2 * f, at] = jnp.where(even, turned[f], first[f])


def pack_all(counts_ref, old_ref, shell, core, counts, boxes, sems):
    copies, moved = fetch(counts_ref, old_ref, counts, boxes, sems, MOVED)
    for copy in copies:
        copy.wait()
    for g in range(GROUPS):
        pack(boxes, moved, shell, g, g, "edge")
    for g in range(GROUPS):
        for which in range(3):
            pack(boxes, moved, core, 3 * g + which, g, which)


def interleave(v):
    lane = iota(v[0].shape, 1)
    half = lane < 2 * EDGE
    even = (lane // EDGE) % 2 == 0
    outer = (lane < EDGE) | (lane >= 3 * EDGE)
    pairs = []
    for a, b in ((v[0], v[1]), (v[2], v[3])):
        turned = pltpu.roll(jnp.where(even, b, a), EDGE, 1)
        pairs.append((jnp.where(even, a, turned), jnp.where(even, turned, b)))
    (a0, a1), (b0, b1) = pairs
    turned = pltpu.roll(jnp.where(half, b0, a0), 2 * EDGE, 1)
    crossed = pltpu.roll(jnp.where(half, b1, a1), 2 * EDGE, 1)
    kept = jnp.where(half, a1, b1)
    return [
        jnp.where(half, a0, turned),
        jnp.where(outer, crossed, kept),
        jnp.where(half, turned, b0),
        jnp.where(outer, kept, crossed),
    ]


def relayout(counts_ref, old_ref, out, edges, counts, boxes, sems):
    copies, moved = fetch(counts_ref, old_ref, counts, boxes, sems, 0)
    slots = [jnp.maximum(c - moved, 0) for c in range(COLUMN)]
    low = iota((8, LANES), 0) < 4
    for f in range(FIELDS):
        copies[f].wait()
        for g in range(GROUPS):
            for r, row in enumerate(interleave([boxes[f, slot, :, lane_group(g)] for slot in slots])):
                out[f, 4 * g + r] = row
                edges[f, 4 * g + r] = jnp.where(low, row[0:8], row[24:32])


def unmix(kinds, f):
    if f == 0:
        a = b = kinds[0]
    else:
        a, b = kinds[2 * f - 1], kinds[2 * f]
    return [a, pltpu.roll(b, LANES - EDGE, 1), pltpu.roll(a, 2 * EDGE, 1), pltpu.roll(b, EDGE, 1)]


def wire_rows(shell, core, k, g):
    low = iota((8, LANES), 0) < 4
    edge = shell[k, g]
    mid = [core[k, 3 * g + which] for which in range(3)]
    return jnp.concatenate([jnp.where(low, edge, mid[0]), mid[1], mid[2], jnp.where(low, mid[0], edge)], axis=0)


def pack_x(pressure, right_side, coefficient):
    row = iota((8, LANES), 0)
    high = jnp.where(
        row >= 5, coefficient, jnp.where(row >= 2, pltpu.roll(pressure, 5, 0), pltpu.roll(right_side, 2, 0))
    )
    low = jnp.where(
        row < 3, coefficient, jnp.where(row < 6, pltpu.roll(pressure, 3, 0), pltpu.roll(right_side, 6, 0))
    )
    return high, low


def is_odd(axis):
    return lax.axis_index(axis) % 2 == 1


def make_faces(counts_ref, shell, edges, first, second):
    limit = moved_boxes(counts_ref) * EDGE
    taken = iota((8, LANES), 1) < limit
    odd = is_odd("grp")
    for g in range(GROUPS):
        kinds = [shell[k, g] for k in range(KINDS)]
        rows = [unmix(kinds, f) for f in range(FIELDS)]
        for r in range(4):
            y = 4 * g + r
            edge = [jnp.where(taken, rows[f][r], edges[f, y]) for f in range(FIELDS)]
            up, down = pack_x(*edge)
            first[y] = jnp.where(odd, down, up)
            second[y] = jnp.where(odd, up, down)


def make_slabs(counts_ref, shell, core, own, first, second):
    taken = iota((EDGE, LANES), 1) < moved_boxes(counts_ref) * EDGE
    blacks = [~is_red((EDGE, LANES), y) for y in range(2)]
    sides = []
    for side, g in enumerate((0, GROUPS - 1)):
        kinds = [wire_rows(shell, core, k, g) for k in range(KINDS)]
        p, f, b = [[jnp.where(taken, row, own[i, 4 * g + r]) for r, row in enumerate(unmix(kinds, i))] for i in range(FIELDS)]
        near, next_, far = (3, 2, 1) if side else (0, 1, 2)
        sides.append(
            [
                0.5 * b[near],
                0.5 * b[next_],
                jnp.where(blacks[far % 2], 0.5 * b[far], pltpu.roll(p[far], 1, 1)),
                jnp.where(blacks[near % 2], p[near], p[next_]),
                f[near],
                f[next_],
            ]
        )
    odd = is_odd("dev")
    for i, (down, up) in enumerate(zip(*sides)):
        first[EDGE * i : EDGE * (i + 1)] = jnp.where(odd, down, up)
        second[EDGE * i : EDGE * (i + 1)] = jnp.where(odd, up, down)


def add_corners(x_first, x_second, first_in, second_in, first, second, sems):
    del first_in, second_in
    odd = lax.axis_index("dev") % 2
    copies = []
    for way, out in enumerate((first, second)):
        top = (EDGE - 2) * (odd if way else 1 - odd)
        for d in range(2):
            for side, ref in enumerate((x_first, x_second)):
                at = CORNERS + 8 * (2 * d + side)
                copies.append(pltpu.make_async_copy(ref.at[top + d], out.at[pl.ds(at, 8)], sems.at[way, d, side]))
    for copy in copies:
        copy.start()
    for copy in copies:
        copy.wait()


def is_red(shape, shift):
    return (iota(shape, 0) + iota(shape, 1) + shift) & 1 == 0


def assemble(counts_ref, own, shell, core, half, mix, rhs):
    limit = moved_boxes(counts_ref) * EDGE
    taken = iota((EDGE, LANES), 1) < limit
    reds = [is_red((EDGE, LANES), y) for y in range(2)]
    before = jnp.zeros((EDGE, LANES), F32)
    for g in range(GROUPS):
        kinds = [wire_rows(shell, core, k, g) for k in range(KINDS)]
        parts = [unmix(kinds, f) for f in range(FIELDS)]
        for r in range(4):
            y = 4 * g + r
            p, f, b = [jnp.where(taken, parts[i][r], own[i, y]) for i in range(FIELDS)]
            h = 0.5 * b
            half[y + 4, INNER] = h
            rhs[y + 4, INNER] = f
            mix[y + 3, INNER] = jnp.where(reds[(y - 1) % 2], h * p, before)
            before = p
    mix[EDGE + 3, INNER] = before


def tile(row):
    return pl.ds(row, 8)


class Sweep:
    def __init__(self, shift, out_p, out_r, half, mix, rhs, mix2, mix3, new1, new2, inv, tot, rest):
        self.shift, self.out_p, self.out_r = shift, out_p, out_r
        self.half, self.mix, self.rhs, self.mix2, self.mix3 = half, mix, rhs, mix2, mix3
        self.new1, self.new2, self.inv, self.tot, self.rest = new1, new2, inv, tot, rest
        shape = (8, LANES)
        lane, self.row = iota(shape, 1), iota(shape, 0)
        self.first_lane, self.last_lane = lane == 0, lane == LANES - 1
        self.reds = [is_red(shape, y) for y in range(2)]
        self.nothing = jnp.zeros(shape, F32)
        grp = lax.axis_index("grp")
        low = self.row >= 2 * (grp == 0).astype(jnp.int32)
        high = self.row < 8 - 6 * (grp == lax.axis_size("grp") - 1).astype(jnp.int32)
        self.open_x = [low, None, None, None, high]

    def six(self, ref, y, top, count):
        j = y + self.shift
        sums = []
        for t in range(count):
            r = top + 8 * t
            v = ref[j, tile(r)]
            below = jnp.where(self.first_lane, 0.0, pltpu.roll(v, 1, 1))
            above = jnp.where(self.last_lane, 0.0, pltpu.roll(v, LANES - 1, 1))
            x = ref[j, tile(r - 1)] + ref[j, tile(r + 1)]
            sums.append(((below + above) + x) + (ref[j - 1, tile(r)] + ref[j + 1, tile(r)]))
        return sums

    def red(self, y, odd, carry, shut=None):
        flow_before, new_before = carry
        around = self.six(self.half, y, 6, 5)
        flow = self.six(self.mix, y, 6, 5)
        news = []
        j = y + self.shift
        for t in range(5):
            r = tile(6 + 8 * t)
            h = self.half[j, r]
            total = 6.0 * h + around[t]
            inverse = 1.0 / total
            if self.open_x[t] is not None:
                inverse = jnp.where(self.open_x[t], inverse, 0.0)
            if shut is not None:
                inverse = jnp.where(self.row >= 8 * shut, inverse, 0.0)
            new = (self.rhs[j, r] + (h * flow[t] + flow_before[t])) * inverse
            self.new1[j, r] = new
            self.inv[j, r] = inverse
            self.tot[j, r] = total
            self.mix2[j - 1, r] = jnp.where(self.reds[1 - odd], new_before[t], h * new)
            news.append(new)
        return flow, news

    def black(self, y, odd, carry):
        flow_before, new_before = carry
        flow = self.six(self.mix2, y, 7, 5)
        news = []
        j = y + self.shift
        for t in range(5):
            r = tile(7 + 8 * t)
            h = self.half[j, r]
            full = self.rhs[j, r] + (h * flow[t] + flow_before[t])
            new = full * self.inv[j, r]
            self.new2[j, r] = new
            self.rest[j, r] = full - self.tot[j, r] * new
            self.mix3[j - 1, r] = jnp.where(self.reds[1 - odd], new_before[t], h * new)
            news.append(new)
        return flow, news

    def finish(self, y, odd, flow_before):
        flow = self.six(self.mix3, y, 8, 4)
        j = y + self.shift
        for t in range(4):
            r = tile(8 + 8 * t)
            mine = self.new1[j, r]
            left = (self.rhs[j, r] + (self.half[j, r] * flow[t] + flow_before[t])) - self.tot[j, r] * mine
            rows = pl.ds(y + 8 * t * EDGE, 8, stride=EDGE)
            self.out_p[rows, :] = jnp.where(self.reds[odd], mine, self.new2[j, r])
            self.out_r[rows, :] = jnp.where(self.reds[odd], left, self.rest[j, r])
        return flow

    def strip(self, y, odd, values, last):
        rows = []
        j = y + self.shift
        for v, at, turn_p, turn_f, kept in zip(values, (0, ROWS - 8), (3, 5), (6, 2), last):
            h = 0.5 * v
            p = pltpu.roll(v, turn_p, 0)
            self.half[j, tile(at)] = h
            self.rhs[j, tile(at)] = pltpu.roll(v, turn_f, 0)
            self.mix[j, tile(at)] = jnp.where(self.reds[odd], kept, p)
            rows.append(h * p)
        return tuple(rows)


def fours(first, count, step, carry):
    def body(k, carry):
        for d in range(4):
            carry = step(first + 4 * k + d, (first + d) % 2, carry)
        return carry

    return lax.fori_loop(0, count // 4, body, carry)


def order(axis, first, second):
    odd = is_odd(axis)
    return jnp.where(odd, first, second), jnp.where(odd, second, first)


def sweep_inner(counts_ref, own, shell, core, x_first, x_second, *refs):
    w = Sweep(4, *refs)
    assemble(counts_ref, own, shell, core, w.half, w.mix, w.rhs)

    def strips(k, odd, carry):
        y = EDGE - 1 - k
        return w.strip(y, 1 - odd, order("grp", x_first[y], x_second[y]), carry)

    last = fours(0, EDGE, strips, (w.nothing, w.nothing))
    w.mix[3, tile(0)], w.mix[3, tile(ROWS - 8)] = last
    carry = w.red(1, 1, (w.six(w.mix, 0, 6, 5), [w.nothing] * 5))
    carry = fours(2, EDGE - 4, w.red, carry)
    carry = w.red(EDGE - 2, 0, carry)
    for t in range(5):
        w.mix2[EDGE + 2, tile(6 + 8 * t)] = carry[1][t]
    carry = fours(2, EDGE - 4, w.black, (w.six(w.mix2, 1, 7, 5), [w.nothing] * 5))
    for t in range(5):
        w.mix3[EDGE + 1, tile(7 + 8 * t)] = carry[1][t]
    flow = w.finish(3, 1, w.six(w.mix3, 2, 8, 4))
    flow = fours(4, EDGE - 8, w.finish, flow)
    w.finish(EDGE - 4, 0, flow)


KEPT = ("half", "mix", "rhs", "mix2", "mix3", "new1", "new2", "inv", "tot", "rest")
NEAR = (
    ((0, 3), (0, 2), (0, 3), (1, 3), (2, 4), (1, 3), (2, 3), (1, 2), (1, 3), (2, 3)),
    ((29, 32), (29, 32), (29, 32), (28, 30), (27, 29), (29, 31), (29, 30), (30, 31), (29, 31), (29, 30)),
)


def sweep_outer(y_first, y_second, x_first, x_second, part_p, part_r, *refs):
    n = len(KEPT)
    old, (out_p, out_r), new = refs[:n], refs[n : n + 2], refs[n + 2 :]
    out_p[...] = part_p[...]
    out_r[...] = part_r[...]
    dev = lax.axis_index("dev")
    red_rows = [is_red((EDGE, LANES), y) for y in range(2)]
    zero = jnp.zeros((EDGE, LANES), F32)

    def message(side, row, rows):
        return order("dev", y_first[row : row + rows], y_second[row : row + rows])[side]

    sides = [Sweep(shift, out_p, out_r, *[ref.at[i] for ref in new]) for i, shift in enumerate((4, -26))]
    for side, (w, spans) in enumerate(zip(sides, NEAR)):
        for name, ref, (first, end) in zip(KEPT, old, spans):
            for y in range(first, end):
                getattr(w, name)[y + w.shift] = ref[y + 4]
        h1, h2, far, mixed, f1, f2 = [message(side, EDGE * i, EDGE) for i in range(6)]
        place = (EDGE, EDGE + 1, EDGE + 2) if side else (-1, -2, -3)
        for y, h in zip(place, (h1, h2, far)):
            w.half[y + w.shift, INNER] = h
        for y, f in zip(place, (f1, f2)):
            w.rhs[y + w.shift, INNER] = f
        pressures = dict(zip(place, (mixed, mixed, pltpu.roll(far, LANES - 1, 1))))
        flux = {y: h * pressures[y] for y, h in zip(place, (h1, h2, far))}
        edge = (EDGE - 1 if side else 0) + w.shift
        if side:
            pressures[EDGE - 1] = w.mix[edge, INNER]
        else:
            flux[0] = w.half[edge, INNER] * w.mix[edge, INNER]
        for y in range(EDGE - 1, EDGE + 3) if side else range(-4, 0):
            w.mix[y + w.shift, INNER] = jnp.where(red_rows[y % 2], flux.get(y + 1, zero), pressures.get(y, zero))

    def corners(side, d):
        return order("grp", *[message(side, CORNERS + 8 * (2 * d + i), 8) for i in range(2)])

    low, high = sides
    last = (low.nothing, low.nothing)
    for d in (1, 0):
        last = high.strip(EDGE + d, d, corners(1, d), last)
    high.strip(EDGE - 1, 1, order("grp", x_first[EDGE - 1], x_second[EDGE - 1]), last)
    v = order("grp", x_first[0], x_second[0])
    last = tuple(0.5 * a * pltpu.roll(a, turn, 0) for a, turn in zip(v, (3, 5)))
    for d in (1, 0):
        last = low.strip(d - 2, d, corners(0, d), last)
    low.mix[1, tile(0)], low.mix[1, tile(ROWS - 8)] = last

    low_shut = (dev == 0).astype(jnp.int32)
    high_shut = (dev == lax.axis_size("dev") - 1).astype(jnp.int32)
    carry = (low.six(low.mix, -3, 6, 5), [low.nothing] * 5)
    carry = low.red(-2, 0, carry, low_shut)
    carry = low.red(-1, 1, carry, low_shut)
    carry = low.red(0, 0, carry)
    for t in range(5):
        r = tile(6 + 8 * t)
        low.mix2[4, r] = jnp.where(low.reds[0], carry[1][t], low.half[5, r] * low.new1[5, r])
    top = EDGE - 2
    carry = (high.six(high.mix, top, 6, 5), [high.new1[top + high.shift, tile(6 + 8 * t)] for t in range(5)])
    carry = high.red(top + 1, 1, carry)
    carry = high.red(top + 2, 0, carry, high_shut)
    carry = high.red(top + 3, 1, carry, high_shut)
    for t in range(5):
        high.mix2[top + 3 + high.shift, tile(6 + 8 * t)] = carry[1][t]

    carry = (low.six(low.mix2, -2, 7, 5), [low.nothing] * 5)
    for y in (-1, 0, 1):
        carry = low.black(y, y % 2, carry)
    for t in range(5):
        r = tile(7 + 8 * t)
        low.mix3[5, r] = jnp.where(low.reds[1], carry[1][t], low.half[6, r] * low.new2[6, r])
    top = EDGE - 3
    carry = (high.six(high.mix2, top, 7, 5), [high.new2[top + high.shift, tile(7 + 8 * t)] for t in range(5)])
    for y in range(top + 1, top + 4):
        carry = high.black(y, y % 2, carry)
    for t in range(5):
        high.mix3[top + 3 + high.shift, tile(7 + 8 * t)] = carry[1][t]

    flow = low.six(low.mix3, -1, 8, 4)
    for y in (0, 1, 2):
        flow = low.finish(y, y % 2, flow)
    flow = high.six(high.mix3, EDGE - 4, 8, 4)
    for y in range(EDGE - 3, EDGE):
        flow = high.finish(y, y % 2, flow)


def call(body, inputs, outputs, scratch, flops, moved, aliases=None, hbm=(), anywhere=False, limit=40 * 2**20):
    vmem, place, far = [pl.BlockSpec(memory_space=m) for m in (pltpu.VMEM, pl.ANY, pltpu.HBM)]
    kept = range(len(inputs)) if anywhere else ()
    return pl.pallas_call(
        body,
        out_shape=[jax.ShapeDtypeStruct(shape, F32) for shape in outputs],
        in_specs=[far if i in hbm else place if i in kept else vmem for i in range(len(inputs))],
        out_specs=[place if anywhere else vmem for _ in outputs],
        scratch_shapes=scratch,
        input_output_aliases=aliases or {},
        cost_estimate=pl.CostEstimate(flops=flops, bytes_accessed=moved, transcendentals=0),
        compiler_params=pltpu.CompilerParams(vmem_limit_bytes=limit),
    )(*inputs)


def per_device(old_fields, old_counts):
    groups, columns = lax.axis_size("grp"), lax.axis_size("dev")
    devices = groups * columns
    counts = jnp.pad(old_counts, (0, -devices % LANES)).reshape(-1, LANES)
    chain = [(i, i + 1) for i in range(devices - 1)]

    def swaps(count):
        ways = []
        for first in range(2):
            pairs = [(i, i + 1) for i in range(first, count - 1, 2)]
            ways.append(pairs + [(j, i) for i, j in pairs])
        return ways

    y_ways, x_ways = swaps(columns), swaps(groups)

    def read(body, outputs, after=None, limit=54400000):
        table = counts if after is None else lax.optimization_barrier((counts, after))[0]
        table = pltpu.with_memory_space_constraint(table, pltpu.HBM)
        scratch = [
            VMEM(counts.shape, jnp.int32),
            VMEM((FIELDS, COLUMN, EDGE, EDGE * EDGE), F32),
            pltpu.SemaphoreType.DMA((FIELDS + 1,)),
        ]
        return call(body, (table, old_fields), outputs, scratch, 10**6, 2 * 10**6, hbm=(0, 1), limit=limit)

    strip, message = (EDGE, 8, LANES), (YMSG, LANES)
    deep = (DEEP, ROWS, LANES)
    shell, core = read(pack_all, [(KINDS, GROUPS, 8, LANES), (KINDS, CORE, 8, LANES)])
    shell = lax.ppermute(shell, ("grp", "dev"), chain)
    core = lax.ppermute(core, ("grp", "dev"), chain)
    own, edges = read(relayout, [(FIELDS, EDGE, EDGE, LANES), (FIELDS, EDGE, 8, LANES)])
    x_first, x_second = call(make_faces, (counts, shell, edges), [strip, strip], [], 10**6, 10**6)
    table = lax.optimization_barrier((counts, x_first))[0]
    x_first = lax.ppermute(x_first, "grp", x_ways[0])
    x_second = lax.ppermute(x_second, "grp", x_ways[1])
    y_first, y_second = call(make_slabs, (table, shell, core, own), [message, message], [], 10**6, 10**6)
    y_first, y_second = call(
        add_corners,
        (x_first, x_second, y_first, y_second),
        [message, message],
        [pltpu.SemaphoreType.DMA((2, 2, 2))],
        10**4,
        10**5,
        aliases={2: 0, 3: 1},
        anywhere=True,
    )
    y_first = lax.ppermute(y_first, "dev", y_ways[0])
    y_second = lax.ppermute(y_second, "dev", y_ways[1])
    flat = (EDGE * EDGE, LANES)
    part_p, part_r, *kept = call(
        sweep_inner,
        (counts, own, shell, core, x_first, x_second),
        [flat, flat] + [deep] * len(KEPT),
        [],
        10**8,
        5 * 10**6,
    )
    outs = call(
        sweep_outer,
        (y_first, y_second, x_first, x_second, part_p, part_r, *kept),
        [flat, flat],
        [VMEM((2, 10, ROWS, LANES), F32)] * len(KEPT),
        10**7,
        10**6,
    )
    return tuple(out.reshape(EDGE, EDGE, LANES) for out in outs)


def solution(mesh):
    placed = (P(None, ("grp", "dev"), None, None), P())
    return jax.shard_map(
        per_device,
        mesh=mesh,
        in_specs=placed,
        out_specs=(P("grp", "dev", None), P("grp", "dev", None)),
        check_vma=False,
    )
```
